256 devices in a mesh: span: 32 (over z, x), elem: 8 (over y, core).
Axes of the slice: x: 4, y: 4, z: 8, core: 2. Of those that a mesh axis runs over, the one named last changes fastest.
Arguments:
- species: float32 [81, 3, 512, 1024], P(None, None, 'span', 'elem'), may hold values from 0.02 to 0.3
- laplacian: float32 [81, 3, 512, 1024], P(None, None, 'span', 'elem'), may hold values from -6 to 6
- binary: float32 [3, 4], replicated, may hold values from 0.3 to 3
- dref: float32 [3], replicated, may hold values from 0.5 to 2
- stiff_eig: float32 [9], replicated, may hold values from 0.02 to 3
- basis: float32 [9, 9], replicated, may hold values from -1 to 1, as said below
- rounds: int32 [256], replicated, may hold values from 1 to 4
- adjacency: int32 [1024, 4], P('elem'), may hold values from 0 to 1023, as said below
- edge_map: int32 [1024, 4], P('elem'), may hold values from 0 to 3
Outputs:
- updated: float32 [81, 3, 512, 1024], P(None, None, 'span', 'elem')
The draws below stay inside these ranges and needn't reach their ends.
Inputs may be any that keep to these rules, and one draw needn't show every extreme that they name: basis is an orthogonal matrix. The elements form a periodic mesh of 16 columns and 8 * 8 rows; each index of elem holds 8 whole rows in some order. adjacency is symmetric: element e lies across edge edge_map[e, j] of element adjacency[e, j]. The element across an edge lies on the same index of elem or on the one just before or after it, cyclically; exactly 16 elements of each index have an edge facing the next index and 16 one facing the previous, one such edge each.
All inputs are finite; a program needn't handle non-finite values.
Results may differ from the reference program's by a relative error of at most 0.0001.
Values sent between devices are 32-bit elements; how exact they have to be, the bound alone decides.
A program may use at most 128 MiB of HBM per device.

```python
import math
import jax
import jax.numpy as jnp
import numpy as np
from jax import lax

NP = 9
NN = 81
SPECIES = 3
NZ = 512
MODES = 256
MESH_X = 16
ROWS_DEV = 8
ELEM_DEV = 128
ELEM = 1024
N_ELEM = 8


def draw_basis(key, part):
    raw_draw = jax.random.normal(key, (NP, NP), jnp.float32)
    columns = []
    for index in range(NP):
        vector = raw_draw[:, index]
        for repeat in range(2):
            for other in columns:
                vector = vector - jnp.dot(other, vector) * other
        columns.append(vector / jnp.sqrt(jnp.sum(vector * vector)))
    return jnp.stack(columns, axis=1)


def draw_rounds(key, part):
    mode_ids = jnp.arange(MODES, dtype=jnp.int32)
    baseline = 4 - 4 * mode_ids // MODES
    jitter = jax.random.randint(jax.random.fold_in(key, 3), (MODES,), -1, 2)
    return jnp.clip(baseline + jitter, 1, 4).astype(jnp.int32)


def mesh_tables(key):
    base_key = jax.random.fold_in(key, 5)
    mesh_rows = ROWS_DEV * N_ELEM
    device_keys = jax.random.split(jax.random.fold_in(base_key, 1), N_ELEM)
    orders = jax.vmap(lambda device_key: jax.random.permutation(device_key, ELEM_DEV))(device_keys).astype(jnp.int32)
    rotations = jax.random.randint(jax.random.fold_in(base_key, 2), (mesh_rows, MESH_X), 0, 4)
    row_ids = jnp.arange(mesh_rows, dtype=jnp.int32)[:, None]
    col_ids = jnp.arange(MESH_X, dtype=jnp.int32)[None, :]
    device_ids = row_ids // ROWS_DEV
    within = row_ids % ROWS_DEV * MESH_X + col_ids
    identity = device_ids * ELEM_DEV + orders[device_ids, within]
    adjacency = jnp.zeros((ELEM_DEV * N_ELEM, 4), jnp.int32)
    edge_map = jnp.zeros((ELEM_DEV * N_ELEM, 4), jnp.int32)
    for local_edge in range(4):
        direction = (local_edge + rotations) % 4
        row_step = jnp.where(direction == 0, -1, jnp.where(direction == 2, 1, 0))
        col_step = jnp.where(direction == 1, 1, jnp.where(direction == 3, -1, 0))
        next_row = (row_ids + row_step) % mesh_rows
        next_col = (col_ids + col_step) % MESH_X
        neighbour = identity[next_row, next_col]
        back_edge = (direction + 2 - rotations[next_row, next_col]) % 4
        adjacency = adjacency.at[identity.reshape(-1), local_edge].set(neighbour.reshape(-1).astype(jnp.int32))
        edge_map = edge_map.at[identity.reshape(-1), local_edge].set(back_edge.reshape(-1).astype(jnp.int32))
    return (adjacency, edge_map)


def draw_adjacency(key, part):
    return mesh_tables(key)[0]


def draw_edge_map(key, part):
    return mesh_tables(key)[1]


def block_levels(rng, extent, cuts, least, top_value):
    level = 1.0
    for dim, parts in cuts:
        steps = jax.random.uniform(jax.random.fold_in(jax.random.fold_in(rng, 6), dim), (parts,), jnp.float32, least / len(cuts), top_value / len(cuts))
        level = level * jnp.repeat(jnp.exp(steps), extent[dim] // parts).reshape((-1,) + (1,) * (len(extent) - 1 - dim))
    return level


def noise(rng, extent, width, reach, cuts=(), kind=jnp.bfloat16):
    values = jax.random.normal(rng, extent, jnp.float32) * width
    if len(cuts) > 0:
        values = block_levels(rng, extent, cuts, -0.22, 0.18) * values
    return jnp.clip(values, min=-reach, max=reach).astype(kind)


def setup_inputs(seed: int = 0) -> dict:
    key_list = jax.random.split(jax.random.key(seed), 10)
    return {
        "species": jnp.clip(0.02 + 0.28 * jax.random.uniform(key_list[0], (NN, SPECIES, NZ, ELEM), jnp.float32) ** block_levels(key_list[0], (NN, SPECIES, NZ, ELEM), ((2, 32), (3, 8)), -0.2, 0.2), 0.02, 0.3),
        "laplacian": noise(key_list[1], (NN, SPECIES, NZ, ELEM), 1.0, 6.0, ((2, 32), (3, 8)), jnp.float32),
        "binary": jnp.clip(jnp.exp(jax.random.uniform(key_list[2], (SPECIES, SPECIES + 1), jnp.float32, math.log(0.3), math.log(3.0))), 0.3, 3.0),
        "dref": jnp.clip(jnp.exp(jax.random.uniform(key_list[3], (SPECIES,), jnp.float32, math.log(0.5), math.log(2.0))), 0.5, 2.0),
        "stiff_eig": jnp.clip(jnp.exp(jax.random.uniform(key_list[4], (NP,), jnp.float32, math.log(0.02), math.log(3.0))), 0.02, 3.0),
        "basis": draw_basis(jax.random.fold_in(key_list[9], 71), 0),
        "rounds": draw_rounds(jax.random.fold_in(key_list[9], 71), 0),
        "adjacency": draw_adjacency(jax.random.fold_in(key_list[9], 71), 0),
        "edge_map": draw_edge_map(jax.random.fold_in(key_list[9], 71), 0),
    }


coupling = 0.2
highest = lax.Precision.HIGHEST


def edge_lists(per_side):
    last_node = per_side - 1
    bottom = [i for i in range(per_side)]
    right_edge = [i * per_side + last_node for i in range(per_side)]
    top_edge = [last_node * per_side + last_node - i for i in range(per_side)]
    left_edge = [(last_node - i) * per_side for i in range(per_side)]
    return [bottom, right_edge, top_edge, left_edge]


def edge_matrix(per_side):
    edge_table = np.zeros((4, per_side, per_side * per_side), np.float32)
    for edge_id, node_list in enumerate(edge_lists(per_side)):
        for i, node_id in enumerate(node_list):
            edge_table[edge_id, i, node_id] = 1.0
    return edge_table


def mixture_source(species, laplacian, binary, dref):
    n_species = species.shape[1]
    bath_share = 1.0 - jnp.sum(species, axis=1)
    source_parts = []
    for s in range(n_species):
        resistance = bath_share / binary[s, n_species]
        for j in range(n_species):
            if j != s:
                resistance = resistance + species[:, j] / binary[s, j]
        mixture = (1.0 - species[:, s]) / resistance
        source_parts.append((species[:, s] + (mixture - dref[s]) * laplacian[:, s]) / dref[s])
    return jnp.stack(source_parts, axis=1)


def block_inverse(values, kron_basis, inverse_diag):
    n_nodes = values.shape[0]
    inner_part = jnp.dot(kron_basis.T, values.reshape(n_nodes, -1), precision=highest).reshape(values.shape) * inverse_diag
    return jnp.dot(kron_basis, inner_part.reshape(n_nodes, -1), precision=highest).reshape(values.shape)


def reference(species, laplacian, binary, dref, stiff_eig, basis, rounds, adjacency, edge_map):
    per_side = basis.shape[0]
    n_nodes = per_side * per_side
    species = jnp.transpose(species, (0, 1, 3, 2))
    laplacian = jnp.transpose(laplacian, (0, 1, 3, 2))
    source = mixture_source(species, laplacian, binary, dref)
    spectrum = jnp.fft.rfft(source, axis=3)[..., :MODES] / NZ
    modal_rhs = jnp.stack([jnp.real(spectrum), jnp.imag(spectrum)], axis=3)
    wavenumber = jnp.arange(MODES).astype(source.dtype) * (8.0 / NZ)
    shifts = 1.0 / dref[:, None] + (wavenumber * wavenumber)[None, :]
    eig_sum = (stiff_eig[:, None] + stiff_eig[None, :]).reshape(n_nodes)
    inverse_diag = 1.0 / (shifts[None, :, None, None, :] + eig_sum[:, None, None, None, None])
    kron_basis = (basis[:, None, :, None] * basis[None, :, None, :]).reshape(n_nodes, n_nodes)
    flat_index = np.array(edge_lists(per_side)).reshape(-1)
    scatter_table = edge_matrix(per_side)

    def couple(modal_field):
        traces = modal_field[flat_index].reshape((4, per_side) + modal_field.shape[1:])
        across = traces[edge_map, :, :, adjacency][:, :, ::-1]
        return jnp.einsum("jtn,ejtsrm->nserm", scatter_table, across, precision=highest)

    modal = block_inverse(modal_rhs, kron_basis, inverse_diag)
    for sweep_id in range(1, 4):
        proposal = block_inverse(modal_rhs + coupling * couple(modal), kron_basis, inverse_diag)
        modal = jnp.where(sweep_id < rounds, proposal, modal)
    complex_modes = modal[:, :, :, 0] + 1j * modal[:, :, :, 1]
    padded = jnp.concatenate([complex_modes, jnp.zeros_like(complex_modes[..., :1])], axis=3)
    result = jnp.fft.irfft(padded, n=NZ, axis=3) * NZ
    return jnp.transpose(result, (0, 1, 3, 2))
```

```python
import functools

import jax
import jax.numpy as jnp
import numpy as np
from jax import lax
from jax.experimental import pallas as pl
from jax.experimental.pallas import tpu as pltpu
from jax.sharding import PartitionSpec as P

MESH_X = 16
PER_SIDE = 9
SPECIES = 3
NS = PER_SIDE * PER_SIDE * SPECIES
LANES = 256
COUPLING = 0.2
SWEEPS = 3
GROUPS = 2
F32 = jnp.float32
BF16 = jnp.bfloat16
HIGHEST = lax.Precision.HIGHEST
MESH = pl.DeviceIdType.MESH
SOUTH, EAST, NORTH, WEST = 0, 1, 2, 3
VMEM_LIMIT = 60 * 1024 * 1024

NN_DIMS = (((1,), (0,)), ((), ()))
NT_DIMS = (((1,), (1,)), ((), ()))
TN_DIMS = (((0,), (0,)), ((), ()))


def split(x):
    high = x.astype(BF16)
    return high, (x - high.astype(F32)).astype(BF16)


def dot(a, b, dims=NN_DIMS):
    return lax.dot_general(a, b, dims, preferred_element_type=F32)


def dot3(a, b, dims=NN_DIMS):
    return dot(a[0], b[0], dims) + dot(a[0], b[1], dims) + dot(a[1], b[0], dims)


def edge_lists():
    last = PER_SIDE - 1
    return [
        [i for i in range(PER_SIDE)],
        [i * PER_SIDE + last for i in range(PER_SIDE)],
        [last * PER_SIDE + last - i for i in range(PER_SIDE)],
        [(last - i) * PER_SIDE for i in range(PER_SIDE)],
    ]


def selection_tables():
    pair_i = np.zeros((LANES, PER_SIDE), np.float32)
    pair_j = np.zeros((LANES, PER_SIDE), np.float32)
    pair_s = np.full((LANES,), -1)
    for lane in range(NS):
        node, s = divmod(lane, SPECIES)
        pair_i[lane, node // PER_SIDE] = 1.0
        pair_j[lane, node % PER_SIDE] = 1.0
        pair_s[lane] = s
    out_i = np.zeros((4, 128, PER_SIDE), np.float32)
    out_j = np.zeros((4, 128, PER_SIDE), np.float32)
    in_i = np.zeros((4, 128, PER_SIDE), np.float32)
    in_j = np.zeros((4, 128, PER_SIDE), np.float32)
    trace_s = np.full((128,), -2)
    edges = edge_lists()
    for rotation in range(4):
        for d in range(4):
            nodes = edges[(rotation + d) % 4]
            for t in range(PER_SIDE):
                for s in range(SPECIES):
                    lane = d * 32 + t * SPECIES + s
                    trace_s[lane] = s
                    out_i[rotation, lane, nodes[t] // PER_SIDE] = 1.0
                    out_j[rotation, lane, nodes[t] % PER_SIDE] = 1.0
                    back = nodes[PER_SIDE - 1 - t]
                    in_i[rotation, lane, back // PER_SIDE] = 1.0
                    in_j[rotation, lane, back % PER_SIDE] = 1.0
    pair_mask = (pair_s[:, None] == pair_s[None, :]) & (pair_s[:, None] >= 0)
    trace_mask = trace_s[:, None] == pair_s[None, :]
    return dict(
        pair_i=pair_i,
        pair_j=pair_j,
        edges=np.stack([out_i, out_j, in_i, in_j], axis=1).reshape(4, -1),
        pair_mask=pair_mask.astype(np.float32),
        trace_mask=np.tile(trace_mask.astype(np.float32), (4, 1)),
    )


def transform_tables(planes):
    modes = planes // 2
    phase = (np.arange(modes)[:, None] * np.arange(planes)[None, :]) % planes
    angle = phase.astype(np.float64) * (2.0 * np.pi / planes)
    trig = np.concatenate([np.cos(angle), -np.sin(angle)], axis=0)
    weight = np.where(np.arange(modes) == 0, 1.0, 2.0)
    weight = np.concatenate([weight, weight])
    return np.float32(trig / planes), np.float32((trig * weight[:, None]).T)


def split_table(table):
    high = table.astype(BF16)
    low = (table - high.astype(np.float32)).astype(BF16)
    return jnp.asarray(high), jnp.asarray(low)


def order_kernel(n_span, n_elem, own, cols, table_ref, place_ref, turn_ref):
    me = lax.axis_index("elem")
    rows = own // cols
    block_rows = rows // 2
    odd = lax.rem(me, 2)
    start = table_ref[4 * own]
    dart = lax.fori_loop(0, rows * me, lambda i, d: table_ref[d], start)
    norths = []
    for row in range(rows):
        norths.append(dart)
        if row + 1 < rows:
            dart = table_ref[dart]
    easts = []
    for dart in norths:
        edge = dart // own % 8
        easts.append(dart + ((edge + 3) % 4 - edge) * own)
    lane = lax.broadcasted_iota(jnp.int32, (1, own), 1)
    for col in range(cols):
        for row in range(rows):
            dart = easts[row]
            block_row = row // 2
            x = jnp.where(odd == 1, block_rows - 1 - block_row, block_row)
            slot = (row % 2 * 2 + col % 2) * n_span + (col // 2) * block_rows + x
            local = dart % own
            edge = dart // own % 8
            turn_ref[slot] = (edge + 3) % 4
            place_ref[pl.ds(slot, 1), :] = (lane == local).astype(F32)
            if col + 1 < cols:
                easts[row] = table_ref[dart]


def source_kernel(
    n_span, depth, own, species_ref, laplacian_ref, binary_ref, dref_ref, place_ref, out_ref, source_ref
):
    nodes = PER_SIDE * PER_SIDE
    inverse = [[1.0 / binary_ref[s, j] for j in range(SPECIES + 1)] for s in range(SPECIES)]
    dref = [dref_ref[s] for s in range(SPECIES)]
    over = [1.0 / dref_ref[s] for s in range(SPECIES)]
    source_ref[pl.ds(NS * depth, (LANES - NS) * depth), :] = jnp.zeros(((LANES - NS) * depth, own), F32)

    def one_node(node, carry):
        base = pl.multiple_of(node * SPECIES * depth, 8)
        parts = [species_ref[pl.ds(base + s * depth, depth), :] for s in range(SPECIES)]
        slopes = [laplacian_ref[pl.ds(base + s * depth, depth), :] for s in range(SPECIES)]
        bath = 1.0 - (parts[0] + parts[1] + parts[2])
        for s in range(SPECIES):
            resistance = bath * inverse[s][SPECIES]
            for j in range(SPECIES):
                if j != s:
                    resistance = resistance + parts[j] * inverse[s][j]
            mixture = (1.0 - parts[s]) / resistance
            value = (parts[s] + (mixture - dref[s]) * slopes[s]) * over[s]
            source_ref[pl.ds(base + s * depth, depth), :] = value
        return carry

    lax.fori_loop(0, nodes, one_node, 0, unroll=3)
    place = place_ref[...].astype(BF16)
    for plane in range(depth):
        high, low = split(source_ref[pl.ds(plane, LANES, stride=depth), :])
        moved = dot(place, high, NT_DIMS) + dot(place, low, NT_DIMS)
        for e in range(4):
            for h in range(2):
                out_ref[pl.ds((e * 2 + h) * depth + plane, n_span, stride=8 * depth), :] = moved[
                    e * n_span : (e + 1) * n_span, h * 128 : (h + 1) * 128
                ]


def finish_kernel(n_span, depth, own, values_ref, place_ref, out_ref):
    place = place_ref[...].astype(BF16)
    for plane in range(depth):
        for h in range(2):
            parts = [
                values_ref[pl.ds((e * 2 + h) * depth + plane, n_span, stride=8 * depth), :]
                for e in range(4)
            ]
            high, low = split(jnp.concatenate(parts, axis=0))
            moved = dot(high, place, TN_DIMS) + dot(low, place, TN_DIMS)
            count = min(NS - h * 128, 128)
            out_ref[pl.ds(h * 128 * depth + plane, count, stride=depth), :] = moved[:count]


def neighbours(n_span, n_elem, block_rows):
    span, elem = lax.axis_index("span"), lax.axis_index("elem")
    x = span % block_rows
    odd = elem % 2
    up = 1 - 2 * odd
    block_row = jnp.where(odd == 1, block_rows - 1 - x, x)
    last, first = block_row == block_rows - 1, block_row == 0
    return {
        NORTH: (jnp.where(last, span, span + up), jnp.where(last, (elem + 1) % n_elem, elem)),
        SOUTH: (jnp.where(first, span, span - up), jnp.where(first, (elem + n_elem - 1) % n_elem, elem)),
        EAST: ((span + block_rows) % n_span, elem),
        WEST: ((span + n_span - block_rows) % n_span, elem),
    }


def solve_kernel(
    n_span,
    n_elem,
    planes,
    block_rows,
    values_ref,
    forward_high,
    forward_low,
    backward_high,
    backward_low,
    pair_ref,
    out_trace_ref,
    in_trace_ref,
    diag_ref,
    rounds_ref,
    result_ref,
    work_high,
    work_low,
    rhs_ref,
    modal_ref,
    inverse_ref,
    trace_ref,
    send_ref,
    recv_ref,
    send_sem,
    recv_sem,
):
    modes = planes // 2
    depth = planes // n_span
    group = planes // GROUPS
    half = group // 2
    tile = min(256, planes)
    near = neighbours(n_span, n_elem, block_rows)
    barrier = pltpu.get_barrier_semaphore()
    for d in range(4):
        pl.semaphore_signal(barrier, inc=1, device_id=near[d], device_id_type=MESH)

    row = lax.broadcasted_iota(jnp.int32, (planes, LANES), 0)
    mode = jnp.where(row >= modes, row - modes, row).astype(F32)
    wave = mode * (8.0 / planes)
    inverse_ref[...] = 1.0 / (wave * wave + diag_ref[...])

    pair = split(pair_ref[...])

    for e in range(4):
        for start in range(0, planes, tile):
            rows = pl.ds(start, tile)
            blocks = pl.ds(start // depth, tile // depth)
            halves = [values_ref[blocks, e * 2 + h].reshape(tile, 128) for h in range(2)]
            high, low = split(dot3(split(jnp.concatenate(halves, axis=1)), pair))
            work_high[rows, pl.ds(e * LANES, LANES)] = high
            work_low[rows, pl.ds(e * LANES, LANES)] = low

    def to_modes(step, carry):
        rows = pl.ds(pl.multiple_of(step * tile, tile), tile)
        table = forward_high[rows, :], forward_low[rows, :]
        scale = inverse_ref[rows, :]
        for e in range(4):
            cols = pl.ds(e * LANES, LANES)
            rhs = dot3(table, (work_high[:, cols], work_low[:, cols]))
            rhs_ref[e, rows, :] = rhs
            modal_ref[e, rows, :] = rhs * scale
        return carry

    lax.fori_loop(0, planes // tile, to_modes, 0)

    to_trace = [split(out_trace_ref[pl.ds(e * 128, 128), :]) for e in range(4)]
    from_trace = [split(in_trace_ref[pl.ds(e * 128, 128), :]) for e in range(4)]
    lane_group = lax.broadcasted_iota(jnp.int32, (1, 128), 1) // 32
    outer = {NORTH: (2, 3), SOUTH: (0, 1), EAST: (1, 3), WEST: (0, 2)}

    def copies(sweep, g):
        opposite = {NORTH: SOUTH, SOUTH: NORTH, EAST: WEST, WEST: EAST}
        return [
            pltpu.make_async_remote_copy(
                src_ref=send_ref.at[sweep, g, d],
                dst_ref=recv_ref.at[sweep, g, opposite[d]],
                send_sem=send_sem.at[sweep, g, d],
                recv_sem=recv_sem.at[sweep, g, opposite[d]],
                device_id=near[d],
                device_id_type=MESH,
            )
            for d in range(4)
        ]

    def send_traces(sweep, g):
        rows = pl.ds(g * group, group)
        traces = []
        for e in range(4):
            trace = dot3(split(modal_ref[e, rows, :]), to_trace[e], NT_DIMS)
            trace_ref[e, rows, :] = trace
            traces.append(trace)
        for d in range(4):
            packed = None
            for h in range(2):
                for q in range(2):
                    piece = traces[outer[d][q]][h * half : (h + 1) * half]
                    goal = h * 2 + q
                    shift = (goal - d) % 4 * 32
                    if shift:
                        piece = pltpu.roll(piece, shift, 1)
                    packed = piece if packed is None else jnp.where(lane_group == goal, piece, packed)
            send_ref[sweep, g, d] = packed
        for copy in copies(sweep, g):
            copy.start()

    def update(sweep, g):
        for copy in copies(sweep, g):
            copy.wait_recv()
        for h in range(2):
            rows = pl.ds(g * group + h * half, half)
            active = rounds_ref[rows, :] > sweep + 1
            active = jnp.concatenate([active, active], axis=1)
            scale = inverse_ref[rows, :]
            for e in range(4):
                a, b = divmod(e, 2)
                across = None
                sides = (
                    (NORTH, None) if a == 0 else (NORTH, b),
                    (SOUTH, b) if a == 0 else (SOUTH, None),
                    (EAST, None) if b == 0 else (EAST, a),
                    (WEST, a) if b == 0 else (WEST, None),
                )
                for d, q in sides:
                    if q is None:
                        other = (2 * (1 - a) + b) if d in (NORTH, SOUTH) else (2 * a + 1 - b)
                        piece = pltpu.roll(trace_ref[other, rows, :], 64, 1)
                    else:
                        piece = recv_ref[sweep, g, d]
                        shift = (d - (h * 2 + q)) % 4 * 32
                        if shift:
                            piece = pltpu.roll(piece, shift, 1)
                    across = piece if across is None else jnp.where(lane_group == d, piece, across)
                fresh = (rhs_ref[e, rows, :] + dot3(split(across), from_trace[e])) * scale
                modal_ref[e, rows, :] = jnp.where(active, fresh, modal_ref[e, rows, :])

    pl.semaphore_wait(barrier, 4)
    for g in range(GROUPS):
        send_traces(0, g)
    for sweep in range(SWEEPS):
        for g in range(GROUPS):
            update(sweep, g)
            if sweep + 1 < SWEEPS:
                send_traces(sweep + 1, g)

    for e in range(4):
        for start in range(0, planes, tile):
            rows = pl.ds(start, tile)
            high, low = split(dot3(split(modal_ref[e, rows, :]), pair, NT_DIMS))
            work_high[rows, pl.ds(e * LANES, LANES)] = high
            work_low[rows, pl.ds(e * LANES, LANES)] = low

    def to_planes(step, carry):
        rows = pl.ds(pl.multiple_of(step * tile, tile), tile)
        table = backward_high[rows, :], backward_low[rows, :]
        for e in range(4):
            cols = pl.ds(e * LANES, LANES)
            value = dot3(table, (work_high[:, cols], work_low[:, cols]))
            for h in range(2):
                part = value[:, h * 128 : (h + 1) * 128]
                result_ref[pl.ds(step * (tile // depth), tile // depth), e * 2 + h] = part.reshape(
                    tile // depth, depth, 128
                )
        return carry

    lax.fori_loop(0, planes // tile, to_planes, 0)
    for sweep in range(SWEEPS):
        for g in range(GROUPS):
            for copy in copies(sweep, g):
                copy.wait_send()


def vmem():
    return pl.BlockSpec(memory_space=pltpu.VMEM)


def smem():
    return pl.BlockSpec(memory_space=pltpu.SMEM)


def body(species, laplacian, binary, dref, stiff_eig, basis, rounds, adjacency, edge_map):
    n_span = lax.axis_size("span")
    n_elem = lax.axis_size("elem")
    depth = species.shape[2]
    own = species.shape[3]
    planes = depth * n_span
    cols = MESH_X
    block_rows = own // cols // 2
    tables = selection_tables()

    ahead_id, ahead_edge = adjacency.T, edge_map.T
    owner = ahead_id // own
    step = owner * (8 * own) + (ahead_edge + 2) % 4 * own + ahead_id % own
    before = (lax.axis_index("elem") + n_elem - 1) % n_elem
    edge_ids = lax.broadcasted_iota(jnp.int32, (4, own), 0)
    elem_ids = lax.broadcasted_iota(jnp.int32, (4, own), 1)
    facing = jnp.where(owner == before, (edge_ids + 2) % 4 * own + elem_ids, 8 * own)
    start = jnp.broadcast_to(jnp.min(facing), (4, own))
    local_table = jnp.concatenate([step, start], axis=0)
    table = lax.all_to_all(
        jnp.broadcast_to(local_table[None], (n_elem, 8, own)), "elem", split_axis=0, concat_axis=0, tiled=True
    ).reshape(n_elem * 8 * own)

    place, turn = pl.pallas_call(
        functools.partial(order_kernel, n_span, n_elem, own, cols),
        out_shape=(
            jax.ShapeDtypeStruct((own, own), F32),
            jax.ShapeDtypeStruct((own,), jnp.int32),
        ),
        in_specs=[smem()],
        out_specs=(vmem(), smem()),
        name="order",
    )(table)

    sent = pl.pallas_call(
        functools.partial(source_kernel, n_span, depth, own),
        out_shape=jax.ShapeDtypeStruct((n_span * 8 * depth, 128), F32),
        in_specs=[vmem(), vmem(), smem(), smem(), vmem()],
        out_specs=vmem(),
        scratch_shapes=[pltpu.VMEM((LANES * depth, own), F32)],
        compiler_params=pltpu.CompilerParams(vmem_limit_bytes=VMEM_LIMIT),
        name="source",
    )(
        species.reshape(NS * depth, own),
        laplacian.reshape(NS * depth, own),
        binary,
        dref,
        place,
    )
    gathered = lax.all_to_all(
        sent.reshape(n_span, 8, depth, 128), "span", split_axis=0, concat_axis=0, tiled=True
    )

    def spread(left_i, left_j, matrix, right_i, right_j):
        one = jnp.dot(jnp.dot(left_i, matrix, precision=HIGHEST), right_i.T, precision=HIGHEST)
        two = jnp.dot(jnp.dot(left_j, matrix, precision=HIGHEST), right_j.T, precision=HIGHEST)
        return one * two

    pair = spread(tables["pair_i"], tables["pair_j"], basis, tables["pair_i"], tables["pair_j"])
    pair = pair * tables["pair_mask"]
    my_turn = lax.dynamic_slice_in_dim(turn.reshape(4, n_span), lax.axis_index("span"), 1, axis=1)
    chosen = (my_turn == jnp.arange(4)[None, :]).astype(F32)
    edges = jnp.dot(chosen, tables["edges"]).reshape(4, 4, 128, PER_SIDE)
    out_i, out_j, in_i, in_j = [edges[:, i].reshape(512, PER_SIDE) for i in range(4)]
    out_trace = spread(out_i, out_j, basis, tables["pair_i"], tables["pair_j"])
    out_trace = out_trace * tables["trace_mask"]
    in_trace = spread(in_i, in_j, basis, tables["pair_i"], tables["pair_j"])
    in_trace = in_trace * (COUPLING * tables["trace_mask"])
    eig_sum = (stiff_eig[:, None] + stiff_eig[None, :]).reshape(-1)
    diag = (eig_sum[:, None] + 1.0 / dref[None, :]).reshape(1, NS)
    diag = jnp.pad(diag, ((0, 0), (0, LANES - NS)), constant_values=1.0)
    row_rounds = jnp.broadcast_to(jnp.concatenate([rounds, rounds])[:, None], (planes, 128))
    forward, backward = transform_tables(planes)

    group = planes // GROUPS
    halo = (SWEEPS, GROUPS, 4, group // 2, 128)
    solved = pl.pallas_call(
        functools.partial(solve_kernel, n_span, n_elem, planes, block_rows),
        out_shape=jax.ShapeDtypeStruct((n_span, 8, depth, 128), F32),
        in_specs=[vmem()] * 10,
        out_specs=vmem(),
        scratch_shapes=[
            pltpu.VMEM((planes, 4 * LANES), BF16),
            pltpu.VMEM((planes, 4 * LANES), BF16),
            pltpu.VMEM((4, planes, LANES), F32),
            pltpu.VMEM((4, planes, LANES), F32),
            pltpu.VMEM((planes, LANES), F32),
            pltpu.VMEM((4, planes, 128), F32),
            pltpu.VMEM(halo, F32),
            pltpu.VMEM(halo, F32),
            pltpu.SemaphoreType.DMA(halo[:3]),
            pltpu.SemaphoreType.DMA(halo[:3]),
        ],
        compiler_params=pltpu.CompilerParams(
            collective_id=0, has_side_effects=True, vmem_limit_bytes=VMEM_LIMIT
        ),
        name="solve",
    )(
        gathered,
        *split_table(forward),
        *split_table(backward),
        pair,
        out_trace,
        in_trace,
        diag,
        row_rounds,
    )
    returned = lax.all_to_all(solved, "span", split_axis=0, concat_axis=0, tiled=True)
    updated = pl.pallas_call(
        functools.partial(finish_kernel, n_span, depth, own),
        out_shape=jax.ShapeDtypeStruct((NS * depth, own), F32),
        in_specs=[vmem(), vmem()],
        out_specs=vmem(),
        compiler_params=pltpu.CompilerParams(vmem_limit_bytes=VMEM_LIMIT),
        name="finish",
    )(returned.reshape(n_span * 8 * depth, 128), place)
    return updated.reshape(species.shape)


def solution(mesh):
    return jax.shard_map(
        body,
        mesh=mesh,
        in_specs=(
            P(None, None, "span", "elem"),
            P(None, None, "span", "elem"),
            P(),
            P(),
            P(),
            P(),
            P(),
            P("elem", None),
            P("elem", None),
        ),
        out_specs=P(None, None, "span", "elem"),
        check_vma=False,
    )
```

```python
import functools

import jax
import jax.numpy as jnp
import numpy as np
from jax import lax
from jax.experimental import pallas as pl
from jax.experimental.pallas import tpu as pltpu
from jax.sharding import PartitionSpec as P

MESH_X = 16
PER_SIDE = 9
SPECIES = 3
NS = PER_SIDE * PER_SIDE * SPECIES
LANES = 256
COUPLING = 0.2
SWEEPS = 3
GROUPS = 4
F32 = jnp.float32
BF16 = jnp.bfloat16
HIGHEST = lax.Precision.HIGHEST
MESH = pl.DeviceIdType.MESH
SOUTH, EAST, NORTH, WEST = 0, 1, 2, 3
VMEM_LIMIT = 60 * 1024 * 1024

NN_DIMS = (((1,), (0,)), ((), ()))
NT_DIMS = (((1,), (1,)), ((), ()))
TN_DIMS = (((0,), (0,)), ((), ()))


def split(x):
    high = x.astype(BF16)
    return high, (x - high.astype(F32)).astype(BF16)


def dot(a, b, dims=NN_DIMS):
    return lax.dot_general(a, b, dims, preferred_element_type=F32)


def dot3(a, b, dims=NN_DIMS):
    return dot(a[0], b[0], dims) + dot(a[0], b[1], dims) + dot(a[1], b[0], dims)


def edge_lists():
    last = PER_SIDE - 1
    return [
        [i for i in range(PER_SIDE)],
        [i * PER_SIDE + last for i in range(PER_SIDE)],
        [last * PER_SIDE + last - i for i in range(PER_SIDE)],
        [(last - i) * PER_SIDE for i in range(PER_SIDE)],
    ]


def selection_tables():
    pair = np.zeros((2, LANES, 128), np.float32)
    pair_s = np.full((LANES,), -1)
    for lane in range(NS):
        node, s = divmod(lane, SPECIES)
        pair[0, lane, node // PER_SIDE] = 1.0
        pair[1, lane, node % PER_SIDE] = 1.0
        pair_s[lane] = s
    trace = np.zeros((4, 128, 128), np.float32)
    trace_s = np.full((128,), -2)
    for d, nodes in enumerate(edge_lists()):
        for t in range(PER_SIDE):
            for s in range(SPECIES):
                lane = d * 32 + t * SPECIES + s
                trace_s[lane] = s
                back = nodes[PER_SIDE - 1 - t]
                trace[0, lane, nodes[t] // PER_SIDE] = 1.0
                trace[1, lane, nodes[t] % PER_SIDE] = 1.0
                trace[2, lane, back // PER_SIDE] = 1.0
                trace[3, lane, back % PER_SIDE] = 1.0
    pair_mask = (pair_s[:, None] == pair_s[None, :]) & (pair_s[:, None] >= 0)
    trace_mask = trace_s[:, None] == pair_s[None, :]
    hot = np.concatenate([pair.reshape(2 * LANES, 128), trace.reshape(512, 128)], axis=0)
    mask = np.concatenate([pair_mask, trace_mask], axis=0)
    return jnp.asarray(hot.astype(BF16)), jnp.asarray(mask.astype(np.float32))


def transform_tables(planes):
    modes = planes // 2
    phase = (np.arange(modes)[:, None] * np.arange(planes)[None, :]) % planes
    angle = phase.astype(np.float64) * (2.0 * np.pi / planes)
    trig = np.concatenate([np.cos(angle), -np.sin(angle)], axis=0)
    weight = np.where(np.arange(modes) == 0, 1.0, 2.0)
    weight = np.concatenate([weight, weight])
    return np.float32(trig / planes), np.float32((trig * weight[:, None]).T)


def split_table(table):
    high = table.astype(BF16)
    low = (table - high.astype(np.float32)).astype(BF16)
    return jnp.asarray(np.stack([high, low]))


def split3(x):
    high = x.astype(BF16)
    rest = x - high.astype(F32)
    middle = rest.astype(BF16)
    return high, middle, (rest - middle.astype(F32)).astype(BF16)


def pick(hot, x, dims=NN_DIMS):
    return sum(dot(hot, part, dims) for part in split3(x))


def pick_right(x, hot):
    return sum(dot(part, hot, NT_DIMS) for part in split3(x))


def finish_kernel(n_span, depth, own, values_ref, place_ref, out_ref):
    place = place_ref[...].astype(BF16)
    for plane in range(depth):
        for h in range(2):
            parts = [
                values_ref[pl.ds((h * 4 + e) * depth + plane, n_span, stride=8 * depth), :]
                for e in range(4)
            ]
            high, low = split(jnp.concatenate(parts, axis=0))
            moved = dot(high, place, TN_DIMS) + dot(low, place, TN_DIMS)
            count = min(NS - h * 128, 128)
            out_ref[pl.ds(h * 128 * depth + plane, count, stride=depth), :] = moved[:count]


def neighbours(n_span, n_elem, block_rows):
    span, elem = lax.axis_index("span"), lax.axis_index("elem")
    x = span % block_rows
    odd = elem % 2
    up = 1 - 2 * odd
    block_row = jnp.where(odd == 1, block_rows - 1 - x, x)
    last, first = block_row == block_rows - 1, block_row == 0
    return {
        NORTH: (jnp.where(last, span, span + up), jnp.where(last, (elem + 1) % n_elem, elem)),
        SOUTH: (jnp.where(first, span, span - up), jnp.where(first, (elem + n_elem - 1) % n_elem, elem)),
        EAST: ((span + block_rows) % n_span, elem),
        WEST: ((span + n_span - block_rows) % n_span, elem),
    }


def main_kernel(
    n_span,
    n_elem,
    depth,
    own,
    cols,
    species_hbm,
    laplacian_hbm,
    binary_ref,
    dref_ref,
    eig_ref,
    basis_ref,
    rounds_ref,
    adjacency_ref,
    edge_map_ref,
    hot_ref,
    mask_ref,
    forward_hbm,
    backward_hbm,
    result_ref,
    place_ref,
    species_ref,
    laplacian_ref,
    source_ref,
    tables_ref,
    walk_ref,
    turn_ref,
    small_ref,
    forward_ref,
    backward_ref,
    sent_ref,
    values_ref,
    back_ref,
    work_high,
    work_low,
    rhs_ref,
    modal_ref,
    inverse_ref,
    rounds_col,
    trace_ref,
    send_ref,
    recv_ref,
    load_sem,
    walk_sem,
    table_send,
    table_recv,
    out_send,
    out_recv,
    back_send,
    back_recv,
    send_sem,
    recv_sem,
):
    planes = n_span * depth
    modes = planes // 2
    rows = own // cols
    block_rows = rows // 2
    group = planes // GROUPS
    half = group // 2
    tile = min(256, planes)
    block = 8 * depth
    nodes = PER_SIDE * PER_SIDE
    span, elem = lax.axis_index("span"), lax.axis_index("elem")
    near = neighbours(n_span, n_elem, block_rows)

    def span_peer(k):
        z = (span // block_rows + k // block_rows) % (n_span // block_rows)
        x = (span + k) % block_rows
        return z * block_rows + x

    barrier = pltpu.get_barrier_semaphore()

    def greet_span(k, carry):
        pl.semaphore_signal(barrier, inc=1, device_id=(span_peer(k), elem), device_id_type=MESH)
        return carry

    def greet_elem(k, carry):
        pl.semaphore_signal(
            barrier, inc=1, device_id=(span, (elem + k) % n_elem), device_id_type=MESH
        )
        return carry

    lax.fori_loop(1, n_elem, greet_elem, 0)
    lax.fori_loop(1, n_span, greet_span, 0)

    cut = (128 + SPECIES - 1) // SPECIES
    pieces = [(0, cut), (cut, nodes - cut)]
    loads = []
    for i, (first, count) in enumerate(pieces):
        span_rows = pl.ds(first * SPECIES * depth, count * SPECIES * depth)
        for j, (source, target) in enumerate(
            ((species_hbm, species_ref), (laplacian_hbm, laplacian_ref))
        ):
            copy = pltpu.make_async_copy(source.at[span_rows], target.at[span_rows], load_sem.at[i * 2 + j])
            copy.start()
            loads.append(copy)
    table_loads = [
        pltpu.make_async_copy(forward_hbm, forward_ref, load_sem.at[4]),
        pltpu.make_async_copy(backward_hbm, backward_ref, load_sem.at[5]),
    ]
    for copy in table_loads:
        copy.start()

    inverse = [[1.0 / binary_ref[s, j] for j in range(SPECIES + 1)] for s in range(SPECIES)]
    dref = [dref_ref[s] for s in range(SPECIES)]
    over = [1.0 / dref_ref[s] for s in range(SPECIES)]

    def sources(first, count):
        def one_node(node, carry):
            base = pl.multiple_of(node * SPECIES * depth, 8)
            parts = [species_ref[pl.ds(base + s * depth, depth), :] for s in range(SPECIES)]
            slopes = [laplacian_ref[pl.ds(base + s * depth, depth), :] for s in range(SPECIES)]
            bath = 1.0 - (parts[0] + parts[1] + parts[2])
            for s in range(SPECIES):
                resistance = bath * inverse[s][SPECIES]
                for j in range(SPECIES):
                    if j != s:
                        resistance = resistance + parts[j] * inverse[s][j]
                mixture = (1.0 - parts[s]) / resistance
                value = (parts[s] + (mixture - dref[s]) * slopes[s]) * over[s]
                source_ref[pl.ds(base + s * depth, depth), :] = value
            return carry

        lax.fori_loop(first, first + count, one_node, 0, unroll=2)

    source_ref[pl.ds(NS * depth, (LANES - NS) * depth), :] = jnp.zeros(((LANES - NS) * depth, own), F32)
    loads[0].wait()
    loads[1].wait()
    sources(*pieces[0])

    ahead_id, ahead_edge = adjacency_ref[...], edge_map_ref[...]
    owner = ahead_id // own
    step = owner * (8 * own) + (ahead_edge + 2) % 4 * own + ahead_id % own
    before = (elem + n_elem - 1) % n_elem
    edge_ids = lax.broadcasted_iota(jnp.int32, (4, own), 0)
    elem_ids = lax.broadcasted_iota(jnp.int32, (4, own), 1)
    facing = jnp.where(owner == before, (edge_ids + 2) % 4 * own + elem_ids, 8 * own)
    start = jnp.min(jnp.min(facing, axis=0, keepdims=True), axis=1, keepdims=True)
    my_rows = pl.ds(pl.multiple_of(elem * 8, 8), 8)
    tables_ref[my_rows, :] = jnp.concatenate([step, jnp.broadcast_to(start, (4, own))], axis=0)

    pl.semaphore_wait(barrier, n_span + n_elem - 2)

    def table_copy(k):
        return pltpu.make_async_remote_copy(
            src_ref=tables_ref.at[my_rows],
            dst_ref=tables_ref.at[my_rows],
            send_sem=table_send.at[k],
            recv_sem=table_recv.at[k],
            device_id=(span, (elem + k) % n_elem),
            device_id_type=MESH,
        )

    for k in range(1, n_elem):
        table_copy(k).start()
    loads[2].wait()
    loads[3].wait()
    sources(*pieces[1])
    for k in range(1, n_elem):
        table_copy(k).wait_recv()
    walk = pltpu.make_async_copy(tables_ref, walk_ref, walk_sem)
    walk.start()
    walk.wait()

    def ahead(dart):
        return walk_ref[dart // own, dart % own]

    odd = elem % 2
    dart = lax.fori_loop(0, rows * elem, lambda i, d: ahead(d), walk_ref[4, 0])
    norths = []
    for row in range(rows):
        norths.append(dart)
        if row + 1 < rows:
            dart = ahead(dart)
    easts = []
    for dart in norths:
        edge = dart // own % 8
        easts.append(dart + ((edge + 3) % 4 - edge) * own)
    lane = lax.broadcasted_iota(jnp.int32, (1, own), 1)
    for col in range(cols):
        for row in range(rows):
            dart = easts[row]
            block_row = row // 2
            x = jnp.where(odd == 1, block_rows - 1 - block_row, block_row)
            slot = (row % 2 * 2 + col % 2) * n_span + (col // 2) * block_rows + x
            turn_ref[slot] = (dart // own % 8 + 3) % 4
            place_ref[pl.ds(slot, 1), :] = (lane == dart % own).astype(F32)
            if col + 1 < cols:
                easts[row] = ahead(dart)

    def exchange(source, target, send, recv, k, h):
        peer = span_peer(k)
        return pltpu.make_async_remote_copy(
            src_ref=source.at[pl.ds(pl.multiple_of(peer * block + h * (block // 2), 8), block // 2)],
            dst_ref=target.at[pl.ds(pl.multiple_of(span * block + h * (block // 2), 8), block // 2)],
            send_sem=send.at[h, k],
            recv_sem=recv.at[h, k],
            device_id=(peer, elem),
            device_id_type=MESH,
        )

    def send_phase(source, target, send, recv, h):
        def one(k, carry):
            exchange(source, target, send, recv, k, h).start()
            return carry

        lax.fori_loop(1, n_span, one, 0)
        mine = pl.ds(pl.multiple_of(span * block + h * (block // 2), 8), block // 2)
        target[mine, :] = source[mine, :]

    def wait_phase(source, target, send, recv, h, sending):
        def one(k, carry):
            copy = exchange(source, target, send, recv, k, h)
            if sending:
                copy.wait_send()
            else:
                copy.wait_recv()
            return carry

        lax.fori_loop(1, n_span, one, 0)

    place = place_ref[...].astype(BF16)
    for h in range(2):
        for plane in range(depth):
            high, low = split(source_ref[pl.ds(h * 128 * depth + plane, 128, stride=depth), :])
            moved = dot(place, high, NT_DIMS) + dot(place, low, NT_DIMS)
            for e in range(4):
                sent_ref[pl.ds((h * 4 + e) * depth + plane, n_span, stride=block), :] = moved[
                    e * n_span : (e + 1) * n_span
                ]
        send_phase(sent_ref, values_ref, out_send, out_recv, h)

    small_ref[...] = jnp.zeros_like(small_ref)
    small_ref[:PER_SIDE, :PER_SIDE] = basis_ref[...]
    small_ref[128 : 128 + 1, :PER_SIDE] = eig_ref[...]
    basis = small_ref[:128, :]
    hot_i, hot_j = hot_ref[:LANES, :], hot_ref[LANES : 2 * LANES, :]

    def spread(left_i, left_j):
        return pick_right(pick(left_i, basis), hot_i) * pick_right(pick(left_j, basis), hot_j)

    traces_hot = [hot_ref[pl.ds(2 * LANES + i * 128, 128), :] for i in range(4)]
    trace_mask = mask_ref[LANES:, :]
    pair = split(spread(hot_i, hot_j) * mask_ref[:LANES, :])
    out_trace = spread(traces_hot[0], traces_hot[1]) * trace_mask
    in_trace = spread(traces_hot[2], traces_hot[3]) * (COUPLING * trace_mask)

    def turned(matrix, e):
        turn = jnp.full((32, LANES), turn_ref[e * n_span + span], jnp.int32)
        edges = [matrix[d * 32 : (d + 1) * 32] for d in range(4)]
        blocks = []
        for d in range(4):
            chosen = edges[d]
            for r in range(1, 4):
                chosen = jnp.where(turn == r, edges[(d + r) % 4], chosen)
            blocks.append(chosen)
        return split(jnp.concatenate(blocks, axis=0))

    to_trace = [turned(out_trace, e) for e in range(4)]
    from_trace = [turned(in_trace, e) for e in range(4)]

    eig_row = small_ref[128:136, :]
    diag = (pick_right(eig_row, hot_i) + pick_right(eig_row, hot_j))[:1]
    pair_lane = lax.broadcasted_iota(jnp.int32, (1, LANES), 1)
    for s in range(SPECIES):
        diag = diag + jnp.where(pair_lane % SPECIES == s, over[s], 0.0)
    row = lax.broadcasted_iota(jnp.int32, (planes, LANES), 0)
    wave = jnp.where(row >= modes, row - modes, row).astype(F32) * (8.0 / planes)
    inverse_ref[...] = 1.0 / (wave * wave + diag)
    square = lax.broadcasted_iota(jnp.int32, (modes, modes), 0) == lax.broadcasted_iota(
        jnp.int32, (modes, modes), 1
    )
    spread_rounds = jnp.where(square, rounds_ref[...].astype(F32), 0.0).astype(BF16)
    column = dot(spread_rounds, jnp.ones((modes, 128), BF16))
    rounds_col[:modes, :] = column
    rounds_col[modes:, :] = column

    table_loads[0].wait()
    for h in range(2):
        wait_phase(sent_ref, values_ref, out_send, out_recv, h, False)
        for e in (0, 2):
            lanes = []
            for i in range(2):
                first = (h * 4 + e + i) * depth
                lanes.append(
                    jnp.concatenate(
                        [values_ref[pl.ds(d * block + first, depth), :] for d in range(n_span)], axis=0
                    )
                )
            planes_in = split(jnp.concatenate(lanes, axis=1))
            for first in range(0, planes, tile):
                out_rows = pl.ds(first, tile)
                value = split(dot3((forward_ref[0, out_rows, :], forward_ref[1, out_rows, :]), planes_in))
                for i in range(2):
                    target = pl.ds((e + i) * LANES + h * 128, 128)
                    work_high[out_rows, target] = value[0][:, i * 128 : (i + 1) * 128]
                    work_low[out_rows, target] = value[1][:, i * 128 : (i + 1) * 128]

    lane_group = lax.broadcasted_iota(jnp.int32, (1, 128), 1) // 32
    outer = {NORTH: (2, 3), SOUTH: (0, 1), EAST: (1, 3), WEST: (0, 2)}
    opposite = {NORTH: SOUTH, SOUTH: NORTH, EAST: WEST, WEST: EAST}

    def copies(sweep, g):
        return [
            pltpu.make_async_remote_copy(
                src_ref=send_ref.at[sweep, g, d],
                dst_ref=recv_ref.at[sweep, g, opposite[d]],
                send_sem=send_sem.at[sweep, g, d],
                recv_sem=recv_sem.at[sweep, g, opposite[d]],
                device_id=near[d],
                device_id_type=MESH,
            )
            for d in range(4)
        ]

    def send_traces(sweep, g):
        g_rows = pl.ds(g * group, group)
        traces = []
        for e in range(4):
            trace = dot3(split(modal_ref[e, g_rows, :]), to_trace[e], NT_DIMS)
            trace_ref[e, g_rows, :] = trace
            traces.append(trace)
        for d in range(4):
            packed = None
            for h in range(2):
                for q in range(2):
                    piece = traces[outer[d][q]][h * half : (h + 1) * half]
                    goal = h * 2 + q
                    shift = (goal - d) % 4 * 32
                    if shift:
                        piece = pltpu.roll(piece, shift, 1)
                    packed = piece if packed is None else jnp.where(lane_group == goal, piece, packed)
            send_ref[sweep, g, d] = packed
        for copy in copies(sweep, g):
            copy.start()

    def update(sweep, g):
        for copy in copies(sweep, g):
            copy.wait_recv()
        for h in range(2):
            h_rows = pl.ds(g * group + h * half, half)
            active = rounds_col[h_rows, :] > sweep + 1.5
            active = jnp.concatenate([active, active], axis=1)
            scale = inverse_ref[h_rows, :]
            for e in range(4):
                a, b = divmod(e, 2)
                across = None
                sides = (
                    (NORTH, None) if a == 0 else (NORTH, b),
                    (SOUTH, b) if a == 0 else (SOUTH, None),
                    (EAST, None) if b == 0 else (EAST, a),
                    (WEST, a) if b == 0 else (WEST, None),
                )
                for d, q in sides:
                    if q is None:
                        other = (2 * (1 - a) + b) if d in (NORTH, SOUTH) else (2 * a + 1 - b)
                        piece = pltpu.roll(trace_ref[other, h_rows, :], 64, 1)
                    else:
                        piece = recv_ref[sweep, g, d]
                        shift = (d - (h * 2 + q)) % 4 * 32
                        if shift:
                            piece = pltpu.roll(piece, shift, 1)
                    across = piece if across is None else jnp.where(lane_group == d, piece, across)
                fresh = (rhs_ref[e, h_rows, :] + dot3(split(across), from_trace[e])) * scale
                modal_ref[e, h_rows, :] = jnp.where(active, fresh, modal_ref[e, h_rows, :])

    for g in range(GROUPS):
        g_rows = pl.ds(g * group, group)
        scale = inverse_ref[g_rows, :]
        for e in range(4):
            lanes = pl.ds(e * LANES, LANES)
            rhs = dot3((work_high[g_rows, lanes], work_low[g_rows, lanes]), pair)
            rhs_ref[e, g_rows, :] = rhs
            modal_ref[e, g_rows, :] = rhs * scale
        send_traces(0, g)
    for sweep in range(SWEEPS):
        for g in range(GROUPS):
            update(sweep, g)
            if sweep + 1 < SWEEPS:
                send_traces(sweep + 1, g)

    for e in range(4):
        for first in range(0, planes, tile):
            out_rows = pl.ds(first, tile)
            high, low = split(dot3(split(modal_ref[e, out_rows, :]), pair, NT_DIMS))
            work_high[out_rows, pl.ds(e * LANES, LANES)] = high
            work_low[out_rows, pl.ds(e * LANES, LANES)] = low
    table_loads[1].wait()
    for h in range(2):
        for e in (0, 2):
            lanes = [pl.ds((e + i) * LANES + h * 128, 128) for i in range(2)]
            coeffs = tuple(
                jnp.concatenate([ref[:, lanes[0]], ref[:, lanes[1]]], axis=1) for ref in (work_high, work_low)
            )
            for first in range(0, planes, tile):
                out_rows = pl.ds(first, tile)
                value = dot3((backward_ref[0, out_rows, :], backward_ref[1, out_rows, :]), coeffs)
                for i in range(2):
                    for d in range(tile // depth):
                        goal = (first // depth + d) * block + (h * 4 + e + i) * depth
                        back_ref[pl.ds(goal, depth), :] = value[
                            d * depth : (d + 1) * depth, i * 128 : (i + 1) * 128
                        ]
        send_phase(back_ref, result_ref, back_send, back_recv, h)
    for k in range(1, n_elem):
        table_copy(k).wait_send()
    for h in range(2):
        wait_phase(sent_ref, values_ref, out_send, out_recv, h, True)
    for sweep in range(SWEEPS):
        for g in range(GROUPS):
            for copy in copies(sweep, g):
                copy.wait_send()
    for h in range(2):
        wait_phase(back_ref, result_ref, back_send, back_recv, h, True)
        wait_phase(back_ref, result_ref, back_send, back_recv, h, False)


def vmem():
    return pl.BlockSpec(memory_space=pltpu.VMEM)


def smem():
    return pl.BlockSpec(memory_space=pltpu.SMEM)


def hbm():
    return pl.BlockSpec(memory_space=pl.ANY)


def body(species, laplacian, binary, dref, stiff_eig, basis, rounds, adjacency, edge_map):
    n_span = lax.axis_size("span")
    n_elem = lax.axis_size("elem")
    depth = species.shape[2]
    own = species.shape[3]
    planes = depth * n_span
    flat = n_span * 8 * depth
    forward, backward = transform_tables(planes)
    hot, mask = selection_tables()
    halo = (SWEEPS, GROUPS, 4, planes // GROUPS // 2, 128)
    dma = pltpu.SemaphoreType.DMA
    returned, place = pl.pallas_call(
        functools.partial(main_kernel, n_span, n_elem, depth, own, MESH_X),
        out_shape=(
            jax.ShapeDtypeStruct((flat, 128), F32),
            jax.ShapeDtypeStruct((own, own), F32),
        ),
        in_specs=[hbm(), hbm(), smem(), smem()] + [vmem()] * 7 + [hbm(), hbm()],
        out_specs=(vmem(), vmem()),
        scratch_shapes=[
            pltpu.VMEM((NS * depth, own), F32),
            pltpu.VMEM((NS * depth, own), F32),
            pltpu.VMEM((LANES * depth, own), F32),
            pltpu.VMEM((n_elem * 8, own), jnp.int32),
            pltpu.SMEM((n_elem * 8, own), jnp.int32),
            pltpu.SMEM((own,), jnp.int32),
            pltpu.VMEM((136, 128), F32),
            pltpu.VMEM((2, planes, planes), BF16),
            pltpu.VMEM((2, planes, planes), BF16),
            pltpu.VMEM((flat, 128), F32),
            pltpu.VMEM((flat, 128), F32),
            pltpu.VMEM((flat, 128), F32),
            pltpu.VMEM((planes, 4 * LANES), BF16),
            pltpu.VMEM((planes, 4 * LANES), BF16),
            pltpu.VMEM((4, planes, LANES), F32),
            pltpu.VMEM((4, planes, LANES), F32),
            pltpu.VMEM((planes, LANES), F32),
            pltpu.VMEM((planes, 128), F32),
            pltpu.VMEM((4, planes, 128), F32),
            pltpu.VMEM(halo, F32),
            pltpu.VMEM(halo, F32),
            dma((6,)),
            dma,
            dma((n_elem,)),
            dma((n_elem,)),
            dma((2, n_span)),
            dma((2, n_span)),
            dma((2, n_span)),
            dma((2, n_span)),
            dma(halo[:3]),
            dma(halo[:3]),
        ],
        compiler_params=pltpu.CompilerParams(
            collective_id=0, has_side_effects=True, vmem_limit_bytes=VMEM_LIMIT
        ),
        name="main",
    )(
        species.reshape(NS * depth, own),
        laplacian.reshape(NS * depth, own),
        binary,
        dref,
        stiff_eig.reshape(1, PER_SIDE),
        basis,
        rounds.reshape(1, planes // 2),
        adjacency.T,
        edge_map.T,
        hot,
        mask,
        split_table(forward),
        split_table(backward),
    )
    updated = pl.pallas_call(
        functools.partial(finish_kernel, n_span, depth, own),
        out_shape=jax.ShapeDtypeStruct((NS * depth, own), F32),
        in_specs=[vmem(), vmem()],
        out_specs=vmem(),
        compiler_params=pltpu.CompilerParams(vmem_limit_bytes=VMEM_LIMIT),
        name="finish",
    )(returned, place)
    return updated.reshape(species.shape)


def solution(mesh):
    return jax.shard_map(
        body,
        mesh=mesh,
        in_specs=(
            P(None, None, "span", "elem"),
            P(None, None, "span", "elem"),
            P(),
            P(),
            P(),
            P(),
            P(),
            P("elem", None),
            P("elem", None),
        ),
        out_specs=P(None, None, "span", "elem"),
        check_vma=False,
    )
```

```python
import functools

import jax
import jax.numpy as jnp
import numpy as np
from jax import lax
from jax.experimental import pallas as pl
from jax.experimental.pallas import tpu as pltpu
from jax.sharding import PartitionSpec as P

MESH_X = 16
PER_SIDE = 9
SPECIES = 3
NS = PER_SIDE * PER_SIDE * SPECIES
LANES = 256
COUPLING = 0.2
SWEEPS = 3
GROUPS = 4
F32 = jnp.float32
BF16 = jnp.bfloat16
HIGHEST = lax.Precision.HIGHEST
MESH = pl.DeviceIdType.MESH
SOUTH, EAST, NORTH, WEST = 0, 1, 2, 3
VMEM_LIMIT = 60 * 1024 * 1024

NN_DIMS = (((1,), (0,)), ((), ()))
NT_DIMS = (((1,), (1,)), ((), ()))
TN_DIMS = (((0,), (0,)), ((), ()))


def split(x):
    high = x.astype(BF16)
    return high, (x - high.astype(F32)).astype(BF16)


def dot(a, b, dims=NN_DIMS):
    return lax.dot_general(a, b, dims, preferred_element_type=F32)


def dot3(a, b, dims=NN_DIMS):
    return dot(a[0], b[0], dims) + dot(a[0], b[1], dims) + dot(a[1], b[0], dims)


def edge_lists():
    last = PER_SIDE - 1
    return [
        [i for i in range(PER_SIDE)],
        [i * PER_SIDE + last for i in range(PER_SIDE)],
        [last * PER_SIDE + last - i for i in range(PER_SIDE)],
        [(last - i) * PER_SIDE for i in range(PER_SIDE)],
    ]


def selection_tables():
    pair = np.zeros((2, LANES, 128), np.float32)
    pair_s = np.full((LANES,), -1)
    for lane in range(NS):
        node, s = divmod(lane, SPECIES)
        pair[0, lane, node // PER_SIDE] = 1.0
        pair[1, lane, node % PER_SIDE] = 1.0
        pair_s[lane] = s
    trace = np.zeros((4, 128, 128), np.float32)
    trace_s = np.full((128,), -2)
    for d, nodes in enumerate(edge_lists()):
        for t in range(PER_SIDE):
            for s in range(SPECIES):
                lane = d * 32 + t * SPECIES + s
                trace_s[lane] = s
                back = nodes[PER_SIDE - 1 - t]
                trace[0, lane, nodes[t] // PER_SIDE] = 1.0
                trace[1, lane, nodes[t] % PER_SIDE] = 1.0
                trace[2, lane, back // PER_SIDE] = 1.0
                trace[3, lane, back % PER_SIDE] = 1.0
    pair_mask = (pair_s[:, None] == pair_s[None, :]) & (pair_s[:, None] >= 0)
    trace_mask = trace_s[:, None] == pair_s[None, :]
    hot = np.concatenate([pair.reshape(2 * LANES, 128), trace.reshape(512, 128)], axis=0)
    mask = np.concatenate([pair_mask, trace_mask], axis=0)
    return jnp.asarray(hot.astype(BF16)), jnp.asarray(mask.astype(np.float32))


def transform_tables(planes):
    modes = planes // 2
    phase = (np.arange(modes)[:, None] * np.arange(planes)[None, :]) % planes
    angle = phase.astype(np.float64) * (2.0 * np.pi / planes)
    trig = np.concatenate([np.cos(angle), -np.sin(angle)], axis=0)
    weight = np.where(np.arange(modes) == 0, 1.0, 2.0)
    weight = np.concatenate([weight, weight])
    return np.float32(trig / planes), np.float32((trig * weight[:, None]).T)


def split_table(table):
    high = table.astype(BF16)
    low = (table - high.astype(np.float32)).astype(BF16)
    return jnp.asarray(np.stack([high, low]))


def split3(x):
    high = x.astype(BF16)
    rest = x - high.astype(F32)
    middle = rest.astype(BF16)
    return high, middle, (rest - middle.astype(F32)).astype(BF16)


def pick(hot, x, dims=NN_DIMS):
    return sum(dot(hot, part, dims) for part in split3(x))


def pick_right(x, hot):
    return sum(dot(part, hot, NT_DIMS) for part in split3(x))


def place_back(n_span, depth, h, values_ref, stride, place, out_ref):
    count = min(NS - h * 128, 128)
    for first in range(0, depth, 8):
        parts = [
            values_ref[pl.ds(d * stride + e * depth + first, 8), :] for e in range(4) for d in range(n_span)
        ]
        by_plane = jnp.transpose(jnp.stack(parts, axis=0), (1, 0, 2))
        moved = []
        for plane in range(8):
            high, low = split(by_plane[plane])
            moved.append(dot(high, place, TN_DIMS) + dot(low, place, TN_DIMS))
        by_lane = jnp.transpose(jnp.stack(moved, axis=0), (1, 0, 2))
        for lane in range(count):
            out_ref[pl.ds(lane * depth + first, 8), :] = by_lane[lane]


def finish_kernel(
    n_span, depth, own, half_hbm, values_hbm, place_ref, out_hbm, half_ref, values_ref, tail_ref, sems
):
    loads = [
        pltpu.make_async_copy(values_hbm, values_ref, sems.at[0]),
        pltpu.make_async_copy(half_hbm, half_ref, sems.at[1]),
    ]
    for copy in loads:
        copy.start()
    split_row = 128 * depth
    stores = [
        pltpu.make_async_copy(half_ref, out_hbm.at[pl.ds(0, split_row)], sems.at[2]),
        pltpu.make_async_copy(tail_ref, out_hbm.at[pl.ds(split_row, NS * depth - split_row)], sems.at[3]),
    ]
    loads[1].wait()
    stores[0].start()
    place = place_ref[...].astype(BF16)
    loads[0].wait()
    place_back(n_span, depth, 1, values_ref, 4 * depth, place, tail_ref)
    stores[1].start()
    stores[0].wait()
    stores[1].wait()


def neighbours(n_span, n_elem, block_rows):
    span, elem = lax.axis_index("span"), lax.axis_index("elem")
    x = span % block_rows
    odd = elem % 2
    up = 1 - 2 * odd
    block_row = jnp.where(odd == 1, block_rows - 1 - x, x)
    last, first = block_row == block_rows - 1, block_row == 0
    return {
        NORTH: (jnp.where(last, span, span + up), jnp.where(last, (elem + 1) % n_elem, elem)),
        SOUTH: (jnp.where(first, span, span - up), jnp.where(first, (elem + n_elem - 1) % n_elem, elem)),
        EAST: ((span + block_rows) % n_span, elem),
        WEST: ((span + n_span - block_rows) % n_span, elem),
    }


def table_kernel(n_elem, own, adjacency_ref, edge_map_ref, tables_ref, table_send, table_recv):
    span, elem = lax.axis_index("span"), lax.axis_index("elem")
    barrier = pltpu.get_barrier_semaphore()
    for k in range(1, n_elem):
        pl.semaphore_signal(
            barrier, inc=1, device_id=(span, (elem + k) % n_elem), device_id_type=MESH
        )

    ahead_id, ahead_edge = adjacency_ref[...], edge_map_ref[...]
    owner = ahead_id // own
    step = owner * (8 * own) + (ahead_edge + 2) % 4 * own + ahead_id % own
    before = (elem + n_elem - 1) % n_elem
    edge_ids = lax.broadcasted_iota(jnp.int32, (4, own), 0)
    elem_ids = lax.broadcasted_iota(jnp.int32, (4, own), 1)
    facing = jnp.where(owner == before, (edge_ids + 2) % 4 * own + elem_ids, 8 * own)
    start = jnp.min(jnp.min(facing, axis=0, keepdims=True), axis=1, keepdims=True)
    my_rows = pl.ds(pl.multiple_of(elem * 8, 8), 8)
    tables_ref[my_rows, :] = jnp.concatenate([step, jnp.broadcast_to(start, (4, own))], axis=0)

    pl.semaphore_wait(barrier, n_elem - 1)

    def table_copy(k):
        return pltpu.make_async_remote_copy(
            src_ref=tables_ref.at[my_rows],
            dst_ref=tables_ref.at[my_rows],
            send_sem=table_send.at[k],
            recv_sem=table_recv.at[k],
            device_id=(span, (elem + k) % n_elem),
            device_id_type=MESH,
        )

    for k in range(1, n_elem):
        table_copy(k).start()
    for k in range(1, n_elem):
        table_copy(k).wait()


def main_kernel(
    n_span,
    n_elem,
    depth,
    own,
    cols,
    species_hbm,
    laplacian_hbm,
    binary_ref,
    dref_ref,
    eig_ref,
    basis_ref,
    rounds_ref,
    walk_ref,
    hot_ref,
    mask_ref,
    forward_hbm,
    backward_hbm,
    half_ref,
    second_ref,
    place_ref,
    species_ref,
    laplacian_ref,
    source_ref,
    turn_ref,
    small_ref,
    forward_ref,
    backward_ref,
    sent_ref,
    values_ref,
    back_ref,
    result_ref,
    work_high,
    work_low,
    rhs_ref,
    modal_ref,
    inverse_ref,
    rounds_col,
    trace_ref,
    send_ref,
    recv_ref,
    load_sem,
    out_send,
    out_recv,
    back_send,
    back_recv,
    send_sem,
    recv_sem,
):
    planes = n_span * depth
    modes = planes // 2
    rows = own // cols
    block_rows = rows // 2
    group = planes // GROUPS
    half = group // 2
    tile = min(256, planes)
    block = 8 * depth
    nodes = PER_SIDE * PER_SIDE
    span, elem = lax.axis_index("span"), lax.axis_index("elem")
    near = neighbours(n_span, n_elem, block_rows)

    def span_peer(k):
        z = (span // block_rows + k // block_rows) % (n_span // block_rows)
        x = (span + k) % block_rows
        return z * block_rows + x

    barrier = pltpu.get_barrier_semaphore()

    def greet_span(k, carry):
        pl.semaphore_signal(barrier, inc=1, device_id=(span_peer(k), elem), device_id_type=MESH)
        return carry

    def greet_elem(k, carry):
        pl.semaphore_signal(
            barrier, inc=1, device_id=(span, (elem + k) % n_elem), device_id_type=MESH
        )
        return carry

    lax.fori_loop(1, n_elem, greet_elem, 0)
    lax.fori_loop(1, n_span, greet_span, 0)

    cut = (128 + SPECIES - 1) // SPECIES
    pieces = [(0, cut), (cut, nodes - cut)]
    loads = []
    for i, (first, count) in enumerate(pieces):
        span_rows = pl.ds(first * SPECIES * depth, count * SPECIES * depth)
        for j, (source, target) in enumerate(
            ((species_hbm, species_ref), (laplacian_hbm, laplacian_ref))
        ):
            copy = pltpu.make_async_copy(source.at[span_rows], target.at[span_rows], load_sem.at[i * 2 + j])
            copy.start()
            loads.append(copy)
    table_loads = [
        pltpu.make_async_copy(forward_hbm, forward_ref, load_sem.at[4]),
        pltpu.make_async_copy(backward_hbm, backward_ref, load_sem.at[5]),
    ]
    for copy in table_loads:
        copy.start()

    inverse = [[1.0 / binary_ref[s, j] for j in range(SPECIES + 1)] for s in range(SPECIES)]
    dref = [dref_ref[s] for s in range(SPECIES)]
    over = [1.0 / dref_ref[s] for s in range(SPECIES)]

    def sources(first, count):
        def one_node(node, carry):
            base = pl.multiple_of(node * SPECIES * depth, 8)
            parts = [species_ref[pl.ds(base + s * depth, depth), :] for s in range(SPECIES)]
            slopes = [laplacian_ref[pl.ds(base + s * depth, depth), :] for s in range(SPECIES)]
            bath = 1.0 - (parts[0] + parts[1] + parts[2])
            for s in range(SPECIES):
                resistance = bath * inverse[s][SPECIES]
                for j in range(SPECIES):
                    if j != s:
                        resistance = resistance + parts[j] * inverse[s][j]
                mixture = (1.0 - parts[s]) / resistance
                value = (parts[s] + (mixture - dref[s]) * slopes[s]) * over[s]
                source_ref[pl.ds(base + s * depth, depth), :] = value
            return carry

        lax.fori_loop(first, first + count, one_node, 0, unroll=2)

    source_ref[pl.ds(NS * depth, (LANES - NS) * depth), :] = jnp.zeros(((LANES - NS) * depth, own), F32)
    loads[0].wait()
    loads[1].wait()
    sources(*pieces[0])

    loads[2].wait()
    loads[3].wait()
    sources(*pieces[1])

    shift = own.bit_length() - 1

    def ahead(dart):
        return walk_ref[dart]

    odd = elem % 2
    dart = lax.fori_loop(0, rows * elem, lambda i, d: ahead(d), walk_ref[4 * own])
    norths = []
    for row in range(rows):
        norths.append(dart)
        if row + 1 < rows:
            dart = ahead(dart)
    easts = []
    for dart in norths:
        edge = (dart >> shift) & 7
        easts.append(dart + ((((edge + 3) & 3) - edge) << shift))
    lane = lax.broadcasted_iota(jnp.int32, (1, own), 1)
    places = [jnp.where(odd == 1, block_rows - 1 - i, i) for i in range(block_rows)]
    for col in range(cols):
        for row in range(rows):
            dart = easts[row]
            slot = (row % 2 * 2 + col % 2) * n_span + (col // 2) * block_rows + places[row // 2]
            turn_ref[slot] = dart
            place_ref[pl.ds(slot, 1), :] = (lane == (dart & (own - 1))).astype(F32)
            if col + 1 < cols:
                easts[row] = ahead(dart)

    def landing(target, h):
        if isinstance(target, tuple):
            return target[h].at[pl.ds(pl.multiple_of(span * (block // 2), 8), block // 2)]
        return target.at[pl.ds(pl.multiple_of(span * block + h * (block // 2), 8), block // 2)]

    def exchange(source, target, send, recv, k, h):
        peer = span_peer(k)
        return pltpu.make_async_remote_copy(
            src_ref=source.at[pl.ds(pl.multiple_of(peer * block + h * (block // 2), 8), block // 2)],
            dst_ref=landing(target, h),
            send_sem=send.at[h, k],
            recv_sem=recv.at[h, k],
            device_id=(peer, elem),
            device_id_type=MESH,
        )

    def send_phase(source, target, send, recv, h):
        def one(k, carry):
            exchange(source, target, send, recv, k, h).start()
            return carry

        lax.fori_loop(1, n_span, one, 0)
        mine = pl.ds(pl.multiple_of(span * block + h * (block // 2), 8), block // 2)
        landing(target, h)[...] = source[mine, :]

    def wait_phase(source, target, send, recv, h, sending):
        def one(k, carry):
            copy = exchange(source, target, send, recv, k, h)
            if sending:
                copy.wait_send()
            else:
                copy.wait_recv()
            return carry

        lax.fori_loop(1, n_span, one, 0)

    pl.semaphore_wait(barrier, n_span + n_elem - 2)
    place = place_ref[...].astype(BF16)
    for h in range(2):
        for first in range(0, depth, 8):
            moved = []
            for plane in range(first, first + 8):
                high, low = split(source_ref[pl.ds(h * 128 * depth + plane, 128, stride=depth), :])
                moved.append(dot(place, high, NT_DIMS) + dot(place, low, NT_DIMS))
            turned_planes = jnp.transpose(jnp.stack(moved, axis=0), (1, 0, 2))
            for slot in range(own):
                e, p = divmod(slot, n_span)
                sent_ref[pl.ds(p * block + (h * 4 + e) * depth + first, 8), :] = turned_planes[slot]
        send_phase(sent_ref, values_ref, out_send, out_recv, h)

    small_ref[...] = jnp.zeros_like(small_ref)
    small_ref[:PER_SIDE, :PER_SIDE] = basis_ref[...]
    small_ref[128 : 128 + 1, :PER_SIDE] = eig_ref[...]
    basis = small_ref[:128, :]
    hot_i, hot_j = hot_ref[:LANES, :], hot_ref[LANES : 2 * LANES, :]

    def spread(left_i, left_j):
        return pick_right(pick(left_i, basis), hot_i) * pick_right(pick(left_j, basis), hot_j)

    traces_hot = [hot_ref[pl.ds(2 * LANES + i * 128, 128), :] for i in range(4)]
    trace_mask = mask_ref[LANES:, :]
    pair = split(spread(hot_i, hot_j) * mask_ref[:LANES, :])
    out_trace = spread(traces_hot[0], traces_hot[1]) * trace_mask
    in_trace = spread(traces_hot[2], traces_hot[3]) * (COUPLING * trace_mask)

    sides = []
    for e in range(4):
        a, b = divmod(e, 2)
        groups = [0] * 4
        groups[b], groups[1 - b] = (SOUTH, NORTH) if a == 0 else (NORTH, SOUTH)
        groups[2 + a], groups[3 - a] = (WEST, EAST) if b == 0 else (EAST, WEST)
        sides.append(groups)

    def turned(matrix, e):
        edge = ((turn_ref[e * n_span + span] >> shift) + 3) & 3
        turn = jnp.full((32, LANES), edge, jnp.int32)
        edges = [matrix[d * 32 : (d + 1) * 32] for d in range(4)]
        blocks = []
        for d in sides[e]:
            chosen = edges[d]
            for r in range(1, 4):
                chosen = jnp.where(turn == r, edges[(d + r) % 4], chosen)
            blocks.append(chosen)
        return split(jnp.concatenate(blocks, axis=0))

    to_trace, from_trace = [], []
    for e in range(4):
        high, low = turned(out_trace, e)
        to_trace.append(jnp.concatenate([high, low], axis=0))
        high, low = turned(in_trace, e)
        from_trace.append((jnp.concatenate([high, high], axis=0), low))

    eig_row = small_ref[128:136, :]
    diag = (pick_right(eig_row, hot_i) + pick_right(eig_row, hot_j))[:1]
    pair_lane = lax.broadcasted_iota(jnp.int32, (1, LANES), 1)
    for s in range(SPECIES):
        diag = diag + jnp.where(pair_lane % SPECIES == s, over[s], 0.0)
    row = lax.broadcasted_iota(jnp.int32, (planes, LANES), 0)
    wave = jnp.where(row >= modes, row - modes, row).astype(F32) * (8.0 / planes)
    inverse_ref[...] = 1.0 / (wave * wave + diag)
    square = lax.broadcasted_iota(jnp.int32, (modes, modes), 0) == lax.broadcasted_iota(
        jnp.int32, (modes, modes), 1
    )
    spread_rounds = jnp.where(square, rounds_ref[...].astype(F32), 0.0).astype(BF16)
    column = dot(spread_rounds, jnp.ones((modes, 128), BF16))
    rounds_col[:modes, :] = column
    rounds_col[modes:, :] = column

    table_loads[0].wait()
    for h in range(2):
        wait_phase(sent_ref, values_ref, out_send, out_recv, h, False)
        for e in (0, 2):
            lanes = []
            for i in range(2):
                first = (h * 4 + e + i) * depth
                lanes.append(
                    jnp.concatenate(
                        [values_ref[pl.ds(d * block + first, depth), :] for d in range(n_span)], axis=0
                    )
                )
            planes_in = split(jnp.concatenate(lanes, axis=1))
            for first in range(0, planes, tile):
                out_rows = pl.ds(first, tile)
                value = split(dot3((forward_ref[0, out_rows, :], forward_ref[1, out_rows, :]), planes_in))
                for i in range(2):
                    target = pl.ds((e + i) * LANES + h * 128, 128)
                    work_high[out_rows, target] = value[0][:, i * 128 : (i + 1) * 128]
                    work_low[out_rows, target] = value[1][:, i * 128 : (i + 1) * 128]

    lane_group = lax.broadcasted_iota(jnp.int32, (1, 128), 1) // 32
    outer = {NORTH: (2, 3), SOUTH: (0, 1), EAST: (1, 3), WEST: (0, 2)}
    opposite = {NORTH: SOUTH, SOUTH: NORTH, EAST: WEST, WEST: EAST}

    def copies(sweep, g):
        return [
            pltpu.make_async_remote_copy(
                src_ref=send_ref.at[sweep, g, d],
                dst_ref=recv_ref.at[sweep, g, opposite[d]],
                send_sem=send_sem.at[sweep, g, d],
                recv_sem=recv_sem.at[sweep, g, opposite[d]],
                device_id=near[d],
                device_id_type=MESH,
            )
            for d in range(4)
        ]

    def send_traces(sweep, g):
        g_rows = pl.ds(g * group, group)
        traces = []
        for e in range(4):
            high, low = split(modal_ref[e, g_rows, :])
            both = dot(high, to_trace[e], NT_DIMS)
            trace = both[:, :128] + both[:, 128:] + dot(low, to_trace[e][:128], NT_DIMS)
            trace_ref[e, g_rows, :] = trace
            traces.append(trace)
        for d in range(4):
            one, two = (traces[i] for i in outer[d])
            first, second = (0, 1) if d in (NORTH, SOUTH) else (2, 3)
            joined = jnp.where(lane_group == first, one, two)
            low_half = jnp.logical_or(lane_group == first, lane_group == second)
            send_ref[sweep, g, d] = jnp.where(low_half, joined[:half], pltpu.roll(joined[half:], 64, 1))
        for copy in copies(sweep, g):
            copy.start()

    def update(sweep, g):
        for copy in copies(sweep, g):
            copy.wait_recv()
        g_rows = pl.ds(g * group, group)
        active = rounds_col[g_rows, :] > sweep + 1.5
        active = jnp.concatenate([active, active], axis=1)
        scale = inverse_ref[g_rows, :]
        outside = []
        for d in range(4):
            packed = recv_ref[sweep, g, d]
            outside.append(jnp.concatenate([packed, pltpu.roll(packed, 64, 1)], axis=0))
        for e in range(4):
            a, b = divmod(e, 2)
            across = jnp.where(
                lane_group < 2,
                jnp.where(
                    lane_group == b,
                    outside[SOUTH if a == 0 else NORTH],
                    trace_ref[2 * (1 - a) + b, g_rows, :],
                ),
                jnp.where(
                    lane_group == 2 + a,
                    outside[WEST if b == 0 else EAST],
                    trace_ref[2 * a + 1 - b, g_rows, :],
                ),
            )
            high, low = split(across)
            change = dot(jnp.concatenate([high, low], axis=1), from_trace[e][0]) + dot(high, from_trace[e][1])
            fresh = (rhs_ref[e, g_rows, :] + change) * scale
            modal_ref[e, g_rows, :] = jnp.where(active, fresh, modal_ref[e, g_rows, :])

    for g in range(GROUPS):
        g_rows = pl.ds(g * group, group)
        scale = inverse_ref[g_rows, :]
        for e in range(4):
            lanes = pl.ds(e * LANES, LANES)
            rhs = dot3((work_high[g_rows, lanes], work_low[g_rows, lanes]), pair)
            rhs_ref[e, g_rows, :] = rhs
            modal_ref[e, g_rows, :] = rhs * scale
        send_traces(0, g)
    for sweep in range(SWEEPS):
        for g in range(GROUPS):
            update(sweep, g)
            if sweep + 1 < SWEEPS:
                send_traces(sweep + 1, g)

    for e in range(4):
        for first in range(0, planes, tile):
            out_rows = pl.ds(first, tile)
            high, low = split(dot3(split(modal_ref[e, out_rows, :]), pair, NT_DIMS))
            work_high[out_rows, pl.ds(e * LANES, LANES)] = high
            work_low[out_rows, pl.ds(e * LANES, LANES)] = low
    table_loads[1].wait()
    for h in range(2):
        for e in (0, 2):
            lanes = [pl.ds((e + i) * LANES + h * 128, 128) for i in range(2)]
            coeffs = tuple(
                jnp.concatenate([ref[:, lanes[0]], ref[:, lanes[1]]], axis=1) for ref in (work_high, work_low)
            )
            for first in range(0, planes, tile):
                out_rows = pl.ds(first, tile)
                value = dot3((backward_ref[0, out_rows, :], backward_ref[1, out_rows, :]), coeffs)
                for i in range(2):
                    for d in range(tile // depth):
                        goal = (first // depth + d) * block + (h * 4 + e + i) * depth
                        back_ref[pl.ds(goal, depth), :] = value[
                            d * depth : (d + 1) * depth, i * 128 : (i + 1) * 128
                        ]
        send_phase(back_ref, (result_ref, second_ref), back_send, back_recv, h)
    for h in range(2):
        wait_phase(sent_ref, values_ref, out_send, out_recv, h, True)
    for sweep in range(SWEEPS):
        for g in range(GROUPS):
            for copy in copies(sweep, g):
                copy.wait_send()
    wait_phase(back_ref, (result_ref, second_ref), back_send, back_recv, 0, False)
    place_back(n_span, depth, 0, result_ref, 4 * depth, place, half_ref)
    wait_phase(back_ref, (result_ref, second_ref), back_send, back_recv, 0, True)
    wait_phase(back_ref, (result_ref, second_ref), back_send, back_recv, 1, True)
    wait_phase(back_ref, (result_ref, second_ref), back_send, back_recv, 1, False)


def vmem():
    return pl.BlockSpec(memory_space=pltpu.VMEM)


def smem():
    return pl.BlockSpec(memory_space=pltpu.SMEM)


def hbm():
    return pl.BlockSpec(memory_space=pl.ANY)


def body(species, laplacian, binary, dref, stiff_eig, basis, rounds, adjacency, edge_map):
    n_span = lax.axis_size("span")
    n_elem = lax.axis_size("elem")
    depth = species.shape[2]
    own = species.shape[3]
    planes = depth * n_span
    flat = n_span * 8 * depth
    forward, backward = transform_tables(planes)
    hot, mask = selection_tables()
    halo = (SWEEPS, GROUPS, 4, planes // GROUPS // 2, 128)
    dma = pltpu.SemaphoreType.DMA
    tables = pl.pallas_call(
        functools.partial(table_kernel, n_elem, own),
        out_shape=jax.ShapeDtypeStruct((n_elem * 8, own), jnp.int32),
        in_specs=[vmem(), vmem()],
        out_specs=vmem(),
        scratch_shapes=[dma((n_elem,)), dma((n_elem,))],
        compiler_params=pltpu.CompilerParams(collective_id=1, has_side_effects=True),
        name="tables",
    )(adjacency.T, edge_map.T).reshape(n_elem * 8 * own)
    first_half, second_half, place = pl.pallas_call(
        functools.partial(main_kernel, n_span, n_elem, depth, own, MESH_X),
        out_shape=(
            jax.ShapeDtypeStruct((128 * depth, own), F32),
            jax.ShapeDtypeStruct((flat // 2, 128), F32),
            jax.ShapeDtypeStruct((own, own), F32),
        ),
        in_specs=[hbm(), hbm(), smem(), smem()] + [vmem()] * 3 + [smem()] + [vmem()] * 2 + [hbm(), hbm()],
        out_specs=(vmem(), vmem(), vmem()),
        scratch_shapes=[
            pltpu.VMEM((NS * depth, own), F32),
            pltpu.VMEM((NS * depth, own), F32),
            pltpu.VMEM((LANES * depth, own), F32),
            pltpu.SMEM((own,), jnp.int32),
            pltpu.VMEM((136, 128), F32),
            pltpu.VMEM((2, planes, planes), BF16),
            pltpu.VMEM((2, planes, planes), BF16),
            pltpu.VMEM((flat, 128), F32),
            pltpu.VMEM((flat, 128), F32),
            pltpu.VMEM((flat, 128), F32),
            pltpu.VMEM((flat // 2, 128), F32),
            pltpu.VMEM((planes, 4 * LANES), BF16),
            pltpu.VMEM((planes, 4 * LANES), BF16),
            pltpu.VMEM((4, planes, LANES), F32),
            pltpu.VMEM((4, planes, LANES), F32),
            pltpu.VMEM((planes, LANES), F32),
            pltpu.VMEM((planes, 128), F32),
            pltpu.VMEM((4, planes, 128), F32),
            pltpu.VMEM(halo, F32),
            pltpu.VMEM(halo, F32),
            dma((6,)),
            dma((2, n_span)),
            dma((2, n_span)),
            dma((2, n_span)),
            dma((2, n_span)),
            dma(halo[:3]),
            dma(halo[:3]),
        ],
        compiler_params=pltpu.CompilerParams(
            collective_id=0, has_side_effects=True, vmem_limit_bytes=VMEM_LIMIT
        ),
        name="main",
    )(
        species.reshape(NS * depth, own),
        laplacian.reshape(NS * depth, own),
        binary,
        dref,
        stiff_eig.reshape(1, PER_SIDE),
        basis,
        rounds.reshape(1, planes // 2),
        tables,
        hot,
        mask,
        split_table(forward),
        split_table(backward),
    )
    updated = pl.pallas_call(
        functools.partial(finish_kernel, n_span, depth, own),
        out_shape=jax.ShapeDtypeStruct((NS * depth, own), F32),
        in_specs=[hbm(), hbm(), vmem()],
        out_specs=hbm(),
        scratch_shapes=[
            pltpu.VMEM((128 * depth, own), F32),
            pltpu.VMEM((flat // 2, 128), F32),
            pltpu.VMEM((NS * depth - 128 * depth, own), F32),
            dma((4,)),
        ],
        name="finish",
    )(first_half, second_half, place)
    return updated.reshape(species.shape)


def solution(mesh):
    return jax.shard_map(
        body,
        mesh=mesh,
        in_specs=(
            P(None, None, "span", "elem"),
            P(None, None, "span", "elem"),
            P(),
            P(),
            P(),
            P(),
            P(),
            P("elem", None),
            P("elem", None),
        ),
        out_specs=P(None, None, "span", "elem"),
        check_vma=False,
    )
```

```python
import functools

import jax
import jax.numpy as jnp
import numpy as np
from jax import lax
from jax.experimental import pallas as pl
from jax.experimental.pallas import tpu as pltpu
from jax.sharding import PartitionSpec as P

MESH_X = 16
PER_SIDE = 9
SPECIES = 3
NS = PER_SIDE * PER_SIDE * SPECIES
LANES = 256
COUPLING = 0.2
SWEEPS = 3
GROUPS = 4
F32 = jnp.float32
BF16 = jnp.bfloat16
HIGHEST = lax.Precision.HIGHEST
MESH = pl.DeviceIdType.MESH
SOUTH, EAST, NORTH, WEST = 0, 1, 2, 3
VMEM_LIMIT = 60 * 1024 * 1024

NN_DIMS = (((1,), (0,)), ((), ()))
NT_DIMS = (((1,), (1,)), ((), ()))
TN_DIMS = (((0,), (0,)), ((), ()))


def split(x):
    high = x.astype(BF16)
    return high, (x - high.astype(F32)).astype(BF16)


def dot(a, b, dims=NN_DIMS):
    return lax.dot_general(a, b, dims, preferred_element_type=F32)


def dot3(a, b, dims=NN_DIMS):
    return dot(a[0], b[0], dims) + dot(a[0], b[1], dims) + dot(a[1], b[0], dims)


def edge_lists():
    last = PER_SIDE - 1
    return [
        [i for i in range(PER_SIDE)],
        [i * PER_SIDE + last for i in range(PER_SIDE)],
        [last * PER_SIDE + last - i for i in range(PER_SIDE)],
        [(last - i) * PER_SIDE for i in range(PER_SIDE)],
    ]


def selection_tables():
    pair = np.zeros((2, LANES, 128), np.float32)
    for lane in range(NS):
        node, s = divmod(lane, SPECIES)
        pair[0, lane, node // PER_SIDE] = 1.0
        pair[1, lane, node % PER_SIDE] = 1.0
    trace = np.zeros((4, 128, 128), np.float32)
    for d, nodes in enumerate(edge_lists()):
        for t in range(PER_SIDE):
            for s in range(SPECIES):
                lane = d * 32 + t * SPECIES + s
                back = nodes[PER_SIDE - 1 - t]
                trace[0, lane, nodes[t] // PER_SIDE] = 1.0
                trace[1, lane, nodes[t] % PER_SIDE] = 1.0
                trace[2, lane, back // PER_SIDE] = 1.0
                trace[3, lane, back % PER_SIDE] = 1.0
    hot = np.concatenate([pair.reshape(2 * LANES, 128), trace.reshape(512, 128)], axis=0)
    return jnp.asarray(hot.astype(BF16))


def transform_tables(planes):
    modes = planes // 2
    phase = (np.arange(modes)[:, None] * np.arange(planes)[None, :]) % planes
    angle = phase.astype(np.float64) * (2.0 * np.pi / planes)
    trig = np.concatenate([np.cos(angle), -np.sin(angle)], axis=0)
    return np.float32(trig / planes)


def split_table(table):
    high = table.astype(BF16)
    low = (table - high.astype(np.float32)).astype(BF16)
    return jnp.asarray(np.stack([high, low]))


def split3(x):
    high = x.astype(BF16)
    rest = x - high.astype(F32)
    middle = rest.astype(BF16)
    return high, middle, (rest - middle.astype(F32)).astype(BF16)


def pick(hot, x, dims=NN_DIMS):
    return sum(dot(hot, part, dims) for part in split3(x))


def pick_right(x, hot):
    return sum(dot(part, hot, NT_DIMS) for part in split3(x))


def place_back(n_span, depth, h, values_ref, stride, place, out_ref):
    count = min(NS - h * 128, 128)
    for first in range(0, depth, 8):
        parts = [
            values_ref[pl.ds(d * stride + e * depth + first, 8), :] for e in range(4) for d in range(n_span)
        ]
        by_plane = jnp.transpose(jnp.stack(parts, axis=0), (1, 0, 2))
        moved = []
        for plane in range(8):
            high, low = split(by_plane[plane])
            moved.append(dot(high, place, TN_DIMS) + dot(low, place, TN_DIMS))
        by_lane = jnp.transpose(jnp.stack(moved, axis=0), (1, 0, 2))
        for lane in range(count):
            out_ref[pl.ds(lane * depth + first, 8), :] = by_lane[lane]


def finish_kernel(
    n_span, depth, own, half_hbm, values_hbm, place_ref, out_hbm, half_ref, values_ref, tail_ref, sems
):
    loads = [
        pltpu.make_async_copy(values_hbm, values_ref, sems.at[0]),
        pltpu.make_async_copy(half_hbm, half_ref, sems.at[1]),
    ]
    for copy in loads:
        copy.start()
    split_row = 128 * depth
    stores = [
        pltpu.make_async_copy(half_ref, out_hbm.at[pl.ds(0, split_row)], sems.at[2]),
        pltpu.make_async_copy(tail_ref, out_hbm.at[pl.ds(split_row, NS * depth - split_row)], sems.at[3]),
    ]
    loads[1].wait()
    stores[0].start()
    place = place_ref[...].astype(BF16)
    loads[0].wait()
    place_back(n_span, depth, 1, values_ref, 4 * depth, place, tail_ref)
    stores[1].start()
    stores[0].wait()
    stores[1].wait()


def neighbours(n_span, n_elem, block_rows):
    span, elem = lax.axis_index("span"), lax.axis_index("elem")
    x = span % block_rows
    odd = elem % 2
    up = 1 - 2 * odd
    block_row = jnp.where(odd == 1, block_rows - 1 - x, x)
    last, first = block_row == block_rows - 1, block_row == 0
    return {
        NORTH: (jnp.where(last, span, span + up), jnp.where(last, (elem + 1) % n_elem, elem)),
        SOUTH: (jnp.where(first, span, span - up), jnp.where(first, (elem + n_elem - 1) % n_elem, elem)),
        EAST: ((span + block_rows) % n_span, elem),
        WEST: ((span + n_span - block_rows) % n_span, elem),
    }


def table_kernel(n_elem, own, adjacency_ref, edge_map_ref, tables_ref, table_send, table_recv):
    span, elem = lax.axis_index("span"), lax.axis_index("elem")
    barrier = pltpu.get_barrier_semaphore()
    for k in range(1, n_elem):
        pl.semaphore_signal(
            barrier, inc=1, device_id=(span, (elem + k) % n_elem), device_id_type=MESH
        )

    ahead_id, ahead_edge = adjacency_ref[...], edge_map_ref[...]
    owner = ahead_id // own
    step = owner * (8 * own) + (ahead_edge + 2) % 4 * own + ahead_id % own
    before = (elem + n_elem - 1) % n_elem
    edge_ids = lax.broadcasted_iota(jnp.int32, (4, own), 0)
    elem_ids = lax.broadcasted_iota(jnp.int32, (4, own), 1)
    facing = jnp.where(owner == before, (edge_ids + 2) % 4 * own + elem_ids, 8 * own)
    start = jnp.min(jnp.min(facing, axis=0, keepdims=True), axis=1, keepdims=True)
    my_rows = pl.ds(pl.multiple_of(elem * 8, 8), 8)
    tables_ref[my_rows, :] = jnp.concatenate([step, jnp.broadcast_to(start, (4, own))], axis=0)

    pl.semaphore_wait(barrier, n_elem - 1)

    def table_copy(k):
        return pltpu.make_async_remote_copy(
            src_ref=tables_ref.at[my_rows],
            dst_ref=tables_ref.at[my_rows],
            send_sem=table_send.at[k],
            recv_sem=table_recv.at[k],
            device_id=(span, (elem + k) % n_elem),
            device_id_type=MESH,
        )

    for k in range(1, n_elem):
        table_copy(k).start()
    for k in range(1, n_elem):
        table_copy(k).wait()


def main_kernel(
    n_span,
    n_elem,
    depth,
    own,
    cols,
    species_hbm,
    laplacian_hbm,
    binary_ref,
    dref_ref,
    eig_ref,
    basis_ref,
    rounds_ref,
    walk_ref,
    hot_ref,
    forward_hbm,
    half_ref,
    second_ref,
    place_ref,
    species_ref,
    laplacian_ref,
    source_ref,
    turn_ref,
    small_ref,
    forward_ref,
    backward_ref,
    sent_ref,
    values_ref,
    back_ref,
    result_ref,
    work_high,
    work_low,
    rhs_ref,
    modal_ref,
    inverse_ref,
    rounds_col,
    trace_ref,
    send_ref,
    recv_ref,
    load_sem,
    out_send,
    out_recv,
    back_send,
    back_recv,
    send_sem,
    recv_sem,
):
    planes = n_span * depth
    modes = planes // 2
    rows = own // cols
    block_rows = rows // 2
    group = planes // GROUPS
    half = group // 2
    tile = min(256, planes)
    block = 8 * depth
    nodes = PER_SIDE * PER_SIDE
    span, elem = lax.axis_index("span"), lax.axis_index("elem")
    near = neighbours(n_span, n_elem, block_rows)

    def span_peer(k):
        z = (span // block_rows + k // block_rows) % (n_span // block_rows)
        x = (span + k) % block_rows
        return z * block_rows + x

    barrier = pltpu.get_barrier_semaphore()

    def greet_span(k, carry):
        pl.semaphore_signal(barrier, inc=1, device_id=(span_peer(k), elem), device_id_type=MESH)
        return carry

    def greet_elem(k, carry):
        pl.semaphore_signal(
            barrier, inc=1, device_id=(span, (elem + k) % n_elem), device_id_type=MESH
        )
        return carry

    lax.fori_loop(1, n_elem, greet_elem, 0)
    lax.fori_loop(1, n_span, greet_span, 0)

    cut = (128 + SPECIES - 1) // SPECIES
    pieces = [(0, cut), (cut, nodes - cut)]
    loads = []
    for i, (first, count) in enumerate(pieces):
        span_rows = pl.ds(first * SPECIES * depth, count * SPECIES * depth)
        for j, (source, target) in enumerate(
            ((species_hbm, species_ref), (laplacian_hbm, laplacian_ref))
        ):
            copy = pltpu.make_async_copy(source.at[span_rows], target.at[span_rows], load_sem.at[i * 2 + j])
            copy.start()
            loads.append(copy)
    table_load = pltpu.make_async_copy(forward_hbm, forward_ref, load_sem.at[4])
    table_load.start()

    inverse = [[1.0 / binary_ref[s, j] for j in range(SPECIES + 1)] for s in range(SPECIES)]
    dref = [dref_ref[s] for s in range(SPECIES)]
    over = [1.0 / dref_ref[s] for s in range(SPECIES)]

    def sources(first, count):
        def one_node(node, carry):
            base = pl.multiple_of(node * SPECIES * depth, 8)
            parts = [species_ref[pl.ds(base + s * depth, depth), :] for s in range(SPECIES)]
            slopes = [laplacian_ref[pl.ds(base + s * depth, depth), :] for s in range(SPECIES)]
            bath = 1.0 - (parts[0] + parts[1] + parts[2])
            for s in range(SPECIES):
                resistance = bath * inverse[s][SPECIES]
                for j in range(SPECIES):
                    if j != s:
                        resistance = resistance + parts[j] * inverse[s][j]
                mixture = (1.0 - parts[s]) / resistance
                value = (parts[s] + (mixture - dref[s]) * slopes[s]) * over[s]
                source_ref[pl.ds(base + s * depth, depth), :] = value
            return carry

        lax.fori_loop(first, first + count, one_node, 0, unroll=2)

    source_ref[pl.ds(NS * depth, (LANES - NS) * depth), :] = jnp.zeros(((LANES - NS) * depth, own), F32)
    loads[0].wait()
    loads[1].wait()
    sources(*pieces[0])

    loads[2].wait()
    loads[3].wait()
    sources(*pieces[1])

    shift = own.bit_length() - 1

    def ahead(dart):
        return walk_ref[dart]

    odd = elem % 2
    dart = lax.fori_loop(0, rows * elem, lambda i, d: ahead(d), walk_ref[4 * own])
    norths = []
    for row in range(rows):
        norths.append(dart)
        if row + 1 < rows:
            dart = ahead(dart)
    easts = []
    for dart in norths:
        edge = (dart >> shift) & 7
        easts.append(dart + ((((edge + 3) & 3) - edge) << shift))
    lane = lax.broadcasted_iota(jnp.int32, (1, own), 1)
    places = [jnp.where(odd == 1, block_rows - 1 - i, i) for i in range(block_rows)]
    for col in range(cols):
        for row in range(rows):
            dart = easts[row]
            slot = (row % 2 * 2 + col % 2) * n_span + (col // 2) * block_rows + places[row // 2]
            turn_ref[slot] = dart
            place_ref[pl.ds(slot, 1), :] = (lane == (dart & (own - 1))).astype(F32)
            if col + 1 < cols:
                easts[row] = ahead(dart)

    def landing(target, h):
        if isinstance(target, tuple):
            return target[h].at[pl.ds(pl.multiple_of(span * (block // 2), 8), block // 2)]
        return target.at[pl.ds(pl.multiple_of(span * block + h * (block // 2), 8), block // 2)]

    def exchange(source, target, send, recv, k, h):
        peer = span_peer(k)
        return pltpu.make_async_remote_copy(
            src_ref=source.at[pl.ds(pl.multiple_of(peer * block + h * (block // 2), 8), block // 2)],
            dst_ref=landing(target, h),
            send_sem=send.at[h, k],
            recv_sem=recv.at[h, k],
            device_id=(peer, elem),
            device_id_type=MESH,
        )

    def send_phase(source, target, send, recv, h):
        def one(k, carry):
            exchange(source, target, send, recv, k, h).start()
            return carry

        lax.fori_loop(1, n_span, one, 0)
        mine = pl.ds(pl.multiple_of(span * block + h * (block // 2), 8), block // 2)
        landing(target, h)[...] = source[mine, :]

    def wait_phase(source, target, send, recv, h, sending):
        def one(k, carry):
            copy = exchange(source, target, send, recv, k, h)
            if sending:
                copy.wait_send()
            else:
                copy.wait_recv()
            return carry

        lax.fori_loop(1, n_span, one, 0)

    pl.semaphore_wait(barrier, n_span + n_elem - 2)
    place = place_ref[...].astype(BF16)
    for h in range(2):
        for first in range(0, depth, 8):
            moved = []
            for plane in range(first, first + 8):
                high, low = split(source_ref[pl.ds(h * 128 * depth + plane, 128, stride=depth), :])
                moved.append(dot(place, high, NT_DIMS) + dot(place, low, NT_DIMS))
            turned_planes = jnp.transpose(jnp.stack(moved, axis=0), (1, 0, 2))
            for slot in range(own):
                e, p = divmod(slot, n_span)
                sent_ref[pl.ds(p * block + (h * 4 + e) * depth + first, 8), :] = turned_planes[slot]
        send_phase(sent_ref, values_ref, out_send, out_recv, h)

    small_ref[...] = jnp.zeros_like(small_ref)
    small_ref[:PER_SIDE, :PER_SIDE] = basis_ref[...]
    small_ref[128 : 128 + 1, :PER_SIDE] = eig_ref[...]
    basis = small_ref[:128, :]
    hot_i, hot_j = hot_ref[:LANES, :], hot_ref[LANES : 2 * LANES, :]

    def spread(left_i, left_j):
        return pick_right(pick(left_i, basis), hot_i) * pick_right(pick(left_j, basis), hot_j)

    traces_hot = [hot_ref[pl.ds(2 * LANES + i * 128, 128), :] for i in range(4)]

    def same_species(shape, width):
        left = lax.broadcasted_iota(jnp.int32, shape, 0) % width % SPECIES
        return left == lax.broadcasted_iota(jnp.int32, shape, 1) % SPECIES

    pair_same, trace_same = same_species((LANES, LANES), LANES), same_species((128, LANES), 32)
    pair = split(jnp.where(pair_same, spread(hot_i, hot_j), 0.0))
    out_trace = jnp.where(trace_same, spread(traces_hot[0], traces_hot[1]), 0.0)
    in_trace = jnp.where(trace_same, COUPLING * spread(traces_hot[2], traces_hot[3]), 0.0)

    sides = []
    for e in range(4):
        a, b = divmod(e, 2)
        groups = [0] * 4
        groups[b], groups[1 - b] = (SOUTH, NORTH) if a == 0 else (NORTH, SOUTH)
        groups[2 + a], groups[3 - a] = (WEST, EAST) if b == 0 else (EAST, WEST)
        sides.append(groups)

    def turned(matrix, e):
        edge = ((turn_ref[e * n_span + span] >> shift) + 3) & 3
        turn = jnp.full((32, LANES), edge, jnp.int32)
        edges = [matrix[d * 32 : (d + 1) * 32] for d in range(4)]
        blocks = []
        for d in sides[e]:
            chosen = edges[d]
            for r in range(1, 4):
                chosen = jnp.where(turn == r, edges[(d + r) % 4], chosen)
            blocks.append(chosen)
        return split(jnp.concatenate(blocks, axis=0))

    to_trace, from_trace = [], []
    for e in range(4):
        high, low = turned(out_trace, e)
        to_trace.append(jnp.concatenate([high, low], axis=0))
        high, low = turned(in_trace, e)
        from_trace.append((jnp.concatenate([high, high], axis=0), low))

    eig_row = small_ref[128:136, :]
    diag = (pick_right(eig_row, hot_i) + pick_right(eig_row, hot_j))[:1]
    pair_lane = lax.broadcasted_iota(jnp.int32, (1, LANES), 1)
    for s in range(SPECIES):
        diag = diag + jnp.where(pair_lane % SPECIES == s, over[s], 0.0)
    row = lax.broadcasted_iota(jnp.int32, (planes, LANES), 0)
    wave = jnp.where(row >= modes, row - modes, row).astype(F32) * (8.0 / planes)
    inverse_ref[...] = 1.0 / (wave * wave + diag)
    square = lax.broadcasted_iota(jnp.int32, (modes, modes), 0) == lax.broadcasted_iota(
        jnp.int32, (modes, modes), 1
    )
    spread_rounds = jnp.where(square, rounds_ref[...].astype(F32), 0.0).astype(BF16)
    column = dot(spread_rounds, jnp.ones((modes, 128), BF16))
    rounds_col[:modes, :] = column
    rounds_col[modes:, :] = column

    table_load.wait()
    for part in range(2):
        for first in range(0, planes, min(128, planes)):
            strip = pl.ds(first, min(128, planes))
            turned_strip = forward_ref[part, strip, :].astype(F32).T
            backward_ref[part, :, strip] = turned_strip.astype(BF16)
    for h in range(2):
        wait_phase(sent_ref, values_ref, out_send, out_recv, h, False)
        for e in (0, 2):
            lanes = []
            for i in range(2):
                first = (h * 4 + e + i) * depth
                lanes.append(
                    jnp.concatenate(
                        [values_ref[pl.ds(d * block + first, depth), :] for d in range(n_span)], axis=0
                    )
                )
            planes_in = split(jnp.concatenate(lanes, axis=1))
            for first in range(0, planes, tile):
                out_rows = pl.ds(first, tile)
                value = split(dot3((forward_ref[0, out_rows, :], forward_ref[1, out_rows, :]), planes_in))
                for i in range(2):
                    target = pl.ds((e + i) * LANES + h * 128, 128)
                    work_high[out_rows, target] = value[0][:, i * 128 : (i + 1) * 128]
                    work_low[out_rows, target] = value[1][:, i * 128 : (i + 1) * 128]

    lane_group = lax.broadcasted_iota(jnp.int32, (1, 128), 1) // 32
    outer = {NORTH: (2, 3), SOUTH: (0, 1), EAST: (1, 3), WEST: (0, 2)}
    opposite = {NORTH: SOUTH, SOUTH: NORTH, EAST: WEST, WEST: EAST}

    def copies(sweep, g):
        return [
            pltpu.make_async_remote_copy(
                src_ref=send_ref.at[sweep, g, d],
                dst_ref=recv_ref.at[sweep, g, opposite[d]],
                send_sem=send_sem.at[sweep, g, d],
                recv_sem=recv_sem.at[sweep, g, opposite[d]],
                device_id=near[d],
                device_id_type=MESH,
            )
            for d in range(4)
        ]

    def send_traces(sweep, g):
        g_rows = pl.ds(pl.multiple_of(g * group, group), group)
        traces = []
        for e in range(4):
            high, low = split(modal_ref[e, g_rows, :])
            both = dot(high, to_trace[e], NT_DIMS)
            trace = both[:, :128] + both[:, 128:] + dot(low, to_trace[e][:128], NT_DIMS)
            trace_ref[e, g_rows, :] = trace
            traces.append(trace)
        for d in range(4):
            one, two = (traces[i] for i in outer[d])
            first, second = (0, 1) if d in (NORTH, SOUTH) else (2, 3)
            joined = jnp.where(lane_group == first, one, two)
            low_half = jnp.logical_or(lane_group == first, lane_group == second)
            send_ref[sweep, g, d] = jnp.where(low_half, joined[:half], pltpu.roll(joined[half:], 64, 1))
        for copy in copies(sweep, g):
            copy.start()

    def update(sweep, g):
        for copy in copies(sweep, g):
            copy.wait_recv()
        g_rows = pl.ds(pl.multiple_of(g * group, group), group)
        active = rounds_col[g_rows, :] > jnp.asarray(sweep, F32) + 1.5
        active = jnp.concatenate([active, active], axis=1)
        scale = inverse_ref[g_rows, :]
        outside = []
        for d in range(4):
            packed = recv_ref[sweep, g, d]
            outside.append(jnp.concatenate([packed, pltpu.roll(packed, 64, 1)], axis=0))
        for e in range(4):
            a, b = divmod(e, 2)
            across = jnp.where(
                lane_group < 2,
                jnp.where(
                    lane_group == b,
                    outside[SOUTH if a == 0 else NORTH],
                    trace_ref[2 * (1 - a) + b, g_rows, :],
                ),
                jnp.where(
                    lane_group == 2 + a,
                    outside[WEST if b == 0 else EAST],
                    trace_ref[2 * a + 1 - b, g_rows, :],
                ),
            )
            high, low = split(across)
            change = dot(jnp.concatenate([high, low], axis=1), from_trace[e][0]) + dot(high, from_trace[e][1])
            fresh = (rhs_ref[e, g_rows, :] + change) * scale
            modal_ref[e, g_rows, :] = jnp.where(active, fresh, modal_ref[e, g_rows, :])

    def begin(g, carry):
        g_rows = pl.ds(pl.multiple_of(g * group, group), group)
        scale = inverse_ref[g_rows, :]
        for e in range(4):
            lanes = pl.ds(e * LANES, LANES)
            rhs = dot3((work_high[g_rows, lanes], work_low[g_rows, lanes]), pair)
            rhs_ref[e, g_rows, :] = rhs
            modal_ref[e, g_rows, :] = rhs * scale
        send_traces(0, g)
        return carry

    def sweep_on(i, carry):
        sweep, g = i // GROUPS, i % GROUPS
        update(sweep, g)
        send_traces(sweep + 1, g)
        return carry

    def sweep_last(g, carry):
        update(SWEEPS - 1, g)
        return carry

    lax.fori_loop(0, GROUPS, begin, 0)
    lax.fori_loop(0, (SWEEPS - 1) * GROUPS, sweep_on, 0)
    lax.fori_loop(0, GROUPS, sweep_last, 0)

    tile_row = lax.broadcasted_iota(jnp.int32, (tile, LANES), 0)
    for first in range(0, planes, tile):
        out_rows = pl.ds(first, tile)
        column = tile_row + first
        constant = jnp.logical_or(column == 0, column == modes)
        weight = jnp.where(constant, float(planes), float(2 * planes))
        for e in range(4):
            high, low = split(dot3(split(modal_ref[e, out_rows, :]), pair, NT_DIMS) * weight)
            work_high[out_rows, pl.ds(e * LANES, LANES)] = high
            work_low[out_rows, pl.ds(e * LANES, LANES)] = low
    for h in range(2):
        for e in (0, 2):
            lanes = [pl.ds((e + i) * LANES + h * 128, 128) for i in range(2)]
            coeffs = tuple(
                jnp.concatenate([ref[:, lanes[0]], ref[:, lanes[1]]], axis=1) for ref in (work_high, work_low)
            )
            for first in range(0, planes, tile):
                out_rows = pl.ds(first, tile)
                value = dot3((backward_ref[0, out_rows, :], backward_ref[1, out_rows, :]), coeffs)
                for i in range(2):
                    for d in range(tile // depth):
                        goal = (first // depth + d) * block + (h * 4 + e + i) * depth
                        back_ref[pl.ds(goal, depth), :] = value[
                            d * depth : (d + 1) * depth, i * 128 : (i + 1) * 128
                        ]
        send_phase(back_ref, (result_ref, second_ref), back_send, back_recv, h)
    for h in range(2):
        wait_phase(sent_ref, values_ref, out_send, out_recv, h, True)

    def sent_traces(i, carry):
        for copy in copies(i // GROUPS, i % GROUPS):
            copy.wait_send()
        return carry

    lax.fori_loop(0, SWEEPS * GROUPS, sent_traces, 0)
    wait_phase(back_ref, (result_ref, second_ref), back_send, back_recv, 0, False)
    place_back(n_span, depth, 0, result_ref, 4 * depth, place, half_ref)
    wait_phase(back_ref, (result_ref, second_ref), back_send, back_recv, 0, True)
    wait_phase(back_ref, (result_ref, second_ref), back_send, back_recv, 1, True)
    wait_phase(back_ref, (result_ref, second_ref), back_send, back_recv, 1, False)


def vmem():
    return pl.BlockSpec(memory_space=pltpu.VMEM)


def smem():
    return pl.BlockSpec(memory_space=pltpu.SMEM)


def hbm():
    return pl.BlockSpec(memory_space=pl.ANY)


def body(species, laplacian, binary, dref, stiff_eig, basis, rounds, adjacency, edge_map):
    n_span = lax.axis_size("span")
    n_elem = lax.axis_size("elem")
    depth = species.shape[2]
    own = species.shape[3]
    planes = depth * n_span
    flat = n_span * 8 * depth
    forward = transform_tables(planes)
    hot = selection_tables()
    halo = (SWEEPS, GROUPS, 4, planes // GROUPS // 2, 128)
    dma = pltpu.SemaphoreType.DMA
    tables = pl.pallas_call(
        functools.partial(table_kernel, n_elem, own),
        out_shape=jax.ShapeDtypeStruct((n_elem * 8, own), jnp.int32),
        in_specs=[vmem(), vmem()],
        out_specs=vmem(),
        scratch_shapes=[dma((n_elem,)), dma((n_elem,))],
        compiler_params=pltpu.CompilerParams(collective_id=1, has_side_effects=True),
        name="tables",
    )(adjacency.T, edge_map.T).reshape(n_elem * 8 * own)
    first_half, second_half, place = pl.pallas_call(
        functools.partial(main_kernel, n_span, n_elem, depth, own, MESH_X),
        out_shape=(
            jax.ShapeDtypeStruct((128 * depth, own), F32),
            jax.ShapeDtypeStruct((flat // 2, 128), F32),
            jax.ShapeDtypeStruct((own, own), F32),
        ),
        in_specs=[hbm(), hbm(), smem(), smem()] + [vmem()] * 3 + [smem(), vmem(), hbm()],
        out_specs=(vmem(), vmem(), vmem()),
        scratch_shapes=[
            pltpu.VMEM((NS * depth, own), F32),
            pltpu.VMEM((NS * depth, own), F32),
            pltpu.VMEM((LANES * depth, own), F32),
            pltpu.SMEM((own,), jnp.int32),
            pltpu.VMEM((136, 128), F32),
            pltpu.VMEM((2, planes, planes), BF16),
            pltpu.VMEM((2, planes, planes), BF16),
            pltpu.VMEM((flat, 128), F32),
            pltpu.VMEM((flat, 128), F32),
            pltpu.VMEM((flat, 128), F32),
            pltpu.VMEM((flat // 2, 128), F32),
            pltpu.VMEM((planes, 4 * LANES), BF16),
            pltpu.VMEM((planes, 4 * LANES), BF16),
            pltpu.VMEM((4, planes, LANES), F32),
            pltpu.VMEM((4, planes, LANES), F32),
            pltpu.VMEM((planes, LANES), F32),
            pltpu.VMEM((planes, 128), F32),
            pltpu.VMEM((4, planes, 128), F32),
            pltpu.VMEM(halo, F32),
            pltpu.VMEM(halo, F32),
            dma((5,)),
            dma((2, n_span)),
            dma((2, n_span)),
            dma((2, n_span)),
            dma((2, n_span)),
            dma(halo[:3]),
            dma(halo[:3]),
        ],
        compiler_params=pltpu.CompilerParams(
            collective_id=0, has_side_effects=True, vmem_limit_bytes=VMEM_LIMIT
        ),
        name="main",
    )(
        species.reshape(NS * depth, own),
        laplacian.reshape(NS * depth, own),
        binary,
        dref,
        stiff_eig.reshape(1, PER_SIDE),
        basis,
        rounds.reshape(1, planes // 2),
        tables,
        hot,
        split_table(forward),
    )
    updated = pl.pallas_call(
        functools.partial(finish_kernel, n_span, depth, own),
        out_shape=jax.ShapeDtypeStruct((NS * depth, own), F32),
        in_specs=[hbm(), hbm(), vmem()],
        out_specs=hbm(),
        scratch_shapes=[
            pltpu.VMEM((128 * depth, own), F32),
            pltpu.VMEM((flat // 2, 128), F32),
            pltpu.VMEM((NS * depth - 128 * depth, own), F32),
            dma((4,)),
        ],
        name="finish",
    )(first_half, second_half, place)
    return updated.reshape(species.shape)


def solution(mesh):
    return jax.shard_map(
        body,
        mesh=mesh,
        in_specs=(
            P(None, None, "span", "elem"),
            P(None, None, "span", "elem"),
            P(),
            P(),
            P(),
            P(),
            P(),
            P("elem", None),
            P("elem", None),
        ),
        out_specs=P(None, None, "span", "elem"),
        check_vma=False,
    )
```

```python
import functools

import jax
import jax.numpy as jnp
import numpy as np
from jax import lax
from jax.experimental import pallas as pl
from jax.experimental.pallas import tpu as pltpu
from jax.sharding import PartitionSpec as P

MESH_X = 16
PER_SIDE = 9
SPECIES = 3
NS = PER_SIDE * PER_SIDE * SPECIES
LANES = 256
COUPLING = 0.2
SWEEPS = 3
GROUPS = 4
F32 = jnp.float32
BF16 = jnp.bfloat16
HIGHEST = lax.Precision.HIGHEST
MESH = pl.DeviceIdType.MESH
SOUTH, EAST, NORTH, WEST = 0, 1, 2, 3
VMEM_LIMIT = 60 * 1024 * 1024

NN_DIMS = (((1,), (0,)), ((), ()))
NT_DIMS = (((1,), (1,)), ((), ()))
TN_DIMS = (((0,), (0,)), ((), ()))


def split(x):
    high = x.astype(BF16)
    return high, (x - high.astype(F32)).astype(BF16)


def dot(a, b, dims=NN_DIMS):
    return lax.dot_general(a, b, dims, preferred_element_type=F32)


def dot3(a, b, dims=NN_DIMS):
    return dot(a[0], b[0], dims) + dot(a[0], b[1], dims) + dot(a[1], b[0], dims)


def edge_lists():
    last = PER_SIDE - 1
    return [
        [i for i in range(PER_SIDE)],
        [i * PER_SIDE + last for i in range(PER_SIDE)],
        [last * PER_SIDE + last - i for i in range(PER_SIDE)],
        [(last - i) * PER_SIDE for i in range(PER_SIDE)],
    ]


def selection_tables():
    pair = np.zeros((2, LANES, 128), np.float32)
    for lane in range(NS):
        node, s = divmod(lane, SPECIES)
        pair[0, lane, node // PER_SIDE] = 1.0
        pair[1, lane, node % PER_SIDE] = 1.0
    trace = np.zeros((4, 128, 128), np.float32)
    for d, nodes in enumerate(edge_lists()):
        for t in range(PER_SIDE):
            for s in range(SPECIES):
                lane = d * 32 + t * SPECIES + s
                back = nodes[PER_SIDE - 1 - t]
                trace[0, lane, nodes[t] // PER_SIDE] = 1.0
                trace[1, lane, nodes[t] % PER_SIDE] = 1.0
                trace[2, lane, back // PER_SIDE] = 1.0
                trace[3, lane, back % PER_SIDE] = 1.0
    hot = np.concatenate([pair.reshape(2 * LANES, 128), trace.reshape(512, 128)], axis=0)
    return jnp.asarray(hot.astype(BF16))


def transform_tables(planes):
    modes = planes // 2
    phase = (np.arange(modes)[:, None] * np.arange(planes)[None, :]) % planes
    angle = phase.astype(np.float64) * (2.0 * np.pi / planes)
    trig = np.concatenate([np.cos(angle), -np.sin(angle)], axis=0)
    return np.float32(trig / planes)


def split_table(table):
    high = table.astype(BF16)
    low = (table - high.astype(np.float32)).astype(BF16)
    return jnp.asarray(np.stack([high, low]))


def split3(x):
    high = x.astype(BF16)
    rest = x - high.astype(F32)
    middle = rest.astype(BF16)
    return high, middle, (rest - middle.astype(F32)).astype(BF16)


def pick(hot, x, dims=NN_DIMS):
    return sum(dot(hot, part, dims) for part in split3(x))


def pick_right(x, hot):
    return sum(dot(part, hot, NT_DIMS) for part in split3(x))


def place_back(n_span, depth, h, values_ref, stride, place, out_ref):
    count = min(NS - h * 128, 128)
    for first in range(0, depth, 8):
        parts = [
            values_ref[pl.ds(d * stride + e * depth + first, 8), :] for e in range(4) for d in range(n_span)
        ]
        by_plane = jnp.transpose(jnp.stack(parts, axis=0), (1, 0, 2))
        moved = []
        for plane in range(8):
            high, low = split(by_plane[plane])
            moved.append(dot(high, place, TN_DIMS) + dot(low, place, TN_DIMS))
        by_lane = jnp.transpose(jnp.stack(moved, axis=0), (1, 0, 2))
        for lane in range(count):
            out_ref[pl.ds(lane * depth + first, 8), :] = by_lane[lane]


def finish_kernel(
    n_span, depth, own, half_hbm, values_hbm, place_ref, out_hbm, half_ref, values_ref, tail_ref, sems
):
    loads = [
        pltpu.make_async_copy(values_hbm, values_ref, sems.at[0]),
        pltpu.make_async_copy(half_hbm, half_ref, sems.at[1]),
    ]
    for copy in loads:
        copy.start()
    split_row = 128 * depth
    stores = [
        pltpu.make_async_copy(half_ref, out_hbm.at[pl.ds(0, split_row)], sems.at[2]),
        pltpu.make_async_copy(tail_ref, out_hbm.at[pl.ds(split_row, NS * depth - split_row)], sems.at[3]),
    ]
    loads[1].wait()
    stores[0].start()
    place = place_ref[...].astype(BF16)
    loads[0].wait()
    place_back(n_span, depth, 1, values_ref, 4 * depth, place, tail_ref)
    stores[1].start()
    stores[0].wait()
    stores[1].wait()


def neighbours(n_span, n_elem, block_rows):
    span, elem = lax.axis_index("span"), lax.axis_index("elem")
    x = span % block_rows
    odd = elem % 2
    up = 1 - 2 * odd
    block_row = jnp.where(odd == 1, block_rows - 1 - x, x)
    last, first = block_row == block_rows - 1, block_row == 0
    return {
        NORTH: (jnp.where(last, span, span + up), jnp.where(last, (elem + 1) % n_elem, elem)),
        SOUTH: (jnp.where(first, span, span - up), jnp.where(first, (elem + n_elem - 1) % n_elem, elem)),
        EAST: ((span + block_rows) % n_span, elem),
        WEST: ((span + n_span - block_rows) % n_span, elem),
    }


def main_kernel(
    n_span,
    n_elem,
    depth,
    own,
    cols,
    species_hbm,
    laplacian_hbm,
    binary_ref,
    dref_ref,
    eig_ref,
    basis_ref,
    rounds_ref,
    adjacency_ref,
    edge_map_ref,
    hot_ref,
    forward_hbm,
    half_ref,
    second_ref,
    place_ref,
    species_ref,
    laplacian_ref,
    source_ref,
    tables_ref,
    walk_ref,
    turn_ref,
    small_ref,
    forward_ref,
    backward_ref,
    sent_ref,
    values_ref,
    back_ref,
    result_ref,
    work_high,
    work_low,
    rhs_ref,
    modal_ref,
    inverse_ref,
    rounds_col,
    trace_ref,
    send_ref,
    recv_ref,
    load_sem,
    walk_sem,
    table_send,
    table_recv,
    out_send,
    out_recv,
    back_send,
    back_recv,
    send_sem,
    recv_sem,
):
    planes = n_span * depth
    modes = planes // 2
    rows = own // cols
    block_rows = rows // 2
    group = planes // GROUPS
    half = group // 2
    tile = min(256, planes)
    block = 8 * depth
    nodes = PER_SIDE * PER_SIDE
    span, elem = lax.axis_index("span"), lax.axis_index("elem")
    near = neighbours(n_span, n_elem, block_rows)

    def span_peer(k):
        z = (span // block_rows + k // block_rows) % (n_span // block_rows)
        x = (span + k) % block_rows
        return z * block_rows + x

    barrier = pltpu.get_barrier_semaphore()

    def greet_span(k, carry):
        pl.semaphore_signal(barrier, inc=1, device_id=(span_peer(k), elem), device_id_type=MESH)
        return carry

    def greet_elem(k, carry):
        pl.semaphore_signal(
            barrier, inc=1, device_id=(span, (elem + k) % n_elem), device_id_type=MESH
        )
        return carry

    lax.fori_loop(1, n_elem, greet_elem, 0)
    lax.fori_loop(1, n_span, greet_span, 0)

    cut = (128 + SPECIES - 1) // SPECIES
    pieces = [(0, cut), (cut, nodes - cut)]
    loads = []
    for i, (first, count) in enumerate(pieces):
        span_rows = pl.ds(first * SPECIES * depth, count * SPECIES * depth)
        for j, (source, target) in enumerate(
            ((species_hbm, species_ref), (laplacian_hbm, laplacian_ref))
        ):
            copy = pltpu.make_async_copy(source.at[span_rows], target.at[span_rows], load_sem.at[i * 2 + j])
            copy.start()
            loads.append(copy)
    table_load = pltpu.make_async_copy(forward_hbm, forward_ref, load_sem.at[4])
    table_load.start()

    inverse = [[1.0 / binary_ref[s, j] for j in range(SPECIES + 1)] for s in range(SPECIES)]
    dref = [dref_ref[s] for s in range(SPECIES)]
    over = [1.0 / dref_ref[s] for s in range(SPECIES)]

    def sources(first, count):
        def one_node(node, carry):
            base = pl.multiple_of(node * SPECIES * depth, 8)
            parts = [species_ref[pl.ds(base + s * depth, depth), :] for s in range(SPECIES)]
            slopes = [laplacian_ref[pl.ds(base + s * depth, depth), :] for s in range(SPECIES)]
            bath = 1.0 - (parts[0] + parts[1] + parts[2])
            for s in range(SPECIES):
                resistance = bath * inverse[s][SPECIES]
                for j in range(SPECIES):
                    if j != s:
                        resistance = resistance + parts[j] * inverse[s][j]
                mixture = (1.0 - parts[s]) / resistance
                value = (parts[s] + (mixture - dref[s]) * slopes[s]) * over[s]
                source_ref[pl.ds(base + s * depth, depth), :] = value
            return carry

        lax.fori_loop(first, first + count, one_node, 0, unroll=2)

    source_ref[pl.ds(NS * depth, (LANES - NS) * depth), :] = jnp.zeros(((LANES - NS) * depth, own), F32)
    loads[0].wait()
    loads[1].wait()
    sources(*pieces[0])

    ahead_id, ahead_edge = adjacency_ref[...], edge_map_ref[...]
    owner = ahead_id // own
    step = owner * (8 * own) + (ahead_edge + 2) % 4 * own + ahead_id % own
    before = (elem + n_elem - 1) % n_elem
    edge_ids = lax.broadcasted_iota(jnp.int32, (4, own), 0)
    elem_ids = lax.broadcasted_iota(jnp.int32, (4, own), 1)
    facing = jnp.where(owner == before, (edge_ids + 2) % 4 * own + elem_ids, 8 * own)
    start = jnp.min(jnp.min(facing, axis=0, keepdims=True), axis=1, keepdims=True)
    my_rows = pl.ds(pl.multiple_of(elem * 8, 8), 8)
    tables_ref[my_rows, :] = jnp.concatenate([step, jnp.broadcast_to(start, (4, own))], axis=0)

    pl.semaphore_wait(barrier, n_span + n_elem - 2)

    def table_copy(k):
        return pltpu.make_async_remote_copy(
            src_ref=tables_ref.at[my_rows],
            dst_ref=tables_ref.at[my_rows],
            send_sem=table_send.at[k],
            recv_sem=table_recv.at[k],
            device_id=(span, (elem + k) % n_elem),
            device_id_type=MESH,
        )

    for k in range(1, n_elem):
        table_copy(k).start()
    loads[2].wait()
    loads[3].wait()
    sources(*pieces[1])
    for k in range(1, n_elem):
        table_copy(k).wait_recv()
    walk = pltpu.make_async_copy(tables_ref, walk_ref, walk_sem)
    walk.start()
    walk.wait()

    shift = own.bit_length() - 1

    def ahead(dart):
        return walk_ref[dart >> shift, dart & (own - 1)]

    odd = elem % 2
    dart = lax.fori_loop(0, rows * elem, lambda i, d: ahead(d), walk_ref[4, 0])
    norths = []
    for row in range(rows):
        norths.append(dart)
        if row + 1 < rows:
            dart = ahead(dart)
    easts = []
    for dart in norths:
        edge = (dart >> shift) & 7
        easts.append(dart + ((((edge + 3) & 3) - edge) << shift))
    lane = lax.broadcasted_iota(jnp.int32, (1, own), 1)
    places = [jnp.where(odd == 1, block_rows - 1 - i, i) for i in range(block_rows)]
    for col in range(cols):
        for row in range(rows):
            dart = easts[row]
            slot = (row % 2 * 2 + col % 2) * n_span + (col // 2) * block_rows + places[row // 2]
            turn_ref[slot] = dart
            place_ref[pl.ds(slot, 1), :] = (lane == (dart & (own - 1))).astype(F32)
            if col + 1 < cols:
                easts[row] = ahead(dart)

    def landing(target, h):
        if isinstance(target, tuple):
            return target[h].at[pl.ds(pl.multiple_of(span * (block // 2), 8), block // 2)]
        return target.at[pl.ds(pl.multiple_of(span * block + h * (block // 2), 8), block // 2)]

    def exchange(source, target, send, recv, k, h):
        peer = span_peer(k)
        return pltpu.make_async_remote_copy(
            src_ref=source.at[pl.ds(pl.multiple_of(peer * block + h * (block // 2), 8), block // 2)],
            dst_ref=landing(target, h),
            send_sem=send.at[h, k],
            recv_sem=recv.at[h, k],
            device_id=(peer, elem),
            device_id_type=MESH,
        )

    def send_phase(source, target, send, recv, h):
        def one(k, carry):
            exchange(source, target, send, recv, k, h).start()
            return carry

        lax.fori_loop(1, n_span, one, 0)
        mine = pl.ds(pl.multiple_of(span * block + h * (block // 2), 8), block // 2)
        landing(target, h)[...] = source[mine, :]

    def wait_phase(source, target, send, recv, h, sending):
        def one(k, carry):
            copy = exchange(source, target, send, recv, k, h)
            if sending:
                copy.wait_send()
            else:
                copy.wait_recv()
            return carry

        lax.fori_loop(1, n_span, one, 0)

    place = place_ref[...].astype(BF16)
    for h in range(2):
        for first in range(0, depth, 8):
            moved = []
            for plane in range(first, first + 8):
                high, low = split(source_ref[pl.ds(h * 128 * depth + plane, 128, stride=depth), :])
                moved.append(dot(place, high, NT_DIMS) + dot(place, low, NT_DIMS))
            turned_planes = jnp.transpose(jnp.stack(moved, axis=0), (1, 0, 2))
            for slot in range(own):
                e, p = divmod(slot, n_span)
                sent_ref[pl.ds(p * block + (h * 4 + e) * depth + first, 8), :] = turned_planes[slot]
        send_phase(sent_ref, values_ref, out_send, out_recv, h)

    small_ref[...] = jnp.zeros_like(small_ref)
    small_ref[:PER_SIDE, :PER_SIDE] = basis_ref[...]
    small_ref[128 : 128 + 1, :PER_SIDE] = eig_ref[...]
    basis = small_ref[:128, :]
    hot_i, hot_j = hot_ref[:LANES, :], hot_ref[LANES : 2 * LANES, :]

    def spread(left_i, left_j):
        return pick_right(pick(left_i, basis), hot_i) * pick_right(pick(left_j, basis), hot_j)

    traces_hot = [hot_ref[pl.ds(2 * LANES + i * 128, 128), :] for i in range(4)]

    def same_species(shape, width):
        left = lax.broadcasted_iota(jnp.int32, shape, 0) % width % SPECIES
        return left == lax.broadcasted_iota(jnp.int32, shape, 1) % SPECIES

    pair_same, trace_same = same_species((LANES, LANES), LANES), same_species((128, LANES), 32)
    pair = split(jnp.where(pair_same, spread(hot_i, hot_j), 0.0))
    out_trace = jnp.where(trace_same, spread(traces_hot[0], traces_hot[1]), 0.0)
    in_trace = jnp.where(trace_same, COUPLING * spread(traces_hot[2], traces_hot[3]), 0.0)

    sides = []
    for e in range(4):
        a, b = divmod(e, 2)
        groups = [0] * 4
        groups[b], groups[1 - b] = (SOUTH, NORTH) if a == 0 else (NORTH, SOUTH)
        groups[2 + a], groups[3 - a] = (WEST, EAST) if b == 0 else (EAST, WEST)
        sides.append(groups)

    def turned(matrix, e):
        edge = ((turn_ref[e * n_span + span] >> shift) + 3) & 3
        turn = jnp.full((32, LANES), edge, jnp.int32)
        edges = [matrix[d * 32 : (d + 1) * 32] for d in range(4)]
        blocks = []
        for d in sides[e]:
            chosen = edges[d]
            for r in range(1, 4):
                chosen = jnp.where(turn == r, edges[(d + r) % 4], chosen)
            blocks.append(chosen)
        return split(jnp.concatenate(blocks, axis=0))

    to_trace, from_trace = [], []
    for e in range(4):
        high, low = turned(out_trace, e)
        to_trace.append(jnp.concatenate([high, low], axis=0))
        high, low = turned(in_trace, e)
        from_trace.append((jnp.concatenate([high, high], axis=0), low))

    eig_row = small_ref[128:136, :]
    diag = (pick_right(eig_row, hot_i) + pick_right(eig_row, hot_j))[:1]
    pair_lane = lax.broadcasted_iota(jnp.int32, (1, LANES), 1)
    for s in range(SPECIES):
        diag = diag + jnp.where(pair_lane % SPECIES == s, over[s], 0.0)
    row = lax.broadcasted_iota(jnp.int32, (planes, LANES), 0)
    wave = jnp.where(row >= modes, row - modes, row).astype(F32) * (8.0 / planes)
    inverse_ref[...] = 1.0 / (wave * wave + diag)
    square = lax.broadcasted_iota(jnp.int32, (modes, modes), 0) == lax.broadcasted_iota(
        jnp.int32, (modes, modes), 1
    )
    spread_rounds = jnp.where(square, rounds_ref[...].astype(F32), 0.0).astype(BF16)
    column = dot(spread_rounds, jnp.ones((modes, 128), BF16))
    rounds_col[:modes, :] = column
    rounds_col[modes:, :] = column

    table_load.wait()
    for part in range(2):
        for first in range(0, planes, min(128, planes)):
            strip = pl.ds(first, min(128, planes))
            turned_strip = forward_ref[part, strip, :].astype(F32).T
            backward_ref[part, :, strip] = turned_strip.astype(BF16)
    for h in range(2):
        wait_phase(sent_ref, values_ref, out_send, out_recv, h, False)
        for e in (0, 2):
            lanes = []
            for i in range(2):
                first = (h * 4 + e + i) * depth
                lanes.append(
                    jnp.concatenate(
                        [values_ref[pl.ds(d * block + first, depth), :] for d in range(n_span)], axis=0
                    )
                )
            planes_in = split(jnp.concatenate(lanes, axis=1))
            for first in range(0, planes, tile):
                out_rows = pl.ds(first, tile)
                value = split(dot3((forward_ref[0, out_rows, :], forward_ref[1, out_rows, :]), planes_in))
                for i in range(2):
                    target = pl.ds((e + i) * LANES + h * 128, 128)
                    work_high[out_rows, target] = value[0][:, i * 128 : (i + 1) * 128]
                    work_low[out_rows, target] = value[1][:, i * 128 : (i + 1) * 128]

    lane_group = lax.broadcasted_iota(jnp.int32, (1, 128), 1) // 32
    outer = {NORTH: (2, 3), SOUTH: (0, 1), EAST: (1, 3), WEST: (0, 2)}
    opposite = {NORTH: SOUTH, SOUTH: NORTH, EAST: WEST, WEST: EAST}

    def copies(sweep, g):
        return [
            pltpu.make_async_remote_copy(
                src_ref=send_ref.at[sweep, g, d],
                dst_ref=recv_ref.at[sweep, g, opposite[d]],
                send_sem=send_sem.at[sweep, g, d],
                recv_sem=recv_sem.at[sweep, g, opposite[d]],
                device_id=near[d],
                device_id_type=MESH,
            )
            for d in range(4)
        ]

    def send_traces(sweep, g):
        g_rows = pl.ds(pl.multiple_of(g * group, group), group)
        traces = []
        for e in range(4):
            high, low = split(modal_ref[e, g_rows, :])
            both = dot(high, to_trace[e], NT_DIMS)
            trace = both[:, :128] + both[:, 128:] + dot(low, to_trace[e][:128], NT_DIMS)
            trace_ref[e, g_rows, :] = trace
            traces.append(trace)
        for d in range(4):
            one, two = (traces[i] for i in outer[d])
            first, second = (0, 1) if d in (NORTH, SOUTH) else (2, 3)
            joined = jnp.where(lane_group == first, one, two)
            low_half = jnp.logical_or(lane_group == first, lane_group == second)
            send_ref[sweep, g, d] = jnp.where(low_half, joined[:half], pltpu.roll(joined[half:], 64, 1))
        for copy in copies(sweep, g):
            copy.start()

    def update(sweep, g):
        for copy in copies(sweep, g):
            copy.wait_recv()
        g_rows = pl.ds(pl.multiple_of(g * group, group), group)
        active = rounds_col[g_rows, :] > jnp.asarray(sweep, F32) + 1.5
        active = jnp.concatenate([active, active], axis=1)
        scale = inverse_ref[g_rows, :]
        outside = []
        for d in range(4):
            packed = recv_ref[sweep, g, d]
            outside.append(jnp.concatenate([packed, pltpu.roll(packed, 64, 1)], axis=0))
        for e in range(4):
            a, b = divmod(e, 2)
            across = jnp.where(
                lane_group < 2,
                jnp.where(
                    lane_group == b,
                    outside[SOUTH if a == 0 else NORTH],
                    trace_ref[2 * (1 - a) + b, g_rows, :],
                ),
                jnp.where(
                    lane_group == 2 + a,
                    outside[WEST if b == 0 else EAST],
                    trace_ref[2 * a + 1 - b, g_rows, :],
                ),
            )
            high, low = split(across)
            change = dot(jnp.concatenate([high, low], axis=1), from_trace[e][0]) + dot(high, from_trace[e][1])
            fresh = (rhs_ref[e, g_rows, :] + change) * scale
            modal_ref[e, g_rows, :] = jnp.where(active, fresh, modal_ref[e, g_rows, :])

    def begin(g, carry):
        g_rows = pl.ds(pl.multiple_of(g * group, group), group)
        scale = inverse_ref[g_rows, :]
        for e in range(4):
            lanes = pl.ds(e * LANES, LANES)
            rhs = dot3((work_high[g_rows, lanes], work_low[g_rows, lanes]), pair)
            rhs_ref[e, g_rows, :] = rhs
            modal_ref[e, g_rows, :] = rhs * scale
        send_traces(0, g)
        return carry

    def sweep_on(i, carry):
        sweep, g = i // GROUPS, i % GROUPS
        update(sweep, g)
        send_traces(sweep + 1, g)
        return carry

    def sweep_last(g, carry):
        update(SWEEPS - 1, g)
        return carry

    lax.fori_loop(0, GROUPS, begin, 0)
    lax.fori_loop(0, (SWEEPS - 1) * GROUPS, sweep_on, 0)
    lax.fori_loop(0, GROUPS, sweep_last, 0)

    tile_row = lax.broadcasted_iota(jnp.int32, (tile, 128), 0)
    for h in range(2):
        half_pair = tuple(part[h * 128 : (h + 1) * 128] for part in pair)
        for first in range(0, planes, tile):
            out_rows = pl.ds(first, tile)
            column = tile_row + first
            constant = jnp.logical_or(column == 0, column == modes)
            weight = jnp.where(constant, float(planes), float(2 * planes))
            for e in range(4):
                lanes = pl.ds(e * LANES + h * 128, 128)
                high, low = split(dot3(split(modal_ref[e, out_rows, :]), half_pair, NT_DIMS) * weight)
                work_high[out_rows, lanes] = high
                work_low[out_rows, lanes] = low
        for e in (0, 2):
            lanes = [pl.ds((e + i) * LANES + h * 128, 128) for i in range(2)]
            coeffs = tuple(
                jnp.concatenate([ref[:, lanes[0]], ref[:, lanes[1]]], axis=1) for ref in (work_high, work_low)
            )
            for first in range(0, planes, tile):
                out_rows = pl.ds(first, tile)
                value = dot3((backward_ref[0, out_rows, :], backward_ref[1, out_rows, :]), coeffs)
                for i in range(2):
                    for d in range(tile // depth):
                        goal = (first // depth + d) * block + (h * 4 + e + i) * depth
                        back_ref[pl.ds(goal, depth), :] = value[
                            d * depth : (d + 1) * depth, i * 128 : (i + 1) * 128
                        ]
        send_phase(back_ref, (result_ref, second_ref), back_send, back_recv, h)
    for h in range(2):
        wait_phase(sent_ref, values_ref, out_send, out_recv, h, True)

    def sent_traces(i, carry):
        for copy in copies(i // GROUPS, i % GROUPS):
            copy.wait_send()
        return carry

    lax.fori_loop(0, SWEEPS * GROUPS, sent_traces, 0)
    for k in range(1, n_elem):
        table_copy(k).wait_send()
    wait_phase(back_ref, (result_ref, second_ref), back_send, back_recv, 0, False)
    place_back(n_span, depth, 0, result_ref, 4 * depth, place, half_ref)
    wait_phase(back_ref, (result_ref, second_ref), back_send, back_recv, 0, True)
    wait_phase(back_ref, (result_ref, second_ref), back_send, back_recv, 1, True)
    wait_phase(back_ref, (result_ref, second_ref), back_send, back_recv, 1, False)


def vmem():
    return pl.BlockSpec(memory_space=pltpu.VMEM)


def smem():
    return pl.BlockSpec(memory_space=pltpu.SMEM)


def hbm():
    return pl.BlockSpec(memory_space=pl.ANY)


def body(species, laplacian, binary, dref, stiff_eig, basis, rounds, adjacency, edge_map):
    n_span = lax.axis_size("span")
    n_elem = lax.axis_size("elem")
    depth = species.shape[2]
    own = species.shape[3]
    planes = depth * n_span
    flat = n_span * 8 * depth
    forward = transform_tables(planes)
    hot = selection_tables()
    halo = (SWEEPS, GROUPS, 4, planes // GROUPS // 2, 128)
    dma = pltpu.SemaphoreType.DMA
    first_half, second_half, place = pl.pallas_call(
        functools.partial(main_kernel, n_span, n_elem, depth, own, MESH_X),
        out_shape=(
            jax.ShapeDtypeStruct((128 * depth, own), F32),
            jax.ShapeDtypeStruct((flat // 2, 128), F32),
            jax.ShapeDtypeStruct((own, own), F32),
        ),
        in_specs=[hbm(), hbm(), smem(), smem()] + [vmem()] * 6 + [hbm()],
        out_specs=(vmem(), vmem(), vmem()),
        scratch_shapes=[
            pltpu.VMEM((NS * depth, own), F32),
            pltpu.VMEM((NS * depth, own), F32),
            pltpu.VMEM((LANES * depth, own), F32),
            pltpu.VMEM((n_elem * 8, own), jnp.int32),
            pltpu.SMEM((n_elem * 8, own), jnp.int32),
            pltpu.SMEM((own,), jnp.int32),
            pltpu.VMEM((136, 128), F32),
            pltpu.VMEM((2, planes, planes), BF16),
            pltpu.VMEM((2, planes, planes), BF16),
            pltpu.VMEM((flat, 128), F32),
            pltpu.VMEM((flat, 128), F32),
            pltpu.VMEM((flat, 128), F32),
            pltpu.VMEM((flat // 2, 128), F32),
            pltpu.VMEM((planes, 4 * LANES), BF16),
            pltpu.VMEM((planes, 4 * LANES), BF16),
            pltpu.VMEM((4, planes, LANES), F32),
            pltpu.VMEM((4, planes, LANES), F32),
            pltpu.VMEM((planes, LANES), F32),
            pltpu.VMEM((planes, 128), F32),
            pltpu.VMEM((4, planes, 128), F32),
            pltpu.VMEM(halo, F32),
            pltpu.VMEM(halo, F32),
            dma((5,)),
            dma,
            dma((n_elem,)),
            dma((n_elem,)),
            dma((2, n_span)),
            dma((2, n_span)),
            dma((2, n_span)),
            dma((2, n_span)),
            dma(halo[:3]),
            dma(halo[:3]),
        ],
        compiler_params=pltpu.CompilerParams(
            collective_id=0, has_side_effects=True, vmem_limit_bytes=VMEM_LIMIT
        ),
        name="main",
    )(
        species.reshape(NS * depth, own),
        laplacian.reshape(NS * depth, own),
        binary,
        dref,
        stiff_eig.reshape(1, PER_SIDE),
        basis,
        rounds.reshape(1, planes // 2),
        adjacency.T,
        edge_map.T,
        hot,
        split_table(forward),
    )
    updated = pl.pallas_call(
        functools.partial(finish_kernel, n_span, depth, own),
        out_shape=jax.ShapeDtypeStruct((NS * depth, own), F32),
        in_specs=[hbm(), hbm(), vmem()],
        out_specs=hbm(),
        scratch_shapes=[
            pltpu.VMEM((128 * depth, own), F32),
            pltpu.VMEM((flat // 2, 128), F32),
            pltpu.VMEM((NS * depth - 128 * depth, own), F32),
            dma((4,)),
        ],
        name="finish",
    )(first_half, second_half, place)
    return updated.reshape(species.shape)


def solution(mesh):
    return jax.shard_map(
        body,
        mesh=mesh,
        in_specs=(
            P(None, None, "span", "elem"),
            P(None, None, "span", "elem"),
            P(),
            P(),
            P(),
            P(),
            P(),
            P("elem", None),
            P("elem", None),
        ),
        out_specs=P(None, None, "span", "elem"),
        check_vma=False,
    )
```

```python
import functools

import jax
import jax.numpy as jnp
import numpy as np
from jax import lax
from jax.experimental import pallas as pl
from jax.experimental.pallas import tpu as pltpu
from jax.sharding import PartitionSpec as P

MESH_X = 16
PER_SIDE = 9
SPECIES = 3
NS = PER_SIDE * PER_SIDE * SPECIES
LANES = 256
COUPLING = 0.2
SWEEPS = 3
GROUPS = 4
F32 = jnp.float32
BF16 = jnp.bfloat16
HIGHEST = lax.Precision.HIGHEST
MESH = pl.DeviceIdType.MESH
SOUTH, EAST, NORTH, WEST = 0, 1, 2, 3
VMEM_LIMIT = 60 * 1024 * 1024

NN_DIMS = (((1,), (0,)), ((), ()))
NT_DIMS = (((1,), (1,)), ((), ()))
TN_DIMS = (((0,), (0,)), ((), ()))


def split(x):
    high = x.astype(BF16)
    return high, (x - high.astype(F32)).astype(BF16)


def dot(a, b, dims=NN_DIMS):
    return lax.dot_general(a, b, dims, preferred_element_type=F32)


def dot3(a, b, dims=NN_DIMS):
    return dot(a[0], b[0], dims) + dot(a[0], b[1], dims) + dot(a[1], b[0], dims)


def edge_lists():
    last = PER_SIDE - 1
    return [
        [i for i in range(PER_SIDE)],
        [i * PER_SIDE + last for i in range(PER_SIDE)],
        [last * PER_SIDE + last - i for i in range(PER_SIDE)],
        [(last - i) * PER_SIDE for i in range(PER_SIDE)],
    ]


def selection_tables():
    pair = np.zeros((2, LANES, 128), np.float32)
    for lane in range(NS):
        node, s = divmod(lane, SPECIES)
        pair[0, lane, node // PER_SIDE] = 1.0
        pair[1, lane, node % PER_SIDE] = 1.0
    trace = np.zeros((4, 128, 128), np.float32)
    for d, nodes in enumerate(edge_lists()):
        for t in range(PER_SIDE):
            for s in range(SPECIES):
                lane = d * 32 + t * SPECIES + s
                back = nodes[PER_SIDE - 1 - t]
                trace[0, lane, nodes[t] // PER_SIDE] = 1.0
                trace[1, lane, nodes[t] % PER_SIDE] = 1.0
                trace[2, lane, back // PER_SIDE] = 1.0
                trace[3, lane, back % PER_SIDE] = 1.0
    hot = np.concatenate([pair.reshape(2 * LANES, 128), trace.reshape(512, 128)], axis=0)
    return jnp.asarray(hot.astype(BF16))


def transform_tables(planes):
    modes = planes // 2
    phase = (np.arange(modes)[:, None] * np.arange(planes)[None, :]) % planes
    angle = phase.astype(np.float64) * (2.0 * np.pi / planes)
    trig = np.concatenate([np.cos(angle), -np.sin(angle)], axis=0)
    return np.float32(trig / planes)


def split_table(table):
    high = table.astype(BF16)
    low = (table - high.astype(np.float32)).astype(BF16)
    return jnp.asarray(np.stack([high, low]))


def split3(x):
    high = x.astype(BF16)
    rest = x - high.astype(F32)
    middle = rest.astype(BF16)
    return high, middle, (rest - middle.astype(F32)).astype(BF16)


def pick(hot, x, dims=NN_DIMS):
    return sum(dot(hot, part, dims) for part in split3(x))


def pick_right(x, hot):
    return sum(dot(part, hot, NT_DIMS) for part in split3(x))


def place_back(n_span, depth, h, values_ref, stride, place, out_ref):
    count = min(NS - h * 128, 128)
    for first in range(0, depth, 8):
        parts = [
            values_ref[pl.ds(d * stride + e * depth + first, 8), :] for e in range(4) for d in range(n_span)
        ]
        by_plane = jnp.transpose(jnp.stack(parts, axis=0), (1, 0, 2))
        moved = []
        for plane in range(8):
            high, low = split(by_plane[plane])
            moved.append(dot(high, place, TN_DIMS) + dot(low, place, TN_DIMS))
        by_lane = jnp.transpose(jnp.stack(moved, axis=0), (1, 0, 2))
        for lane in range(count):
            out_ref[pl.ds(lane * depth + first, 8), :] = by_lane[lane]


def neighbours(n_span, n_elem, block_rows):
    span, elem = lax.axis_index("span"), lax.axis_index("elem")
    x = span % block_rows
    odd = elem % 2
    up = 1 - 2 * odd
    block_row = jnp.where(odd == 1, block_rows - 1 - x, x)
    last, first = block_row == block_rows - 1, block_row == 0
    return {
        NORTH: (jnp.where(last, span, span + up), jnp.where(last, (elem + 1) % n_elem, elem)),
        SOUTH: (jnp.where(first, span, span - up), jnp.where(first, (elem + n_elem - 1) % n_elem, elem)),
        EAST: ((span + block_rows) % n_span, elem),
        WEST: ((span + n_span - block_rows) % n_span, elem),
    }


def main_kernel(
    n_span,
    n_elem,
    depth,
    own,
    cols,
    species_hbm,
    laplacian_hbm,
    binary_ref,
    dref_ref,
    eig_ref,
    basis_ref,
    rounds_ref,
    adjacency_ref,
    edge_map_ref,
    hot_ref,
    forward_hbm,
    out_hbm,
    half_ref,
    tail_ref,
    second_ref,
    place_ref,
    species_ref,
    laplacian_ref,
    source_ref,
    tables_ref,
    walk_ref,
    turn_ref,
    small_ref,
    forward_ref,
    backward_ref,
    sent_ref,
    values_ref,
    back_ref,
    result_ref,
    work_high,
    work_low,
    rhs_ref,
    modal_ref,
    inverse_ref,
    rounds_col,
    trace_ref,
    send_ref,
    recv_ref,
    load_sem,
    store_sem,
    walk_sem,
    table_send,
    table_recv,
    out_send,
    out_recv,
    back_send,
    back_recv,
    send_sem,
    recv_sem,
):
    planes = n_span * depth
    modes = planes // 2
    rows = own // cols
    block_rows = rows // 2
    group = planes // GROUPS
    half = group // 2
    tile = min(256, planes)
    block = 8 * depth
    nodes = PER_SIDE * PER_SIDE
    span, elem = lax.axis_index("span"), lax.axis_index("elem")
    near = neighbours(n_span, n_elem, block_rows)

    def span_peer(k):
        z = (span // block_rows + k // block_rows) % (n_span // block_rows)
        x = (span + k) % block_rows
        return z * block_rows + x

    barrier = pltpu.get_barrier_semaphore()

    def greet_span(k, carry):
        pl.semaphore_signal(barrier, inc=1, device_id=(span_peer(k), elem), device_id_type=MESH)
        return carry

    def greet_elem(k, carry):
        pl.semaphore_signal(
            barrier, inc=1, device_id=(span, (elem + k) % n_elem), device_id_type=MESH
        )
        return carry

    lax.fori_loop(1, n_elem, greet_elem, 0)
    lax.fori_loop(1, n_span, greet_span, 0)

    cut = (128 + SPECIES - 1) // SPECIES
    pieces = [(0, cut), (cut, nodes - cut)]
    loads = []
    for i, (first, count) in enumerate(pieces):
        span_rows = pl.ds(first * SPECIES * depth, count * SPECIES * depth)
        for j, (source, target) in enumerate(
            ((species_hbm, species_ref), (laplacian_hbm, laplacian_ref))
        ):
            copy = pltpu.make_async_copy(source.at[span_rows], target.at[span_rows], load_sem.at[i * 2 + j])
            copy.start()
            loads.append(copy)
    table_load = pltpu.make_async_copy(forward_hbm, forward_ref, load_sem.at[4])
    table_load.start()

    inverse = [[1.0 / binary_ref[s, j] for j in range(SPECIES + 1)] for s in range(SPECIES)]
    dref = [dref_ref[s] for s in range(SPECIES)]
    over = [1.0 / dref_ref[s] for s in range(SPECIES)]

    def sources(first, count):
        def one_node(node, carry):
            base = pl.multiple_of(node * SPECIES * depth, 8)
            parts = [species_ref[pl.ds(base + s * depth, depth), :] for s in range(SPECIES)]
            slopes = [laplacian_ref[pl.ds(base + s * depth, depth), :] for s in range(SPECIES)]
            bath = 1.0 - (parts[0] + parts[1] + parts[2])
            for s in range(SPECIES):
                resistance = bath * inverse[s][SPECIES]
                for j in range(SPECIES):
                    if j != s:
                        resistance = resistance + parts[j] * inverse[s][j]
                mixture = (1.0 - parts[s]) / resistance
                value = (parts[s] + (mixture - dref[s]) * slopes[s]) * over[s]
                source_ref[pl.ds(base + s * depth, depth), :] = value
            return carry

        lax.fori_loop(first, first + count, one_node, 0, unroll=2)

    source_ref[pl.ds(NS * depth, (LANES - NS) * depth), :] = jnp.zeros(((LANES - NS) * depth, own), F32)
    loads[0].wait()
    loads[1].wait()
    sources(*pieces[0])

    ahead_id, ahead_edge = adjacency_ref[...], edge_map_ref[...]
    owner = ahead_id // own
    step = owner * (8 * own) + (ahead_edge + 2) % 4 * own + ahead_id % own
    before = (elem + n_elem - 1) % n_elem
    edge_ids = lax.broadcasted_iota(jnp.int32, (4, own), 0)
    elem_ids = lax.broadcasted_iota(jnp.int32, (4, own), 1)
    facing = jnp.where(owner == before, (edge_ids + 2) % 4 * own + elem_ids, 8 * own)
    start = jnp.min(jnp.min(facing, axis=0, keepdims=True), axis=1, keepdims=True)
    my_rows = pl.ds(pl.multiple_of(elem * 8, 8), 8)
    tables_ref[my_rows, :] = jnp.concatenate([step, jnp.broadcast_to(start, (4, own))], axis=0)

    pl.semaphore_wait(barrier, n_span + n_elem - 2)

    def table_copy(k):
        return pltpu.make_async_remote_copy(
            src_ref=tables_ref.at[my_rows],
            dst_ref=tables_ref.at[my_rows],
            send_sem=table_send.at[k],
            recv_sem=table_recv.at[k],
            device_id=(span, (elem + k) % n_elem),
            device_id_type=MESH,
        )

    for k in range(1, n_elem):
        table_copy(k).start()
    loads[2].wait()
    loads[3].wait()
    sources(*pieces[1])
    for k in range(1, n_elem):
        table_copy(k).wait_recv()
    walk = pltpu.make_async_copy(tables_ref, walk_ref, walk_sem)
    walk.start()
    walk.wait()

    shift = own.bit_length() - 1

    def ahead(dart):
        return walk_ref[dart >> shift, dart & (own - 1)]

    odd = elem % 2
    dart = lax.fori_loop(0, rows * elem, lambda i, d: ahead(d), walk_ref[4, 0])
    norths = []
    for row in range(rows):
        norths.append(dart)
        if row + 1 < rows:
            dart = ahead(dart)
    easts = []
    for dart in norths:
        edge = (dart >> shift) & 7
        easts.append(dart + ((((edge + 3) & 3) - edge) << shift))
    lane = lax.broadcasted_iota(jnp.int32, (1, own), 1)
    places = [jnp.where(odd == 1, block_rows - 1 - i, i) for i in range(block_rows)]
    for col in range(cols):
        for row in range(rows):
            dart = easts[row]
            slot = (row % 2 * 2 + col % 2) * n_span + (col // 2) * block_rows + places[row // 2]
            turn_ref[slot] = dart
            place_ref[pl.ds(slot, 1), :] = (lane == (dart & (own - 1))).astype(F32)
            if col + 1 < cols:
                easts[row] = ahead(dart)

    def landing(target, h):
        if isinstance(target, tuple):
            return target[h].at[pl.ds(pl.multiple_of(span * (block // 2), 8), block // 2)]
        return target.at[pl.ds(pl.multiple_of(span * block + h * (block // 2), 8), block // 2)]

    def exchange(source, target, send, recv, k, h):
        peer = span_peer(k)
        return pltpu.make_async_remote_copy(
            src_ref=source.at[pl.ds(pl.multiple_of(peer * block + h * (block // 2), 8), block // 2)],
            dst_ref=landing(target, h),
            send_sem=send.at[h, k],
            recv_sem=recv.at[h, k],
            device_id=(peer, elem),
            device_id_type=MESH,
        )

    def send_phase(source, target, send, recv, h):
        def one(k, carry):
            exchange(source, target, send, recv, k, h).start()
            return carry

        lax.fori_loop(1, n_span, one, 0)
        mine = pl.ds(pl.multiple_of(span * block + h * (block // 2), 8), block // 2)
        landing(target, h)[...] = source[mine, :]

    def wait_phase(source, target, send, recv, h, sending):
        def one(k, carry):
            copy = exchange(source, target, send, recv, k, h)
            if sending:
                copy.wait_send()
            else:
                copy.wait_recv()
            return carry

        lax.fori_loop(1, n_span, one, 0)

    place = place_ref[...].astype(BF16)
    for h in range(2):
        for first in range(0, depth, 8):
            moved = []
            for plane in range(first, first + 8):
                high, low = split(source_ref[pl.ds(h * 128 * depth + plane, 128, stride=depth), :])
                moved.append(dot(place, high, NT_DIMS) + dot(place, low, NT_DIMS))
            turned_planes = jnp.transpose(jnp.stack(moved, axis=0), (1, 0, 2))
            for slot in range(own):
                e, p = divmod(slot, n_span)
                sent_ref[pl.ds(p * block + (h * 4 + e) * depth + first, 8), :] = turned_planes[slot]
        send_phase(sent_ref, values_ref, out_send, out_recv, h)

    small_ref[...] = jnp.zeros_like(small_ref)
    small_ref[:PER_SIDE, :PER_SIDE] = basis_ref[...]
    small_ref[128 : 128 + 1, :PER_SIDE] = eig_ref[...]
    basis = small_ref[:128, :]
    hot_i, hot_j = hot_ref[:LANES, :], hot_ref[LANES : 2 * LANES, :]

    def spread(left_i, left_j):
        return pick_right(pick(left_i, basis), hot_i) * pick_right(pick(left_j, basis), hot_j)

    traces_hot = [hot_ref[pl.ds(2 * LANES + i * 128, 128), :] for i in range(4)]

    def same_species(shape, width):
        left = lax.broadcasted_iota(jnp.int32, shape, 0) % width % SPECIES
        return left == lax.broadcasted_iota(jnp.int32, shape, 1) % SPECIES

    pair_same, trace_same = same_species((LANES, LANES), LANES), same_species((128, LANES), 32)
    pair = split(jnp.where(pair_same, spread(hot_i, hot_j), 0.0))
    out_trace = jnp.where(trace_same, spread(traces_hot[0], traces_hot[1]), 0.0)
    in_trace = jnp.where(trace_same, COUPLING * spread(traces_hot[2], traces_hot[3]), 0.0)

    sides = []
    for e in range(4):
        a, b = divmod(e, 2)
        groups = [0] * 4
        groups[b], groups[1 - b] = (SOUTH, NORTH) if a == 0 else (NORTH, SOUTH)
        groups[2 + a], groups[3 - a] = (WEST, EAST) if b == 0 else (EAST, WEST)
        sides.append(groups)

    def turned(matrix, e):
        edge = ((turn_ref[e * n_span + span] >> shift) + 3) & 3
        turn = jnp.full((32, LANES), edge, jnp.int32)
        edges = [matrix[d * 32 : (d + 1) * 32] for d in range(4)]
        blocks = []
        for d in sides[e]:
            chosen = edges[d]
            for r in range(1, 4):
                chosen = jnp.where(turn == r, edges[(d + r) % 4], chosen)
            blocks.append(chosen)
        return split(jnp.concatenate(blocks, axis=0))

    to_trace, from_trace = [], []
    for e in range(4):
        high, low = turned(out_trace, e)
        to_trace.append(jnp.concatenate([high, low], axis=0))
        high, low = turned(in_trace, e)
        from_trace.append((jnp.concatenate([high, high], axis=0), low))

    eig_row = small_ref[128:136, :]
    diag = (pick_right(eig_row, hot_i) + pick_right(eig_row, hot_j))[:1]
    pair_lane = lax.broadcasted_iota(jnp.int32, (1, LANES), 1)
    for s in range(SPECIES):
        diag = diag + jnp.where(pair_lane % SPECIES == s, over[s], 0.0)
    row = lax.broadcasted_iota(jnp.int32, (planes, LANES), 0)
    wave = jnp.where(row >= modes, row - modes, row).astype(F32) * (8.0 / planes)
    inverse_ref[...] = 1.0 / (wave * wave + diag)
    square = lax.broadcasted_iota(jnp.int32, (modes, modes), 0) == lax.broadcasted_iota(
        jnp.int32, (modes, modes), 1
    )
    spread_rounds = jnp.where(square, rounds_ref[...].astype(F32), 0.0).astype(BF16)
    column = dot(spread_rounds, jnp.ones((modes, 128), BF16))
    rounds_col[:modes, :] = column
    rounds_col[modes:, :] = column

    table_load.wait()
    for part in range(2):
        for first in range(0, planes, min(128, planes)):
            strip = pl.ds(first, min(128, planes))
            turned_strip = forward_ref[part, strip, :].astype(F32).T
            backward_ref[part, :, strip] = turned_strip.astype(BF16)
    for h in range(2):
        wait_phase(sent_ref, values_ref, out_send, out_recv, h, False)
        for e in (0, 2):
            lanes = []
            for i in range(2):
                first = (h * 4 + e + i) * depth
                lanes.append(
                    jnp.concatenate(
                        [values_ref[pl.ds(d * block + first, depth), :] for d in range(n_span)], axis=0
                    )
                )
            planes_in = split(jnp.concatenate(lanes, axis=1))
            for first in range(0, planes, tile):
                out_rows = pl.ds(first, tile)
                value = split(dot3((forward_ref[0, out_rows, :], forward_ref[1, out_rows, :]), planes_in))
                for i in range(2):
                    target = pl.ds((e + i) * LANES + h * 128, 128)
                    work_high[out_rows, target] = value[0][:, i * 128 : (i + 1) * 128]
                    work_low[out_rows, target] = value[1][:, i * 128 : (i + 1) * 128]

    lane_group = lax.broadcasted_iota(jnp.int32, (1, 128), 1) // 32
    outer = {NORTH: (2, 3), SOUTH: (0, 1), EAST: (1, 3), WEST: (0, 2)}
    opposite = {NORTH: SOUTH, SOUTH: NORTH, EAST: WEST, WEST: EAST}

    def copies(sweep, g):
        return [
            pltpu.make_async_remote_copy(
                src_ref=send_ref.at[sweep, g, d],
                dst_ref=recv_ref.at[sweep, g, opposite[d]],
                send_sem=send_sem.at[sweep, g, d],
                recv_sem=recv_sem.at[sweep, g, opposite[d]],
                device_id=near[d],
                device_id_type=MESH,
            )
            for d in range(4)
        ]

    def send_traces(sweep, g):
        g_rows = pl.ds(pl.multiple_of(g * group, group), group)
        traces = []
        for e in range(4):
            high, low = split(modal_ref[e, g_rows, :])
            both = dot(high, to_trace[e], NT_DIMS)
            trace = both[:, :128] + both[:, 128:] + dot(low, to_trace[e][:128], NT_DIMS)
            trace_ref[e, g_rows, :] = trace
            traces.append(trace)
        for d in range(4):
            one, two = (traces[i] for i in outer[d])
            first, second = (0, 1) if d in (NORTH, SOUTH) else (2, 3)
            joined = jnp.where(lane_group == first, one, two)
            low_half = jnp.logical_or(lane_group == first, lane_group == second)
            send_ref[sweep, g, d] = jnp.where(low_half, joined[:half], pltpu.roll(joined[half:], 64, 1))
        for copy in copies(sweep, g):
            copy.start()

    def update(sweep, g):
        for copy in copies(sweep, g):
            copy.wait_recv()
        g_rows = pl.ds(pl.multiple_of(g * group, group), group)
        active = rounds_col[g_rows, :] > jnp.asarray(sweep, F32) + 1.5
        active = jnp.concatenate([active, active], axis=1)
        scale = inverse_ref[g_rows, :]
        outside = []
        for d in range(4):
            packed = recv_ref[sweep, g, d]
            outside.append(jnp.concatenate([packed, pltpu.roll(packed, 64, 1)], axis=0))
        for e in range(4):
            a, b = divmod(e, 2)
            across = jnp.where(
                lane_group < 2,
                jnp.where(
                    lane_group == b,
                    outside[SOUTH if a == 0 else NORTH],
                    trace_ref[2 * (1 - a) + b, g_rows, :],
                ),
                jnp.where(
                    lane_group == 2 + a,
                    outside[WEST if b == 0 else EAST],
                    trace_ref[2 * a + 1 - b, g_rows, :],
                ),
            )
            high, low = split(across)
            change = dot(jnp.concatenate([high, low], axis=1), from_trace[e][0]) + dot(high, from_trace[e][1])
            fresh = (rhs_ref[e, g_rows, :] + change) * scale
            modal_ref[e, g_rows, :] = jnp.where(active, fresh, modal_ref[e, g_rows, :])

    def begin(g, carry):
        g_rows = pl.ds(pl.multiple_of(g * group, group), group)
        scale = inverse_ref[g_rows, :]
        for e in range(4):
            lanes = pl.ds(e * LANES, LANES)
            rhs = dot3((work_high[g_rows, lanes], work_low[g_rows, lanes]), pair)
            rhs_ref[e, g_rows, :] = rhs
            modal_ref[e, g_rows, :] = rhs * scale
        send_traces(0, g)
        return carry

    def sweep_on(i, carry):
        sweep, g = i // GROUPS, i % GROUPS
        update(sweep, g)
        send_traces(sweep + 1, g)
        return carry

    def sweep_last(g, carry):
        update(SWEEPS - 1, g)
        return carry

    lax.fori_loop(0, GROUPS, begin, 0)
    lax.fori_loop(0, (SWEEPS - 1) * GROUPS, sweep_on, 0)
    lax.fori_loop(0, GROUPS, sweep_last, 0)

    tile_row = lax.broadcasted_iota(jnp.int32, (tile, 128), 0)
    for h in range(2):
        half_pair = tuple(part[h * 128 : (h + 1) * 128] for part in pair)
        for first in range(0, planes, tile):
            out_rows = pl.ds(first, tile)
            column = tile_row + first
            constant = jnp.logical_or(column == 0, column == modes)
            weight = jnp.where(constant, float(planes), float(2 * planes))
            for e in range(4):
                lanes = pl.ds(e * LANES + h * 128, 128)
                high, low = split(dot3(split(modal_ref[e, out_rows, :]), half_pair, NT_DIMS) * weight)
                work_high[out_rows, lanes] = high
                work_low[out_rows, lanes] = low
        for e in (0, 2):
            lanes = [pl.ds((e + i) * LANES + h * 128, 128) for i in range(2)]
            coeffs = tuple(
                jnp.concatenate([ref[:, lanes[0]], ref[:, lanes[1]]], axis=1) for ref in (work_high, work_low)
            )
            for first in range(0, planes, tile):
                out_rows = pl.ds(first, tile)
                value = dot3((backward_ref[0, out_rows, :], backward_ref[1, out_rows, :]), coeffs)
                for i in range(2):
                    for d in range(tile // depth):
                        goal = (first // depth + d) * block + (h * 4 + e + i) * depth
                        back_ref[pl.ds(goal, depth), :] = value[
                            d * depth : (d + 1) * depth, i * 128 : (i + 1) * 128
                        ]
        send_phase(back_ref, (result_ref, second_ref), back_send, back_recv, h)
    for h in range(2):
        wait_phase(sent_ref, values_ref, out_send, out_recv, h, True)

    def sent_traces(i, carry):
        for copy in copies(i // GROUPS, i % GROUPS):
            copy.wait_send()
        return carry

    lax.fori_loop(0, SWEEPS * GROUPS, sent_traces, 0)
    for k in range(1, n_elem):
        table_copy(k).wait_send()
    wait_phase(back_ref, (result_ref, second_ref), back_send, back_recv, 0, False)
    split_row = 128 * depth
    stores = [
        pltpu.make_async_copy(half_ref, out_hbm.at[pl.ds(0, split_row)], store_sem.at[0]),
        pltpu.make_async_copy(tail_ref, out_hbm.at[pl.ds(split_row, NS * depth - split_row)], store_sem.at[1]),
    ]
    place_back(n_span, depth, 0, result_ref, 4 * depth, place, half_ref)
    stores[0].start()
    wait_phase(back_ref, (result_ref, second_ref), back_send, back_recv, 0, True)
    wait_phase(back_ref, (result_ref, second_ref), back_send, back_recv, 1, True)
    wait_phase(back_ref, (result_ref, second_ref), back_send, back_recv, 1, False)
    place_back(n_span, depth, 1, second_ref, 4 * depth, place, tail_ref)
    stores[1].start()
    stores[0].wait()
    stores[1].wait()


def vmem():
    return pl.BlockSpec(memory_space=pltpu.VMEM)


def smem():
    return pl.BlockSpec(memory_space=pltpu.SMEM)


def hbm():
    return pl.BlockSpec(memory_space=pl.ANY)


def body(species, laplacian, binary, dref, stiff_eig, basis, rounds, adjacency, edge_map):
    n_span = lax.axis_size("span")
    n_elem = lax.axis_size("elem")
    depth = species.shape[2]
    own = species.shape[3]
    planes = depth * n_span
    flat = n_span * 8 * depth
    forward = transform_tables(planes)
    hot = selection_tables()
    halo = (SWEEPS, GROUPS, 4, planes // GROUPS // 2, 128)
    dma = pltpu.SemaphoreType.DMA
    updated = pl.pallas_call(
        functools.partial(main_kernel, n_span, n_elem, depth, own, MESH_X),
        out_shape=jax.ShapeDtypeStruct((NS * depth, own), F32),
        in_specs=[hbm(), hbm(), smem(), smem()] + [vmem()] * 6 + [hbm()],
        out_specs=hbm(),
        scratch_shapes=[
            pltpu.VMEM((128 * depth, own), F32),
            pltpu.VMEM((NS * depth - 128 * depth, own), F32),
            pltpu.VMEM((flat // 2, 128), F32),
            pltpu.VMEM((own, own), F32),
            pltpu.VMEM((NS * depth, own), F32),
            pltpu.VMEM((NS * depth, own), F32),
            pltpu.VMEM((LANES * depth, own), F32),
            pltpu.VMEM((n_elem * 8, own), jnp.int32),
            pltpu.SMEM((n_elem * 8, own), jnp.int32),
            pltpu.SMEM((own,), jnp.int32),
            pltpu.VMEM((136, 128), F32),
            pltpu.VMEM((2, planes, planes), BF16),
            pltpu.VMEM((2, planes, planes), BF16),
            pltpu.VMEM((flat, 128), F32),
            pltpu.VMEM((flat, 128), F32),
            pltpu.VMEM((flat, 128), F32),
            pltpu.VMEM((flat // 2, 128), F32),
            pltpu.VMEM((planes, 4 * LANES), BF16),
            pltpu.VMEM((planes, 4 * LANES), BF16),
            pltpu.VMEM((4, planes, LANES), F32),
            pltpu.VMEM((4, planes, LANES), F32),
            pltpu.VMEM((planes, LANES), F32),
            pltpu.VMEM((planes, 128), F32),
            pltpu.VMEM((4, planes, 128), F32),
            pltpu.VMEM(halo, F32),
            pltpu.VMEM(halo, F32),
            dma((5,)),
            dma((2,)),
            dma,
            dma((n_elem,)),
            dma((n_elem,)),
            dma((2, n_span)),
            dma((2, n_span)),
            dma((2, n_span)),
            dma((2, n_span)),
            dma(halo[:3]),
            dma(halo[:3]),
        ],
        compiler_params=pltpu.CompilerParams(
            collective_id=0, has_side_effects=True, vmem_limit_bytes=VMEM_LIMIT
        ),
        name="main",
    )(
        species.reshape(NS * depth, own),
        laplacian.reshape(NS * depth, own),
        binary,
        dref,
        stiff_eig.reshape(1, PER_SIDE),
        basis,
        rounds.reshape(1, planes // 2),
        adjacency.T,
        edge_map.T,
        hot,
        split_table(forward),
    )
    return updated.reshape(species.shape)


def solution(mesh):
    return jax.shard_map(
        body,
        mesh=mesh,
        in_specs=(
            P(None, None, "span", "elem"),
            P(None, None, "span", "elem"),
            P(),
            P(),
            P(),
            P(),
            P(),
            P("elem", None),
            P("elem", None),
        ),
        out_specs=P(None, None, "span", "elem"),
        check_vma=False,
    )
```

```python
import functools

import jax
import jax.numpy as jnp
import numpy as np
from jax import lax
from jax.experimental import pallas as pl
from jax.experimental.pallas import tpu as pltpu
from jax.sharding import PartitionSpec as P

MESH_X = 16
PER_SIDE = 9
SPECIES = 3
NS = PER_SIDE * PER_SIDE * SPECIES
LANES = 256
COUPLING = 0.2
SWEEPS = 3
GROUPS = 4
F32 = jnp.float32
BF16 = jnp.bfloat16
HIGHEST = lax.Precision.HIGHEST
MESH = pl.DeviceIdType.MESH
SOUTH, EAST, NORTH, WEST = 0, 1, 2, 3
VMEM_LIMIT = 60 * 1024 * 1024

NN_DIMS = (((1,), (0,)), ((), ()))
NT_DIMS = (((1,), (1,)), ((), ()))
TN_DIMS = (((0,), (0,)), ((), ()))


def split(x):
    high = x.astype(BF16)
    return high, (x - high.astype(F32)).astype(BF16)


def dot(a, b, dims=NN_DIMS):
    return lax.dot_general(a, b, dims, preferred_element_type=F32)


def dot3(a, b, dims=NN_DIMS):
    return dot(a[0], b[0], dims) + dot(a[0], b[1], dims) + dot(a[1], b[0], dims)


def edge_lists():
    last = PER_SIDE - 1
    return [
        [i for i in range(PER_SIDE)],
        [i * PER_SIDE + last for i in range(PER_SIDE)],
        [last * PER_SIDE + last - i for i in range(PER_SIDE)],
        [(last - i) * PER_SIDE for i in range(PER_SIDE)],
    ]


def selection_tables():
    pair = np.zeros((2, LANES, 128), np.float32)
    for lane in range(NS):
        node, s = divmod(lane, SPECIES)
        pair[0, lane, node // PER_SIDE] = 1.0
        pair[1, lane, node % PER_SIDE] = 1.0
    trace = np.zeros((4, 128, 128), np.float32)
    for d, nodes in enumerate(edge_lists()):
        for t in range(PER_SIDE):
            for s in range(SPECIES):
                lane = d * 32 + t * SPECIES + s
                back = nodes[PER_SIDE - 1 - t]
                trace[0, lane, nodes[t] // PER_SIDE] = 1.0
                trace[1, lane, nodes[t] % PER_SIDE] = 1.0
                trace[2, lane, back // PER_SIDE] = 1.0
                trace[3, lane, back % PER_SIDE] = 1.0
    hot = np.concatenate([pair.reshape(2 * LANES, 128), trace.reshape(512, 128)], axis=0)
    return jnp.asarray(hot.astype(BF16))


def transform_tables(planes):
    modes = planes // 2
    phase = (np.arange(modes)[:, None] * np.arange(planes)[None, :]) % planes
    angle = phase.astype(np.float64) * (2.0 * np.pi / planes)
    trig = np.concatenate([np.cos(angle), -np.sin(angle)], axis=0)
    return np.float32(trig / planes)


def split_table(table):
    high = table.astype(BF16)
    low = (table - high.astype(np.float32)).astype(BF16)
    return jnp.asarray(np.stack([high, low]))


def split3(x):
    high = x.astype(BF16)
    rest = x - high.astype(F32)
    middle = rest.astype(BF16)
    return high, middle, (rest - middle.astype(F32)).astype(BF16)


def pick(hot, x, dims=NN_DIMS):
    return sum(dot(hot, part, dims) for part in split3(x))


def pick_right(x, hot):
    return sum(dot(part, hot, NT_DIMS) for part in split3(x))


def place_back(n_span, depth, h, values_ref, stride, place, out_ref):
    count = min(NS - h * 128, 128)
    for first in range(0, depth, 8):
        parts = [
            values_ref[pl.ds(d * stride + e * depth + first, 8), :] for e in range(4) for d in range(n_span)
        ]
        by_plane = jnp.transpose(jnp.stack(parts, axis=0), (1, 0, 2))
        moved = []
        for plane in range(8):
            high, low = split(by_plane[plane])
            moved.append(dot(high, place, TN_DIMS) + dot(low, place, TN_DIMS))
        by_lane = jnp.transpose(jnp.stack(moved, axis=0), (1, 0, 2))
        for lane in range(count):
            out_ref[pl.ds(lane * depth + first, 8), :] = by_lane[lane]


def neighbours(n_span, n_elem, block_rows):
    span, elem = lax.axis_index("span"), lax.axis_index("elem")
    x = span % block_rows
    odd = elem % 2
    up = 1 - 2 * odd
    block_row = jnp.where(odd == 1, block_rows - 1 - x, x)
    last, first = block_row == block_rows - 1, block_row == 0
    return {
        NORTH: (jnp.where(last, span, span + up), jnp.where(last, (elem + 1) % n_elem, elem)),
        SOUTH: (jnp.where(first, span, span - up), jnp.where(first, (elem + n_elem - 1) % n_elem, elem)),
        EAST: ((span + block_rows) % n_span, elem),
        WEST: ((span + n_span - block_rows) % n_span, elem),
    }


def main_kernel(
    n_span,
    n_elem,
    depth,
    own,
    cols,
    species_hbm,
    laplacian_hbm,
    binary_ref,
    dref_ref,
    eig_ref,
    basis_ref,
    rounds_ref,
    adjacency_ref,
    edge_map_ref,
    hot_ref,
    forward_hbm,
    out_hbm,
    half_ref,
    tail_ref,
    second_ref,
    place_ref,
    species_ref,
    laplacian_ref,
    source_ref,
    tables_ref,
    walk_ref,
    turn_ref,
    small_ref,
    forward_ref,
    backward_ref,
    sent_ref,
    values_ref,
    back_ref,
    result_ref,
    work_high,
    work_low,
    rhs_ref,
    modal_ref,
    inverse_ref,
    rounds_col,
    trace_ref,
    send_ref,
    recv_ref,
    load_sem,
    store_sem,
    walk_sem,
    table_send,
    table_recv,
    out_send,
    out_recv,
    back_send,
    back_recv,
    send_sem,
    recv_sem,
):
    planes = n_span * depth
    modes = planes // 2
    rows = own // cols
    block_rows = rows // 2
    group = planes // GROUPS
    half = group // 2
    tile = min(256, planes)
    block = 8 * depth
    nodes = PER_SIDE * PER_SIDE
    span, elem = lax.axis_index("span"), lax.axis_index("elem")
    near = neighbours(n_span, n_elem, block_rows)

    def span_peer(k):
        z = (span // block_rows + k // block_rows) % (n_span // block_rows)
        x = (span + k) % block_rows
        return z * block_rows + x

    barrier = pltpu.get_barrier_semaphore()

    def greet_span(k, carry):
        pl.semaphore_signal(barrier, inc=1, device_id=(span_peer(k), elem), device_id_type=MESH)
        return carry

    def greet_elem(k, carry):
        pl.semaphore_signal(
            barrier, inc=1, device_id=(span, (elem + k) % n_elem), device_id_type=MESH
        )
        return carry

    lax.fori_loop(1, n_elem, greet_elem, 0)
    lax.fori_loop(1, n_span, greet_span, 0)

    cut = (128 + SPECIES - 1) // SPECIES
    pieces = [(0, cut), (cut, nodes - cut)]
    loads = []
    for i, (first, count) in enumerate(pieces):
        span_rows = pl.ds(first * SPECIES * depth, count * SPECIES * depth)
        for j, (source, target) in enumerate(
            ((species_hbm, species_ref), (laplacian_hbm, laplacian_ref))
        ):
            copy = pltpu.make_async_copy(source.at[span_rows], target.at[span_rows], load_sem.at[i * 2 + j])
            copy.start()
            loads.append(copy)
    table_load = pltpu.make_async_copy(forward_hbm, forward_ref, load_sem.at[4])
    table_load.start()

    inverse = [[1.0 / binary_ref[s, j] for j in range(SPECIES + 1)] for s in range(SPECIES)]
    dref = [dref_ref[s] for s in range(SPECIES)]
    over = [1.0 / dref_ref[s] for s in range(SPECIES)]

    def sources(first, count):
        def one_node(node, carry):
            base = pl.multiple_of(node * SPECIES * depth, 8)
            parts = [species_ref[pl.ds(base + s * depth, depth), :] for s in range(SPECIES)]
            slopes = [laplacian_ref[pl.ds(base + s * depth, depth), :] for s in range(SPECIES)]
            bath = 1.0 - (parts[0] + parts[1] + parts[2])
            for s in range(SPECIES):
                resistance = bath * inverse[s][SPECIES]
                for j in range(SPECIES):
                    if j != s:
                        resistance = resistance + parts[j] * inverse[s][j]
                mixture = (1.0 - parts[s]) / resistance
                value = (parts[s] + (mixture - dref[s]) * slopes[s]) * over[s]
                source_ref[pl.ds(base + s * depth, depth), :] = value
            return carry

        lax.fori_loop(first, first + count, one_node, 0, unroll=2)

    source_ref[pl.ds(NS * depth, (LANES - NS) * depth), :] = jnp.zeros(((LANES - NS) * depth, own), F32)
    loads[0].wait()
    loads[1].wait()
    sources(*pieces[0])

    ahead_id, ahead_edge = adjacency_ref[...], edge_map_ref[...]
    owner = ahead_id // own
    step = owner * (8 * own) + (ahead_edge + 2) % 4 * own + ahead_id % own
    before = (elem + n_elem - 1) % n_elem
    edge_ids = lax.broadcasted_iota(jnp.int32, (4, own), 0)
    elem_ids = lax.broadcasted_iota(jnp.int32, (4, own), 1)
    facing = jnp.where(owner == before, (edge_ids + 2) % 4 * own + elem_ids, 8 * own)
    start = jnp.min(jnp.min(facing, axis=0, keepdims=True), axis=1, keepdims=True)
    my_rows = pl.ds(pl.multiple_of(elem * 8, 8), 8)
    tables_ref[my_rows, :] = jnp.concatenate([step, jnp.broadcast_to(start, (4, own))], axis=0)

    pl.semaphore_wait(barrier, n_span + n_elem - 2)

    def table_copy(k):
        return pltpu.make_async_remote_copy(
            src_ref=tables_ref.at[my_rows],
            dst_ref=tables_ref.at[my_rows],
            send_sem=table_send.at[k],
            recv_sem=table_recv.at[k],
            device_id=(span, (elem + k) % n_elem),
            device_id_type=MESH,
        )

    for k in range(1, n_elem):
        table_copy(k).start()
    loads[2].wait()
    loads[3].wait()
    sources(*pieces[1])
    for k in range(1, n_elem):
        table_copy(k).wait_recv()
    walk = pltpu.make_async_copy(tables_ref, walk_ref, walk_sem)
    walk.start()
    walk.wait()

    shift = own.bit_length() - 1

    def ahead(dart):
        return walk_ref[dart >> shift, dart & (own - 1)]

    odd = elem % 2
    dart = lax.fori_loop(0, rows * elem, lambda i, d: ahead(d), walk_ref[4, 0])
    norths = []
    for row in range(rows):
        norths.append(dart)
        if row + 1 < rows:
            dart = ahead(dart)
    easts = []
    for dart in norths:
        edge = (dart >> shift) & 7
        easts.append(dart + ((((edge + 3) & 3) - edge) << shift))
    lane = lax.broadcasted_iota(jnp.int32, (1, own), 1)
    places = [jnp.where(odd == 1, block_rows - 1 - i, i) for i in range(block_rows)]
    for col in range(cols):
        for row in range(rows):
            dart = easts[row]
            slot = (row % 2 * 2 + col % 2) * n_span + (col // 2) * block_rows + places[row // 2]
            turn_ref[slot] = dart
            place_ref[pl.ds(slot, 1), :] = (lane == (dart & (own - 1))).astype(F32)
            if col + 1 < cols:
                easts[row] = ahead(dart)

    def landing(target, h):
        if isinstance(target, tuple):
            return target[h].at[pl.ds(pl.multiple_of(span * (block // 2), 8), block // 2)]
        return target.at[pl.ds(pl.multiple_of(span * block + h * (block // 2), 8), block // 2)]

    def exchange(source, target, send, recv, k, h):
        peer = span_peer(k)
        return pltpu.make_async_remote_copy(
            src_ref=source.at[pl.ds(pl.multiple_of(peer * block + h * (block // 2), 8), block // 2)],
            dst_ref=landing(target, h),
            send_sem=send.at[h, k],
            recv_sem=recv.at[h, k],
            device_id=(peer, elem),
            device_id_type=MESH,
        )

    def send_phase(source, target, send, recv, h):
        def one(k, carry):
            exchange(source, target, send, recv, k, h).start()
            return carry

        lax.fori_loop(1, n_span, one, 0)
        mine = pl.ds(pl.multiple_of(span * block + h * (block // 2), 8), block // 2)
        landing(target, h)[...] = source[mine, :]

    def wait_phase(source, target, send, recv, h, sending):
        def one(k, carry):
            copy = exchange(source, target, send, recv, k, h)
            if sending:
                copy.wait_send()
            else:
                copy.wait_recv()
            return carry

        lax.fori_loop(1, n_span, one, 0)

    place = place_ref[...].astype(BF16)
    for h in range(2):
        for first in range(0, depth, 8):
            moved = []
            for plane in range(first, first + 8):
                high, low = split(source_ref[pl.ds(h * 128 * depth + plane, 128, stride=depth), :])
                moved.append(dot(place, high, NT_DIMS) + dot(place, low, NT_DIMS))
            turned_planes = jnp.transpose(jnp.stack(moved, axis=0), (1, 0, 2))
            for slot in range(own):
                e, p = divmod(slot, n_span)
                sent_ref[pl.ds(p * block + (h * 4 + e) * depth + first, 8), :] = turned_planes[slot]
        send_phase(sent_ref, values_ref, out_send, out_recv, h)

    small_ref[...] = jnp.zeros_like(small_ref)
    small_ref[:PER_SIDE, :PER_SIDE] = basis_ref[...]
    small_ref[128 : 128 + 1, :PER_SIDE] = eig_ref[...]
    basis = small_ref[:128, :]
    hot_i, hot_j = hot_ref[:LANES, :], hot_ref[LANES : 2 * LANES, :]

    def spread(left_i, left_j):
        return pick_right(pick(left_i, basis), hot_i) * pick_right(pick(left_j, basis), hot_j)

    traces_hot = [hot_ref[pl.ds(2 * LANES + i * 128, 128), :] for i in range(4)]

    def same_species(shape, width):
        left = lax.broadcasted_iota(jnp.int32, shape, 0) % width % SPECIES
        return left == lax.broadcasted_iota(jnp.int32, shape, 1) % SPECIES

    pair_same, trace_same = same_species((LANES, LANES), LANES), same_species((128, LANES), 32)
    pair = split(jnp.where(pair_same, spread(hot_i, hot_j), 0.0))
    out_trace = jnp.where(trace_same, spread(traces_hot[0], traces_hot[1]), 0.0)
    in_trace = jnp.where(trace_same, COUPLING * spread(traces_hot[2], traces_hot[3]), 0.0)

    sides = []
    for e in range(4):
        a, b = divmod(e, 2)
        groups = [0] * 4
        groups[b], groups[1 - b] = (SOUTH, NORTH) if a == 0 else (NORTH, SOUTH)
        groups[2 + a], groups[3 - a] = (WEST, EAST) if b == 0 else (EAST, WEST)
        sides.append(groups)

    def turned(matrix, e):
        edge = ((turn_ref[e * n_span + span] >> shift) + 3) & 3
        turn = jnp.full((32, LANES), edge, jnp.int32)
        edges = [matrix[d * 32 : (d + 1) * 32] for d in range(4)]
        blocks = []
        for d in sides[e]:
            chosen = edges[d]
            for r in range(1, 4):
                chosen = jnp.where(turn == r, edges[(d + r) % 4], chosen)
            blocks.append(chosen)
        return split(jnp.concatenate(blocks, axis=0))

    to_trace, from_trace = [], []
    for e in range(4):
        high, low = turned(out_trace, e)
        to_trace.append(jnp.concatenate([high, low], axis=0))
        high, low = turned(in_trace, e)
        from_trace.append((jnp.concatenate([high, high], axis=0), low))

    eig_row = small_ref[128:136, :]
    diag = (pick_right(eig_row, hot_i) + pick_right(eig_row, hot_j))[:1]
    pair_lane = lax.broadcasted_iota(jnp.int32, (1, LANES), 1)
    for s in range(SPECIES):
        diag = diag + jnp.where(pair_lane % SPECIES == s, over[s], 0.0)
    row = lax.broadcasted_iota(jnp.int32, (planes, LANES), 0)
    wave = jnp.where(row >= modes, row - modes, row).astype(F32) * (8.0 / planes)
    inverse_ref[...] = 1.0 / (wave * wave + diag)
    square = lax.broadcasted_iota(jnp.int32, (modes, modes), 0) == lax.broadcasted_iota(
        jnp.int32, (modes, modes), 1
    )
    spread_rounds = jnp.where(square, rounds_ref[...].astype(F32), 0.0).astype(BF16)
    column = dot(spread_rounds, jnp.ones((modes, 128), BF16))
    rounds_col[:modes, :] = column
    rounds_col[modes:, :] = column

    table_load.wait()
    for part in range(2):
        for first in range(0, planes, min(128, planes)):
            strip = pl.ds(first, min(128, planes))
            turned_strip = forward_ref[part, strip, :].astype(F32).T
            backward_ref[part, :, strip] = turned_strip.astype(BF16)
    for h in range(2):
        wait_phase(sent_ref, values_ref, out_send, out_recv, h, False)
        for e in (0, 2):
            lanes = []
            for i in range(2):
                first = (h * 4 + e + i) * depth
                lanes.append(
                    jnp.concatenate(
                        [values_ref[pl.ds(d * block + first, depth), :] for d in range(n_span)], axis=0
                    )
                )
            planes_in = split(jnp.concatenate(lanes, axis=1))
            for first in range(0, planes, tile):
                out_rows = pl.ds(first, tile)
                value = split(dot3((forward_ref[0, out_rows, :], forward_ref[1, out_rows, :]), planes_in))
                for i in range(2):
                    target = pl.ds((e + i) * LANES + h * 128, 128)
                    work_high[out_rows, target] = value[0][:, i * 128 : (i + 1) * 128]
                    work_low[out_rows, target] = value[1][:, i * 128 : (i + 1) * 128]

    lane_group = lax.broadcasted_iota(jnp.int32, (1, 128), 1) // 32
    outer = {NORTH: (2, 3), SOUTH: (0, 1), EAST: (1, 3), WEST: (0, 2)}
    opposite = {NORTH: SOUTH, SOUTH: NORTH, EAST: WEST, WEST: EAST}

    def copies(sweep, g):
        return [
            pltpu.make_async_remote_copy(
                src_ref=send_ref.at[sweep, g, d],
                dst_ref=recv_ref.at[sweep, g, opposite[d]],
                send_sem=send_sem.at[sweep, g, d],
                recv_sem=recv_sem.at[sweep, g, opposite[d]],
                device_id=near[d],
                device_id_type=MESH,
            )
            for d in range(4)
        ]

    def send_traces(sweep, g):
        g_rows = pl.ds(pl.multiple_of(g * group, group), group)
        traces = []
        for e in range(4):
            high, low = split(modal_ref[e, g_rows, :])
            both = dot(high, to_trace[e], NT_DIMS)
            trace = both[:, :128] + both[:, 128:] + dot(low, to_trace[e][:128], NT_DIMS)
            trace_ref[e, g_rows, :] = trace
            traces.append(trace)
        for d in range(4):
            one, two = (traces[i] for i in outer[d])
            first, second = (0, 1) if d in (NORTH, SOUTH) else (2, 3)
            joined = jnp.where(lane_group == first, one, two)
            low_half = jnp.logical_or(lane_group == first, lane_group == second)
            send_ref[sweep, g, d] = jnp.where(low_half, joined[:half], pltpu.roll(joined[half:], 64, 1))
        for copy in copies(sweep, g):
            copy.start()

    def update(sweep, g):
        for copy in copies(sweep, g):
            copy.wait_recv()
        g_rows = pl.ds(pl.multiple_of(g * group, group), group)
        active = rounds_col[g_rows, :] > jnp.asarray(sweep, F32) + 1.5
        active = jnp.concatenate([active, active], axis=1)
        scale = inverse_ref[g_rows, :]
        outside = []
        for d in range(4):
            packed = recv_ref[sweep, g, d]
            outside.append(jnp.concatenate([packed, pltpu.roll(packed, 64, 1)], axis=0))
        for e in range(4):
            a, b = divmod(e, 2)
            across = jnp.where(
                lane_group < 2,
                jnp.where(
                    lane_group == b,
                    outside[SOUTH if a == 0 else NORTH],
                    trace_ref[2 * (1 - a) + b, g_rows, :],
                ),
                jnp.where(
                    lane_group == 2 + a,
                    outside[WEST if b == 0 else EAST],
                    trace_ref[2 * a + 1 - b, g_rows, :],
                ),
            )
            high, low = split(across)
            change = dot(jnp.concatenate([high, low], axis=1), from_trace[e][0]) + dot(high, from_trace[e][1])
            fresh = (rhs_ref[e, g_rows, :] + change) * scale
            modal_ref[e, g_rows, :] = jnp.where(active, fresh, modal_ref[e, g_rows, :])

    def into_basis(step, carry):
        t_rows = pl.ds(pl.multiple_of(step * tile, tile), tile)
        scale = inverse_ref[t_rows, :]
        for e in range(4):
            lanes = pl.ds(e * LANES, LANES)
            rhs = dot3((work_high[t_rows, lanes], work_low[t_rows, lanes]), pair)
            rhs_ref[e, t_rows, :] = rhs
            modal_ref[e, t_rows, :] = rhs * scale
        return carry

    def begin(g, carry):
        send_traces(0, g)
        return carry

    def sweep_on(i, carry):
        sweep, g = i // GROUPS, i % GROUPS
        update(sweep, g)
        send_traces(sweep + 1, g)
        return carry

    def sweep_last(g, carry):
        update(SWEEPS - 1, g)
        return carry

    lax.fori_loop(0, planes // tile, into_basis, 0)
    lax.fori_loop(0, GROUPS, begin, 0)
    lax.fori_loop(0, (SWEEPS - 1) * GROUPS, sweep_on, 0)
    lax.fori_loop(0, GROUPS, sweep_last, 0)

    tile_row = lax.broadcasted_iota(jnp.int32, (tile, 128), 0)
    for h in range(2):
        half_pair = tuple(part[h * 128 : (h + 1) * 128] for part in pair)
        for first in range(0, planes, tile):
            out_rows = pl.ds(first, tile)
            column = tile_row + first
            constant = jnp.logical_or(column == 0, column == modes)
            weight = jnp.where(constant, float(planes), float(2 * planes))
            for e in range(4):
                lanes = pl.ds(e * LANES + h * 128, 128)
                high, low = split(dot3(split(modal_ref[e, out_rows, :]), half_pair, NT_DIMS) * weight)
                work_high[out_rows, lanes] = high
                work_low[out_rows, lanes] = low
        for e in (0, 2):
            lanes = [pl.ds((e + i) * LANES + h * 128, 128) for i in range(2)]
            coeffs = tuple(
                jnp.concatenate([ref[:, lanes[0]], ref[:, lanes[1]]], axis=1) for ref in (work_high, work_low)
            )
            for first in range(0, planes, tile):
                out_rows = pl.ds(first, tile)
                value = dot3((backward_ref[0, out_rows, :], backward_ref[1, out_rows, :]), coeffs)
                for i in range(2):
                    for d in range(tile // depth):
                        goal = (first // depth + d) * block + (h * 4 + e + i) * depth
                        back_ref[pl.ds(goal, depth), :] = value[
                            d * depth : (d + 1) * depth, i * 128 : (i + 1) * 128
                        ]
        send_phase(back_ref, (result_ref, second_ref), back_send, back_recv, h)
    for h in range(2):
        wait_phase(sent_ref, values_ref, out_send, out_recv, h, True)

    def sent_traces(i, carry):
        for copy in copies(i // GROUPS, i % GROUPS):
            copy.wait_send()
        return carry

    lax.fori_loop(0, SWEEPS * GROUPS, sent_traces, 0)
    for k in range(1, n_elem):
        table_copy(k).wait_send()
    wait_phase(back_ref, (result_ref, second_ref), back_send, back_recv, 0, False)
    split_row = 128 * depth
    stores = [
        pltpu.make_async_copy(half_ref, out_hbm.at[pl.ds(0, split_row)], store_sem.at[0]),
        pltpu.make_async_copy(tail_ref, out_hbm.at[pl.ds(split_row, NS * depth - split_row)], store_sem.at[1]),
    ]
    place_back(n_span, depth, 0, result_ref, 4 * depth, place, half_ref)
    stores[0].start()
    wait_phase(back_ref, (result_ref, second_ref), back_send, back_recv, 0, True)
    wait_phase(back_ref, (result_ref, second_ref), back_send, back_recv, 1, True)
    wait_phase(back_ref, (result_ref, second_ref), back_send, back_recv, 1, False)
    place_back(n_span, depth, 1, second_ref, 4 * depth, place, tail_ref)
    stores[1].start()
    stores[0].wait()
    stores[1].wait()


def vmem():
    return pl.BlockSpec(memory_space=pltpu.VMEM)


def smem():
    return pl.BlockSpec(memory_space=pltpu.SMEM)


def hbm():
    return pl.BlockSpec(memory_space=pl.ANY)


def body(species, laplacian, binary, dref, stiff_eig, basis, rounds, adjacency, edge_map):
    n_span = lax.axis_size("span")
    n_elem = lax.axis_size("elem")
    depth = species.shape[2]
    own = species.shape[3]
    planes = depth * n_span
    flat = n_span * 8 * depth
    forward = transform_tables(planes)
    hot = selection_tables()
    halo = (SWEEPS, GROUPS, 4, planes // GROUPS // 2, 128)
    dma = pltpu.SemaphoreType.DMA
    updated = pl.pallas_call(
        functools.partial(main_kernel, n_span, n_elem, depth, own, MESH_X),
        out_shape=jax.ShapeDtypeStruct((NS * depth, own), F32),
        in_specs=[hbm(), hbm(), smem(), smem()] + [vmem()] * 6 + [hbm()],
        out_specs=hbm(),
        scratch_shapes=[
            pltpu.VMEM((128 * depth, own), F32),
            pltpu.VMEM((NS * depth - 128 * depth, own), F32),
            pltpu.VMEM((flat // 2, 128), F32),
            pltpu.VMEM((own, own), F32),
            pltpu.VMEM((NS * depth, own), F32),
            pltpu.VMEM((NS * depth, own), F32),
            pltpu.VMEM((LANES * depth, own), F32),
            pltpu.VMEM((n_elem * 8, own), jnp.int32),
            pltpu.SMEM((n_elem * 8, own), jnp.int32),
            pltpu.SMEM((own,), jnp.int32),
            pltpu.VMEM((136, 128), F32),
            pltpu.VMEM((2, planes, planes), BF16),
            pltpu.VMEM((2, planes, planes), BF16),
            pltpu.VMEM((flat, 128), F32),
            pltpu.VMEM((flat, 128), F32),
            pltpu.VMEM((flat, 128), F32),
            pltpu.VMEM((flat // 2, 128), F32),
            pltpu.VMEM((planes, 4 * LANES), BF16),
            pltpu.VMEM((planes, 4 * LANES), BF16),
            pltpu.VMEM((4, planes, LANES), F32),
            pltpu.VMEM((4, planes, LANES), F32),
            pltpu.VMEM((planes, LANES), F32),
            pltpu.VMEM((planes, 128), F32),
            pltpu.VMEM((4, planes, 128), F32),
            pltpu.VMEM(halo, F32),
            pltpu.VMEM(halo, F32),
            dma((5,)),
            dma((2,)),
            dma,
            dma((n_elem,)),
            dma((n_elem,)),
            dma((2, n_span)),
            dma((2, n_span)),
            dma((2, n_span)),
            dma((2, n_span)),
            dma(halo[:3]),
            dma(halo[:3]),
        ],
        compiler_params=pltpu.CompilerParams(
            collective_id=0, has_side_effects=True, vmem_limit_bytes=VMEM_LIMIT
        ),
        name="main",
    )(
        species.reshape(NS * depth, own),
        laplacian.reshape(NS * depth, own),
        binary,
        dref,
        stiff_eig.reshape(1, PER_SIDE),
        basis,
        rounds.reshape(1, planes // 2),
        adjacency.T,
        edge_map.T,
        hot,
        split_table(forward),
    )
    return updated.reshape(species.shape)


def solution(mesh):
    return jax.shard_map(
        body,
        mesh=mesh,
        in_specs=(
            P(None, None, "span", "elem"),
            P(None, None, "span", "elem"),
            P(),
            P(),
            P(),
            P(),
            P(),
            P("elem", None),
            P("elem", None),
        ),
        out_specs=P(None, None, "span", "elem"),
        check_vma=False,
    )
```
